32 devices in a mesh: sec: 2 (over y), blk: 16 (over z, x, core).
Axes of the slice: x: 2, y: 2, z: 4, core: 2. Of those that a mesh axis runs over, the one named last changes fastest.
Arguments:
- wave_speed: float32 [2, 125, 4096], P('sec', None, 'blk'), may hold values from 0.5 to 2
- inverse_mass: float32 [2, 125, 4096], P('sec', None, 'blk'), may hold values from 0.5 to 2
- source_field: float32 [2, 125, 4096], P('sec', None, 'blk'), may hold values from -4 to 4
- source_time: float32 [2, 12], P('sec'), may hold values from -4 to 4
- face_links: int32 [2, 3, 2048], P('sec', None, 'blk'), may hold values from 0 to 255, as said below
- coupling_links: int32 [5, 8192], P(None, 'blk'), may hold values from -1 to 255, as said below
Outputs:
- adjoint_now: float32 [2, 125, 4096], P('sec', None, 'blk')
- adjoint_before: float32 [2, 125, 4096], P('sec', None, 'blk')
The draws below stay inside these ranges and needn't reach their ends.
Inputs may be any that keep to these rules, and one draw needn't show every extreme that they name: `face_links`: in each section record k of block b and record k of its peer name each other; the peer is b XOR 2^j for a bit j that depends on the section and k only, and equals b for unlinked records, which are the trailing ones. A block's records name distinct elements. A block has at most 16 records with one peer and exactly 16 with some peer. `coupling_links`: owner -1 marks unused points, which are the trailing points of a block. A box block has at most 4 points with one owner, and every box block has exactly 4 points with one common owner.
All inputs are finite; a program needn't handle non-finite values.
Results may differ from the reference program's by a relative error of at most 0.0001.
Values sent between devices are 32-bit elements; how exact they have to be, the bound alone decides.
No kernel may reach another device: no remote copies, remote signals or barrier semaphores. Data moves between devices by JAX's collectives and lax.ppermute only.
A program may use at most 64 MiB of HBM per device.

```python
import math
import jax
import jax.numpy as jnp
import numpy as np
from jax import lax

E_DEV = 256
CP = 512
CAPC = 4
STEPS = 12
CAPF = 16
NPEER = 4
FREC = 128
ELEMS = 4096
N_BLK = 16


def draw_face_links(key, part):
    sections = []
    for section_id in range(2):
        branch = jax.random.fold_in(key, 101 + section_id)
        key_offset, key_count, key_element, key_side = jax.random.split(branch, 4)
        offsets = jnp.left_shift(jnp.ones((NPEER,), jnp.int32), jax.random.permutation(key_offset, NPEER).astype(jnp.int32))
        counts = jax.random.randint(key_count, (NPEER,), CAPF // 2 + 1, CAPF + 1)
        group_index = jnp.arange(NPEER)
        counts = jnp.where(group_index == 0, CAPF, counts)
        group_ends = jnp.cumsum(counts)
        record = jnp.arange(FREC)
        group_of = jnp.sum((record[:, None] >= group_ends[None, :]).astype(jnp.int32), axis=1)
        linked = record < group_ends[-1]
        offset = jnp.where(linked, offsets[jnp.minimum(group_of, NPEER - 1)], 0)
        blocks = jnp.arange(N_BLK)
        peers = jnp.bitwise_xor(blocks[:, None], offset[None, :])
        element_keys = jax.random.split(key_element, N_BLK)
        elements = jax.vmap(lambda single: jax.random.permutation(single, E_DEV)[:FREC])(element_keys)
        side_draw = jax.random.randint(key_side, (N_BLK, FREC), 0, 6)
        link_table = jnp.stack([elements.astype(jnp.int32), side_draw.astype(jnp.int32), peers.astype(jnp.int32)])
        sections.append(link_table.reshape(3, N_BLK * FREC))
    return jnp.stack(sections).astype(jnp.int32)


def draw_coupling_links(key, part):
    branch = jax.random.fold_in(key, 202)
    keys = jax.random.split(branch, 7)
    hot_owner = jax.random.randint(keys[0], (), 0, N_BLK)
    sizes = jax.random.randint(keys[1], (N_BLK, N_BLK - 1), 1, CAPC + 1)
    sizes = sizes.at[:, 0].set(CAPC)
    group_ends = jnp.cumsum(sizes, axis=1)
    point = jnp.arange(CP)
    group_of = jnp.sum((point[None, :, None] >= group_ends[:, None, :]).astype(jnp.int32), axis=2)
    live_count = jax.random.randint(keys[2], (N_BLK, 1), CP // 2, CP)
    in_use = (point[None, :] < live_count) & (point[None, :] < group_ends[:, -1:])
    blocks = jnp.arange(N_BLK)[:, None]
    spread = jnp.mod(blocks + group_of - 1, N_BLK - 1)
    owner = jnp.where(group_of == 0, hot_owner, jnp.mod(hot_owner + 1 + spread, N_BLK))
    owner = jnp.where(in_use, owner, -1)
    elements = jax.random.randint(keys[3], (N_BLK, CP), 0, E_DEV)
    nodes_drawn = jax.random.randint(keys[4], (N_BLK, CP), 0, 125)
    target_elements = jax.random.randint(keys[5], (N_BLK, CP), 0, E_DEV)
    target_nodes = jax.random.randint(keys[6], (N_BLK, CP), 0, 125)
    link_table = jnp.stack([elements, nodes_drawn, owner, target_elements, target_nodes]).astype(jnp.int32)
    return link_table.reshape(5, N_BLK * CP)


def level_of(key, extent, cuts, smallest, high):
    factor_of = 1.0
    for dim, shards_of in cuts:
        heights = jax.random.uniform(jax.random.fold_in(jax.random.fold_in(key, 6), dim), (shards_of,), jnp.float32, smallest / len(cuts), high / len(cuts))
        factor_of = factor_of * jnp.repeat(jnp.exp(heights), extent[dim] // shards_of).reshape((-1,) + (1,) * (len(extent) - 1 - dim))
    return factor_of


def centred(stream_key, dims, width, bound, cuts=(), kind=jnp.bfloat16):
    values = jax.random.normal(stream_key, dims, jnp.float32) * width
    if len(cuts) > 0:
        values = level_of(stream_key, dims, cuts, -0.22, 0.18) * values
    return jnp.clip(values, min=-bound, max=bound).astype(kind)


def setup_inputs(seed: int = 0) -> dict:
    key_of = jax.random.split(jax.random.key(seed), 7)
    wave_speed = jnp.clip(jnp.exp(math.log(2.0) - 1.3862944 * jax.random.uniform(key_of[0], (2, 125, ELEMS), jnp.float32) ** level_of(key_of[0], (2, 125, ELEMS), ((0, 2), (2, 16)), -0.2, 0.2)), 0.5, 2.0)
    inverse_mass = jnp.clip(jnp.exp(math.log(2.0) - 1.3862944 * jax.random.uniform(key_of[1], (2, 125, ELEMS), jnp.float32) ** level_of(key_of[1], (2, 125, ELEMS), ((0, 2), (2, 16)), -0.2, 0.2)), 0.5, 2.0)
    source_field = centred(key_of[2], (2, 125, ELEMS), 0.5, 4.0, ((0, 2), (2, 16)), jnp.float32)
    source_time = centred(key_of[3], (2, STEPS), 1.0, 4.0, ((0, 2),), jnp.float32)
    face_links = draw_face_links(jax.random.fold_in(key_of[6], 71), 0)
    coupling_links = draw_coupling_links(jax.random.fold_in(key_of[6], 71), 0)
    return dict(wave_speed=wave_speed, inverse_mass=inverse_mass, source_field=source_field, source_time=source_time, face_links=face_links, coupling_links=coupling_links)


DT_SQUARED = 0.05
PENALTY = 10.0

def node_tables():
    abscissae = np.array([-1.0, -np.sqrt(3.0 / 7.0), 0.0, np.sqrt(3.0 / 7.0), 1.0])
    weights = np.array([0.1, 49.0 / 90.0, 32.0 / 45.0, 49.0 / 90.0, 0.1])
    legendre = (35.0 * abscissae ** 4 - 30.0 * abscissae ** 2 + 3.0) / 8.0
    derivative = np.zeros((5, 5))
    for i in range(5):
        for j in range(5):
            if i != j:
                derivative[i, j] = legendre[i] / (legendre[j] * (abscissae[i] - abscissae[j]))
    derivative[0, 0] = -2.5
    derivative[4, 4] = 2.5
    identity = np.eye(5)
    operator = np.concatenate([np.kron(np.kron(derivative, identity), identity), np.kron(np.kron(identity, derivative), identity), np.kron(np.kron(identity, identity), derivative)], axis=0)
    weight_cube = weights[:, None, None] * weights[None, :, None] * weights[None, None, :]
    lattice = np.arange(125).reshape(5, 5, 5)
    face_nodes = np.stack([lattice[0].ravel(), lattice[4].ravel(), lattice[:, 0].ravel(), lattice[:, 4].ravel(), lattice[:, :, 0].ravel(), lattice[:, :, 4].ravel()])
    return (operator.astype(np.float32), weight_cube.reshape(125, 1).astype(np.float32), face_nodes.astype(np.int32))

def stiffness(field_in, speed_sq, operator, weight_cube):
    columns = field_in.shape[-1]
    scaling = weight_cube * speed_sq
    grads = jnp.dot(operator, field_in, precision=lax.Precision.HIGHEST, preferred_element_type=jnp.float32)
    scaled = (grads.reshape(3, 125, columns) * scaling[None]).reshape(375, columns)
    return jnp.dot(operator.T, scaled, precision=lax.Precision.HIGHEST, preferred_element_type=jnp.float32)

def blocked(field_in):
    return field_in.reshape(2, 125, N_BLK, E_DEV).transpose(0, 2, 1, 3).reshape(2 * N_BLK, 125, E_DEV)

def unblocked(field_in):
    return field_in.reshape(2, N_BLK, 125, E_DEV).transpose(0, 2, 1, 3).reshape(2, 125, N_BLK * E_DEV)

def reference(wave_speed, inverse_mass, source_field, source_time, face_links, coupling_links):
    operator_np, weight_np, faces_np = node_tables()
    operator = jnp.asarray(operator_np)
    weight_cube = jnp.asarray(weight_np)
    face_nodes = jnp.asarray(faces_np)
    speed_sq = blocked(wave_speed)
    inverse = blocked(inverse_mass)
    forcing = blocked(source_field)
    links = face_links.reshape(2, 3, N_BLK, FREC)
    element = links[:, 0]
    face_side = links[:, 1]
    face_peer = links[:, 2]
    section_ids = jnp.arange(2)[:, None, None]
    block_ids = jnp.arange(N_BLK)[None, :, None]
    record_ids = jnp.arange(FREC)[None, None, :]
    linked = face_peer != block_ids
    flat_block = (section_ids * N_BLK + block_ids)[..., None]
    record_nodes = face_nodes[face_side]
    element_col = element[..., None]
    points = coupling_links.reshape(5, N_BLK, CP)
    box_rows = jnp.arange(N_BLK)[:, None]
    global_rows = N_BLK + jnp.maximum(points[2], 0)
    in_use = points[2] >= 0
    current = jnp.zeros((2 * N_BLK, 125, E_DEV), jnp.float32)
    previous = jnp.zeros((2 * N_BLK, 125, E_DEV), jnp.float32)
    for moment in range(STEPS):
        internal = lax.map(lambda pair: stiffness(pair[0], pair[1], operator, weight_cube), (current, speed_sq))
        face_values = internal[flat_block, record_nodes, element_col]
        partner = face_values[section_ids, face_peer, record_ids]
        partner = jnp.where(linked[..., None], partner, 0.0)
        assembled = internal.at[flat_block, record_nodes, element_col].add(partner)
        velocity = current - previous
        traction = assembled[box_rows, points[1], points[0]]
        remote = velocity[global_rows, points[4], points[3]]
        local_velocity = velocity[box_rows, points[1], points[0]]
        coupling = jnp.zeros_like(current)
        coupling = coupling.at[global_rows, points[4], points[3]].add(jnp.where(in_use, traction, 0.0))
        coupling = coupling.at[box_rows, points[1], points[0]].add(jnp.where(in_use, PENALTY * (remote - local_velocity), 0.0))
        amplitude = jnp.repeat(source_time[:, moment], N_BLK)[:, None, None]
        advanced = 2.0 * current - previous + DT_SQUARED * inverse * (amplitude * forcing - assembled + coupling)
        previous = current
        current = advanced
    return (unblocked(current), unblocked(previous))
```

```python
import jax
import jax.numpy as jnp
import numpy as np
from jax import lax
from jax.experimental import pallas as pl
from jax.experimental.pallas import tpu as pltpu
from jax.sharding import PartitionSpec as P

CAPC = 4
STEPS = 12


DT_SQUARED = 0.05
PENALTY = 10.0


def partner_2(value, axis, stride):
    return lax.ppermute(value, axis, [(i, i ^ 1 << stride) for i in range(lax.axis_size(axis))])


def node_tables():
    abscissae = np.array([-1.0, -np.sqrt(3.0 / 7.0), 0.0, np.sqrt(3.0 / 7.0), 1.0])
    weights = np.array([0.1, 49.0 / 90.0, 32.0 / 45.0, 49.0 / 90.0, 0.1])
    legendre = (35.0 * abscissae**4 - 30.0 * abscissae**2 + 3.0) / 8.0
    derivative = np.zeros((5, 5))
    for i in range(5):
        for j in range(5):
            if i != j:
                derivative[i, j] = legendre[i] / (legendre[j] * (abscissae[i] - abscissae[j]))
    derivative[0, 0] = -2.5
    derivative[4, 4] = 2.5
    identity = np.eye(5)
    operator = np.concatenate(
        [
            np.kron(np.kron(derivative, identity), identity),
            np.kron(np.kron(identity, derivative), identity),
            np.kron(np.kron(identity, identity), derivative),
        ],
        axis=0,
    )
    weight_cube = weights[:, None, None] * weights[None, :, None] * weights[None, None, :]
    lattice = np.arange(125).reshape(5, 5, 5)
    face_nodes = np.stack(
        [
            lattice[0].ravel(),
            lattice[4].ravel(),
            lattice[:, 0].ravel(),
            lattice[:, 4].ravel(),
            lattice[:, :, 0].ravel(),
            lattice[:, :, 4].ravel(),
        ]
    )
    return (
        operator.astype(np.float32),
        weight_cube.reshape(125, 1).astype(np.float32),
        face_nodes.astype(np.int32),
    )


def stiffness(field_in, speed_sq, operator, weight_cube):
    columns = field_in.shape[-1]
    scaling = weight_cube * speed_sq
    grads = jnp.dot(
        operator, field_in, precision=lax.Precision.HIGHEST, preferred_element_type=jnp.float32
    )
    scaled = (grads.reshape(3, 125, columns) * scaling[None]).reshape(375, columns)
    return jnp.dot(
        operator.T, scaled, precision=lax.Precision.HIGHEST, preferred_element_type=jnp.float32
    )


def general_body(wave_speed, inverse_mass, source_field, source_time, face_links, coupling_links):
    operator_np, weight_np, faces_np = node_tables()
    operator = jnp.asarray(operator_np)
    weight_cube = jnp.asarray(weight_np)
    picker_np = np.zeros((150, 125), np.float32)
    for side_number in range(6):
        for node_number in range(25):
            picker_np[side_number * 25 + node_number, faces_np[side_number, node_number]] = 1.0
    picker = jnp.asarray(picker_np)
    spreader = jnp.asarray(picker_np.T.copy())
    speed_sq = wave_speed[0]
    inverse = inverse_mass[0]
    forcing = source_field[0]
    timing = source_time[0]
    element = face_links[0, 0]
    face_side = face_links[0, 1]
    face_peer = face_links[0, 2]
    blocks = lax.axis_size("blk")
    bit_count = blocks.bit_length() - 1
    myself = lax.axis_index("blk")
    is_box = lax.axis_index("sec") == 0
    records = element.shape[0]
    per_peer = records // 8
    ordinal = jnp.arange(records)
    linked = face_peer != myself
    side_mask = face_side[None, None, :] == jnp.arange(6, dtype=jnp.int32)[:, None, None]
    earlier = ordinal[None, :] < ordinal[:, None]
    face_slot = jnp.sum(
        ((face_peer[:, None] == face_peer[None, :]) & earlier).astype(jnp.int32), axis=1
    )
    offset_bits = jnp.bitwise_xor(face_peer, myself)
    bit_index = jnp.zeros((records,), jnp.int32)
    for bit_number in range(bit_count):
        bit_index = bit_index + bit_number * (offset_bits == 1 << bit_number).astype(jnp.int32)
    pair_column = jnp.where(linked, bit_index * per_peer + face_slot, 0)
    point_element = coupling_links[0]
    point_node = coupling_links[1]
    point_owner = coupling_links[2]
    target_element = coupling_links[3]
    target_node = coupling_links[4]
    in_use = point_owner >= 0
    owner_safe = jnp.maximum(point_owner, 0)
    point_ordinal = jnp.arange(point_owner.shape[0])
    point_earlier = point_ordinal[None, :] < point_ordinal[:, None]
    point_slot = jnp.sum(
        ((point_owner[:, None] == point_owner[None, :]) & point_earlier).astype(jnp.int32), axis=1
    )
    point_column = jnp.where(in_use, point_slot * blocks + owner_safe, 0)
    slot_total = CAPC * blocks
    outbound = jnp.zeros((3, slot_total), jnp.int32)
    outbound = outbound.at[0, point_column].add(jnp.where(in_use, target_element, 0))
    outbound = outbound.at[1, point_column].add(jnp.where(in_use, target_node, 0))
    outbound = outbound.at[2, point_column].add(in_use.astype(jnp.int32))
    inbound = lax.all_to_all(
        outbound.reshape(3, CAPC, blocks), "blk", split_axis=2, concat_axis=2, tiled=True
    ).reshape(3, slot_total)
    remote_element = inbound[0]
    remote_node = inbound[1]
    remote_flag = inbound[2].astype(jnp.float32)
    target_rows = jnp.concatenate([point_node, remote_node])
    target_cols = jnp.concatenate([point_element, remote_element])
    current = jnp.zeros(speed_sq.shape, jnp.float32)
    previous = jnp.zeros(speed_sq.shape, jnp.float32)
    def one_step(moment, state):
        current, previous = state
        internal = stiffness(current, speed_sq, operator, weight_cube)
        stacked = jnp.dot(
            picker,
            internal[:, element],
            precision=lax.Precision.HIGHEST,
            preferred_element_type=jnp.float32,
        ).reshape(6, 25, records)
        payload = jnp.sum(jnp.where(side_mask, stacked, 0.0), axis=0)
        payload = jnp.where(linked[None, :], payload, 0.0)
        outgoing = (
            jnp.zeros((25, bit_count * per_peer), jnp.float32).at[:, pair_column].add(payload)
        )
        arrived = []
        for bit_number in range(bit_count):
            piece = outgoing[:, bit_number * per_peer : (bit_number + 1) * per_peer]
            arrived.append(partner_2(piece, "blk", bit_number))
        partner = jnp.concatenate(arrived, axis=1)[:, pair_column]
        partner = jnp.where(linked[None, :], partner, 0.0)
        masked = jnp.where(side_mask, partner[None], 0.0).reshape(150, records)
        assembled = internal.at[:, element].add(
            jnp.dot(
                spreader,
                masked,
                precision=lax.Precision.HIGHEST,
                preferred_element_type=jnp.float32,
            )
        )
        velocity = current - previous
        traction = assembled[point_node, point_element]
        box_send = (
            jnp.zeros((slot_total,), jnp.float32)
            .at[point_column]
            .add(jnp.where(in_use, traction, 0.0))
        )
        global_send = velocity[remote_node, remote_element] * remote_flag
        dispatch = jnp.where(is_box, box_send, global_send).reshape(CAPC, blocks)
        crossed = partner_2(dispatch, "sec", 0)
        received = lax.all_to_all(crossed, "blk", split_axis=1, concat_axis=1, tiled=True)
        received = received.reshape(slot_total)
        remote_velocity = received[point_column]
        box_terms = jnp.where(
            in_use, PENALTY * (remote_velocity - velocity[point_node, point_element]), 0.0
        )
        values = jnp.concatenate(
            [jnp.where(is_box, box_terms, 0.0), jnp.where(is_box, 0.0, received * remote_flag)]
        )
        driving = timing[moment] * forcing - assembled
        driving = driving.at[target_rows, target_cols].add(values)
        advanced = 2.0 * current - previous + DT_SQUARED * inverse * driving
        return advanced, current

    current, previous = lax.fori_loop(0, STEPS, one_step, (current, previous))
    return (current[None], previous[None])


LANES = 128
HALF = 64
SLOTS = 6
LAGS = 10
PAIRS = LAGS // 2
FREE_ROWS = STEPS // 2
GAIN_ROW = FREE_ROWS
INDEX_ROW = GAIN_ROW + SLOTS * PAIRS
FLAG_ROW = INDEX_ROW + SLOTS // 2
PAYLOAD = FLAG_ROW + 1
NODES = 125
EXACT = lax.Precision.HIGHEST


def line_matrix():
    abscissae = np.array([-1.0, -np.sqrt(3.0 / 7.0), 0.0, np.sqrt(3.0 / 7.0), 1.0])
    legendre = (35.0 * abscissae**4 - 30.0 * abscissae**2 + 3.0) / 8.0
    derivative = np.zeros((5, 5))
    for i in range(5):
        for j in range(5):
            if i != j:
                derivative[i, j] = legendre[i] / (legendre[j] * (abscissae[i] - abscissae[j]))
    derivative[0, 0] = -2.5
    derivative[4, 4] = 2.5
    return derivative


def apply_line(matrix, x):
    odd = [x[0] - x[4], x[1] - x[3]]
    even = [x[0] + x[4], x[1] + x[3]]
    out = [None] * 5
    for i in range(2):
        symmetric = (
            float(0.5 * (matrix[i, 0] - matrix[i, 4])) * odd[0]
            + float(0.5 * (matrix[i, 1] - matrix[i, 3])) * odd[1]
        )
        skew = (
            float(0.5 * (matrix[i, 0] + matrix[i, 4])) * even[0]
            + float(0.5 * (matrix[i, 1] + matrix[i, 3])) * even[1]
            + float(matrix[i, 2]) * x[2]
        )
        out[i] = symmetric + skew
        out[4 - i] = symmetric - skew
    out[2] = float(matrix[2, 0]) * odd[0] + float(matrix[2, 1]) * odd[1]
    return out


def stiffness_lines(x_ref, scale_ref, y_ref):
    forward = line_matrix()
    backward = forward.T.copy()

    def along(index):
        x = [x_ref[k] for k in index]
        grads = apply_line(forward, x)
        scaled = [g * scale_ref[k] for g, k in zip(grads, index)]
        return apply_line(backward, scaled)

    for b in range(5):
        for c in range(5):
            index = [25 * j + 5 * b + c for j in range(5)]
            for k, value in zip(index, along(index)):
                y_ref[k] = value
    for a in range(5):
        total = [y_ref[25 * a + k] for k in range(25)]
        for c in range(5):
            local = [5 * j + c for j in range(5)]
            for k, value in zip(local, along([25 * a + k for k in local])):
                total[k] = total[k] + value
        for b in range(5):
            local = [5 * b + j for j in range(5)]
            for k, value in zip(local, along([25 * a + k for k in local])):
                total[k] = total[k] + value
        for k in range(25):
            y_ref[25 * a + k] = total[k]


def partner_faces(load, side):
    _, _, faces = node_tables()
    masks = [side == q for q in range(6)]
    arrived = []
    for t in range(25):
        value = jnp.zeros(side.shape, jnp.float32)
        for q in range(6):
            value = jnp.where(masks[q], load(int(faces[q, t])), value)
        arrived.append(pltpu.roll(value, HALF, 1))
    extra = [None] * NODES
    for q in range(6):
        for t in range(25):
            node = int(faces[q, t])
            before = extra[node]
            zero = jnp.zeros(side.shape, jnp.float32) if before is None else before
            extra[node] = jnp.where(masks[q], arrived[t], zero)
    return extra


def response_kernel(
    coef_ref,
    data_ref,
    side_ref,
    start_ref,
    list_ref,
    index_ref,
    out_ref,
    scale_ref,
    x_ref,
    h_ref,
    y_ref,
    t_ref,
    in_ref,
    rec_ref,
    seen_ref,
):
    row = lax.broadcasted_iota(jnp.int32, (8, LANES), 0)
    low = lax.broadcasted_iota(jnp.int32, (8, LANES), 1) < HALF
    first = row == 0
    side = side_ref[...]
    wanted = list_ref[...]
    forced = row == SLOTS
    shape = (8, LANES)

    def tile(ref, k, n):
        return jnp.broadcast_to(ref[k, n], shape)

    for n in range(NODES):
        x_ref[n] = jnp.where(row == 1, jnp.broadcast_to(start_ref[n], shape), 0.0)
        h_ref[n] = jnp.zeros(shape, jnp.float32)
        y_ref[n] = jnp.zeros(shape, jnp.float32)
        scale_ref[n] = tile(data_ref, 0, n)

    def step(moment, _):
        drive = coef_ref[0, moment]
        keep = coef_ref[1, moment]
        stiff = coef_ref[2, moment]
        begin = coef_ref[3, moment]
        is_box = coef_ref[4, 0]
        for n in range(NODES):
            t_ref[n] = jnp.where(first, y_ref[n], x_ref[n])
        extra = partner_faces(lambda k: t_ref[k], side)
        for n in range(NODES):
            assembled = t_ref[n] if extra[n] is None else t_ref[n] + extra[n]
            inverse = tile(data_ref, 1, n)
            force = tile(data_ref, 2, n)
            damp = tile(data_ref, 3, n)
            x = x_ref[n]
            h = h_ref[n]
            advanced = 2.0 * x - h + inverse * (drive * force - assembled - damp * x)
            in_ref[n] = jnp.where(first, advanced, assembled)
            rec_ref[n] = is_box * assembled + (1.0 - is_box) * (x - h)
        stiffness_lines(in_ref, scale_ref, y_ref)
        seen = jnp.zeros(shape, jnp.float32)
        for n in range(NODES):
            inverse = tile(data_ref, 1, n)
            damp = tile(data_ref, 3, n)
            x = x_ref[n]
            h = h_ref[n]
            dx = damp * x
            adjoint = 2.0 * keep * x - h + inverse * (stiff * y_ref[n] - keep * dx + begin * x)
            x_ref[n] = jnp.where(first, in_ref[n], adjoint)
            h_ref[n] = keep * (x - inverse * dx) + begin * (inverse * x)
            source = jnp.where(
                forced,
                jnp.broadcast_to(rec_ref[n][0:1], shape),
                jnp.broadcast_to(adjoint[1:2], shape),
            )
            seen = seen + jnp.where(wanted == n, source, 0.0)
        seen_ref[moment] = seen + pltpu.roll(seen, HALF, 1)
        return 0

    lax.fori_loop(0, STEPS, step, 0)
    pair_low = lax.broadcasted_iota(jnp.int32, (1, LANES), 1) < HALF
    for k in range(FREE_ROWS):
        out_ref[0, k : k + 1] = jnp.where(
            pair_low,
            seen_ref[2 * k][SLOTS : SLOTS + 1],
            seen_ref[2 * k + 1][SLOTS : SLOTS + 1],
        )
    for q in range(SLOTS):
        for k in range(PAIRS):
            r = GAIN_ROW + q * PAIRS + k
            out_ref[0, r : r + 1] = jnp.where(
                pair_low, seen_ref[2 * k][q : q + 1], seen_ref[2 * k + 1][q : q + 1]
            )
    out_ref[0, INDEX_ROW:PAYLOAD] = index_ref[...]
    for k in range(1, out_ref.shape[0]):
        out_ref[k] = out_ref[0]


def gather_packed(packed, at):
    rows = at // LANES
    lanes = at % LANES
    out = jnp.zeros(at.shape, jnp.float32)
    for k in range(8):
        source = jnp.broadcast_to(packed[k : k + 1], at.shape)
        picked = jnp.take_along_axis(source, lanes, axis=1, mode="promise_in_bounds")
        out = jnp.where(rows == k, picked, out)
    return out


def final_kernel(
    where_ref,
    time_ref,
    mine_ref,
    other_ref,
    data_ref,
    side_ref,
    at_ref,
    node_ref,
    key_ref,
    lane_key_ref,
    home_ref,
    now_ref,
    before_ref,
    both_ref,
    spread_ref,
    input_ref,
    x_ref,
    h_ref,
    y_ref,
    kick_ref,
    flat_ref,
):
    is_box = where_ref[0] == 0
    parity = where_ref[1]
    both_ref[parity] = mine_ref[...]
    both_ref[1 - parity] = other_ref[...]
    low = lax.broadcasted_iota(jnp.int32, (8, LANES), 1) < HALF

    def rows(section, core, r):
        return both_ref[core, section * 8 : section * 8 + 8, r, :]

    index = {}
    for s in range(2):
        for p in range(2):
            for k in range(SLOTS // 2):
                pair = rows(s, p, INDEX_ROW + k).astype(jnp.int32)
                turned = pltpu.roll(pair, HALF, 1)
                index[s, p, 2 * k] = jnp.where(low, pair, turned)
                index[s, p, 2 * k + 1] = jnp.where(low, turned, pair)
    at = at_ref[...]
    packed = {}
    pairs = {}
    last = {}
    zero = jnp.zeros((8, LANES), jnp.float32)
    for n in range(1, STEPS):
        value = {}
        for s in range(2):
            for p in range(2):
                free = rows(s, p, n // 2)
                total = jnp.where(low, free, 0.0) if n % 2 == 0 else jnp.where(low, 0.0, free)
                for q in range(SLOTS):
                    for k in range(PAIRS):
                        m = n - 2 * k - 1
                        if m >= 1:
                            total = total + rows(s, p, GAIN_ROW + q * PAIRS + k) * pairs[s, p, q, m]
                value[s, p] = total + pltpu.roll(total, HALF, 1)
        for s in range(2):
            packed[s] = jnp.where(low, value[s, 0], value[s, 1])
        packed[1] = PENALTY * packed[1]
        input_ref[n] = gather_packed(jnp.where(is_box, packed[1], packed[0]), at)
        if n < STEPS - 1:
            for s in range(2):
                for p in range(2):
                    for q in range(SLOTS):
                        got = gather_packed(packed[1 - s], index[s, p, q])
                        pairs[s, p, q, n] = jnp.where(low, got, last.get((s, p, q), zero))
                        last[s, p, q] = got
    input_ref[0] = zero
    for c in range(3):
        spread_ref[c] = jnp.where(
            key_ref[c * LANES : (c + 1) * LANES] == lane_key_ref[...], 1.0, 0.0
        ).astype(jnp.bfloat16)
    side = side_ref[...]
    for n in range(NODES):
        x_ref[n] = zero[:3]
        h_ref[n] = zero[:3]
        y_ref[n] = zero[:3]
    node_row = lax.broadcasted_iota(jnp.int32, (LANES, LANES), 0)

    def step(moment, _):
        drive = time_ref[moment]
        inputs = input_ref[moment]
        kick = jnp.zeros((LANES, 3 * LANES), jnp.float32)
        for c in range(3):
            chosen = jnp.where(node_row == node_ref[c : c + 1], inputs[c : c + 1], 0.0)
            for _ in range(3):
                part = chosen.astype(jnp.bfloat16)
                kick = kick + jnp.dot(part, spread_ref[c], preferred_element_type=jnp.float32)
                chosen = chosen - part.astype(jnp.float32)
        for c in range(3):
            kick_ref[c * LANES : (c + 1) * LANES] = kick[:, c * LANES : (c + 1) * LANES]
        extra = partner_faces(lambda k: y_ref[k], side)
        for n in range(NODES):
            assembled = y_ref[n] if extra[n] is None else y_ref[n] + extra[n]
            inverse = data_ref[1, n]
            damp = data_ref[3, n]
            x = x_ref[n]
            h = h_ref[n]
            arrived = kick_ref[pl.ds(n, 3, stride=LANES)]
            dx = damp * x
            advanced = 2.0 * x - h + inverse * (drive * data_ref[2, n] - assembled - dx + arrived)
            h_ref[n] = x - inverse * dx
            flat_ref[pl.ds(n, 3, stride=LANES)] = x
            x_ref[n] = advanced
        stiffness_lines(x_ref, data_ref.at[0], y_ref)
        return 0

    lax.fori_loop(0, STEPS, step, 0)
    linked = jnp.where(
        home_ref[...] == lax.broadcasted_iota(jnp.int32, (LANES, 2 * LANES), 0), 1.0, 0.0
    ).astype(jnp.bfloat16)
    alone = home_ref[...] < 0

    def put(out_ref):
        rest = flat_ref[0:LANES]
        moved = jnp.zeros((LANES, 2 * LANES), jnp.float32)
        for _ in range(3):
            part = rest.astype(jnp.bfloat16)
            moved = moved + jnp.dot(part, linked, preferred_element_type=jnp.float32)
            rest = rest - part.astype(jnp.float32)
        for g in range(2):
            own = flat_ref[(g + 1) * LANES : (g + 2) * LANES]
            cut = slice(g * LANES, (g + 1) * LANES)
            merged = jnp.where(alone[:, cut], own, moved[:, cut])
            out_ref[:, cut] = merged[:NODES]

    put(before_ref)
    for n in range(NODES):
        flat_ref[pl.ds(n, 3, stride=LANES)] = x_ref[n]
    put(now_ref)


def fast_body(wave_speed, inverse_mass, source_field, source_time, face_links, coupling_links):
    _, weight_np, _ = node_tables()
    blocks = lax.axis_size("blk")
    bits = blocks.bit_length() - 1
    me = lax.axis_index("blk")
    sec = lax.axis_index("sec")
    is_box = sec == 0
    columns = wave_speed.shape[-1]
    records = face_links.shape[-1]
    per_peer = records // 8
    offsets = [0] + [1 << j for j in range(bits)]

    live = coupling_links[:, : CAPC * blocks]
    owner = live[2]
    ordinal = jnp.arange(HALF)
    rank = jnp.sum(
        ((owner[:, None] == owner[None, :]) & (ordinal[None, :] < ordinal[:, None])).astype(jnp.int32),
        axis=1,
    )
    slot = jnp.where(owner >= 0, owner * CAPC + rank, -1)
    to_slot = (slot[:, None] == ordinal[None, :]).astype(jnp.float32)
    named = (jnp.stack([live[0], live[1], live[3], live[4]]) + 1).astype(jnp.float32)
    links = jnp.dot(named, to_slot, precision=EXACT)
    everyone = lax.all_to_all(
        jnp.broadcast_to(links[None], (blocks, 4, HALF)), "blk", 0, 0, tiled=True
    )

    face_element, face_side, face_peer = face_links[0, 0], face_links[0, 1], face_links[0, 2]
    count = jnp.arange(records)
    linked = face_peer != me
    face_rank = jnp.sum(
        ((face_peer[:, None] == face_peer[None, :]) & (count[None, :] < count[:, None])).astype(jnp.int32),
        axis=1,
    )
    distance = jnp.bitwise_xor(face_peer, me)
    bit = sum([j * (distance == 1 << j).astype(jnp.int32) for j in range(bits)])
    face_slot = jnp.where(linked, bit * per_peer + face_rank, -1)
    to_record = (face_slot[:, None] == ordinal[None, :]).astype(jnp.float32)
    record = jnp.dot(
        (jnp.stack([face_element, face_side]) + 1).astype(jnp.float32), to_record, precision=EXACT
    )

    own_nodes = (jnp.arange(128)[:, None] + 1).astype(jnp.float32) == links[1][None, :]
    own_cols = links[0][:, None] == (jnp.arange(columns)[None, :] + 1).astype(jnp.float32)
    points_at = jnp.dot(own_nodes.astype(jnp.float32), own_cols.astype(jnp.float32), precision=EXACT)
    damping = jnp.where(is_box, PENALTY, 0.0) * points_at

    def padded(field):
        return jnp.concatenate([field, jnp.zeros((3, columns), jnp.float32)], axis=0)

    fields = jnp.stack(
        [
            padded(jnp.asarray(weight_np) * wave_speed[0]),
            padded(DT_SQUARED * inverse_mass[0]),
            padded(source_field[0]),
            damping,
        ]
    )
    take_linked = (record[0][:, None] == (jnp.arange(columns)[None, :] + 1).astype(jnp.float32)).astype(
        jnp.float32
    )
    mine = lax.dot_general(
        take_linked, fields.reshape(512, columns), (((1,), (1,)), ((), ())), precision=EXACT
    )
    mine = mine.at[:, 125].set(record[0]).at[:, 126].set(record[1])
    ghost = jnp.concatenate(
        [
            partner_2(mine[j * per_peer : (j + 1) * per_peer], "blk", j)
            for j in range(bits)
        ],
        axis=0,
    )
    partner_record = ghost[:, 125:127].T
    wide = jnp.concatenate([mine, ghost], axis=0).T.reshape(4, 128, 128)
    home = jnp.concatenate([wide, fields], axis=2)

    box_table = everyone[:, 0:2]
    global_table = (
        everyone[:, 2:4].reshape(blocks, 2, blocks, CAPC).transpose(2, 1, 0, 3).reshape(blocks, 2, HALF)
    )
    table = jnp.where(is_box, box_table, global_table)
    peers = jnp.bitwise_xor(jnp.asarray(offsets, jnp.int32), me)
    near = table[peers]
    element_1 = near[:, 0].reshape(-1)
    node_1 = near[:, 1].reshape(-1)
    where_from = jnp.repeat(jnp.arange(bits + 1), HALF)
    valid = node_1 > 0
    key = jnp.where(valid, where_from * columns + element_1.astype(jnp.int32) - 1, -1)
    within = jnp.arange((bits + 1) * HALF) % HALF
    gid = within // CAPC * HALF + jnp.repeat(peers, HALF) * CAPC + within % CAPC

    point_element = near[0, 0]
    point_node = near[0, 1].astype(jnp.int32) - 1
    of_column = (
        (jnp.arange(columns)[:, None] + 1).astype(jnp.float32) == point_element[None, :]
    ).astype(jnp.float32)
    of_record = (
        (record[0][:, None] == point_element[None, :]) & (point_element[None, :] > 0)
    ).astype(jnp.float32)
    own_part = jnp.dot(fields.reshape(512, columns), of_column, precision=EXACT)
    partner_part = jnp.dot(ghost.T, of_record, precision=EXACT)
    copies = jnp.concatenate([own_part, partner_part], axis=1).reshape(4, 128, 1, 128)[:, :NODES]
    record_key = jnp.where(
        partner_record[0] > 0,
        (1 + jnp.arange(bits * per_peer) // per_peer) * columns + partner_record[0].astype(jnp.int32) - 1,
        0,
    )
    facts = jnp.stack([record[1], partner_record[1], record_key.astype(jnp.float32)])
    facts = jnp.dot(facts, of_record, precision=EXACT)
    copy_side = jnp.concatenate([facts[0], facts[1]]).astype(jnp.int32) - 1
    copy_side = jnp.broadcast_to(copy_side[None], (8, LANES))
    copy_side = jnp.where(jnp.arange(8)[:, None] < 2, copy_side, -1)
    ghost_key = jnp.where(facts[1] > 0, facts[2].astype(jnp.int32), -5)
    own_key = jnp.where(point_element > 0, point_element.astype(jnp.int32) - 1, -5)
    match = (key[:, None] == own_key[None, :]) | (key[:, None] == ghost_key[None, :])
    matched = match.astype(jnp.float32)
    lower = jnp.asarray(np.tril(np.ones((key.shape[0],) * 2, np.float32), -1))
    place = jnp.dot(lower, matched, precision=EXACT)
    picked = jnp.stack([match & (place == q) for q in range(SLOTS)], axis=1).astype(jnp.float32)
    described = jnp.stack([node_1, gid.astype(jnp.float32), (where_from > 0).astype(jnp.float32)])
    lists = jnp.dot(
        described, picked.reshape(key.shape[0], SLOTS * HALF), precision=EXACT
    ).reshape(3, SLOTS, HALF)
    list_node = lists[0].astype(jnp.int32) - 1
    on_partner = lists[2] > 0
    wanted = jnp.concatenate(
        [jnp.where(on_partner, -1, list_node), jnp.where(on_partner, list_node, -1)], axis=1
    )
    own_row = jnp.concatenate([point_node, jnp.full((HALF,), -1, jnp.int32)])[None]
    wanted = jnp.concatenate([wanted, own_row, jnp.full((1, LANES), -1, jnp.int32)], axis=0)
    too_long = jnp.max(jnp.sum(matched, axis=0)) > SLOTS
    index_rows = jnp.concatenate(
        [
            lists[1].reshape(SLOTS // 2, LANES),
            jnp.full((1, LANES), 1.0, jnp.float32) * too_long.astype(jnp.float32),
        ],
        axis=0,
    )
    unit = (
        jnp.arange(NODES)[:, None]
        == jnp.concatenate([point_node, jnp.full((HALF,), -1, jnp.int32)])[None, :]
    ).astype(jnp.float32)[:, None, :]
    late = (jnp.arange(STEPS) > 0).astype(jnp.float32)
    box_f = is_box.astype(jnp.float32)
    coef = jnp.stack(
        [
            source_time[0],
            late,
            jnp.where(late > 0, -1.0, box_f),
            jnp.where(late > 0, 0.0, 1.0 - box_f),
            jnp.full((STEPS,), 1.0, jnp.float32) * box_f,
        ]
    )
    vmem = pl.BlockSpec(memory_space=pltpu.VMEM)
    smem = pl.BlockSpec(memory_space=pltpu.SMEM)
    full = pltpu.VMEM((NODES, 8, LANES), jnp.float32)
    payload = pl.pallas_call(
        response_kernel,
        out_shape=jax.ShapeDtypeStruct((blocks, PAYLOAD, LANES), jnp.float32),
        in_specs=[smem] + [vmem] * 5,
        out_specs=vmem,
        scratch_shapes=[full] * 7 + [pltpu.VMEM((STEPS, 8, LANES), jnp.float32)],
    )(coef, copies, copy_side, unit, wanted, index_rows)

    same_core = [[c + 2 * i for i in range(blocks)] for c in range(2)]
    received = lax.all_to_all(
        payload, ("sec", "blk"), 0, 0, axis_index_groups=same_core, tiled=True
    )
    sibling = partner_2(received, "blk", 0)
    overflow = jnp.max(
        jnp.maximum(received[:, FLAG_ROW, 0], sibling[:, FLAG_ROW, 0])
    ) > 0

    fill = 3 * LANES - key.shape[0]

    def extend(values, rest):
        return jnp.concatenate([values, jnp.full((fill,), rest, jnp.int32)])

    at = jnp.zeros((8, LANES), jnp.int32).at[0:3].set(extend(gid, 0).reshape(3, LANES))
    point_rows = extend(node_1.astype(jnp.int32) - 1, -1).reshape(3, LANES)
    key_column = extend(key, -1)[:, None]
    own_record_key = jnp.where(record[0] > 0, record[0].astype(jnp.int32) - 1, -3)
    ghost_record_key = jnp.where(partner_record[0] > 0, record_key, -3)
    lane_key = jnp.concatenate([own_record_key, ghost_record_key, jnp.arange(columns)])[None]
    home_lane = jnp.dot(
        (jnp.arange(HALF)[None] + 1).astype(jnp.float32), take_linked, precision=EXACT
    ).astype(jnp.int32) - 1
    home_side = jnp.full((3, LANES), -1, jnp.int32)
    home_side = home_side.at[0].set(
        jnp.concatenate([record[1], partner_record[1]]).astype(jnp.int32) - 1
    )
    home = home[:, :NODES].reshape(4, NODES, 3, LANES)
    where_am_i = jnp.stack([sec, me % 2]).astype(jnp.int32)
    three = pltpu.VMEM((NODES, 3, LANES), jnp.float32)

    def quick(_):
        return tuple(pl.pallas_call(
            final_kernel,
            out_shape=[jax.ShapeDtypeStruct((NODES, columns), jnp.float32)] * 2,
            in_specs=[smem] * 2 + [vmem] * 9,
            out_specs=[vmem] * 2,
            scratch_shapes=[
                pltpu.VMEM((2, blocks, PAYLOAD, LANES), jnp.float32),
                pltpu.VMEM((3, LANES, 3 * LANES), jnp.bfloat16),
                pltpu.VMEM((STEPS, 8, LANES), jnp.float32),
                three,
                three,
                three,
                pltpu.VMEM((3 * LANES, LANES), jnp.float32),
                pltpu.VMEM((3 * LANES, LANES), jnp.float32),
            ],
        )(
            where_am_i,
            source_time[0],
            received,
            sibling,
            home,
            home_side,
            at,
            point_rows,
            key_column,
            lane_key,
            home_lane,
        ))

    def slow(_):
        now, before = general_body(
            wave_speed, inverse_mass, source_field, source_time, face_links, coupling_links
        )
        return (now[0], before[0])

    now, before = lax.cond(overflow, slow, quick, 0)
    return (now[None], before[None])


def body(*arguments):
    wave_speed, _, _, _, face_links, coupling_links = arguments
    fits = (
        lax.axis_size("blk") == 16
        and lax.axis_size("sec") == 2
        and wave_speed.shape[1:] == (NODES, 2 * LANES)
        and face_links.shape[-1] == LANES
        and coupling_links.shape[-1] >= CAPC * 16
    )
    return fast_body(*arguments) if fits else general_body(*arguments)


def solution(mesh):
    in_specs = (
        P("sec", None, "blk"),
        P("sec", None, "blk"),
        P("sec", None, "blk"),
        P("sec", None),
        P("sec", None, "blk"),
        P(None, "blk"),
    )
    out_specs = (P("sec", None, "blk"), P("sec", None, "blk"))
    return jax.shard_map(body, mesh=mesh, in_specs=in_specs, out_specs=out_specs, check_vma=False)
```

```python
import jax
import jax.numpy as jnp
import numpy as np
from jax import lax
from jax.experimental import pallas as pl
from jax.experimental.pallas import tpu as pltpu
from jax.sharding import PartitionSpec as P

CAPC = 4
STEPS = 12


DT_SQUARED = 0.05
PENALTY = 10.0


def partner_2(value, axis, stride):
    return lax.ppermute(value, axis, [(i, i ^ 1 << stride) for i in range(lax.axis_size(axis))])


def node_tables():
    abscissae = np.array([-1.0, -np.sqrt(3.0 / 7.0), 0.0, np.sqrt(3.0 / 7.0), 1.0])
    weights = np.array([0.1, 49.0 / 90.0, 32.0 / 45.0, 49.0 / 90.0, 0.1])
    legendre = (35.0 * abscissae**4 - 30.0 * abscissae**2 + 3.0) / 8.0
    derivative = np.zeros((5, 5))
    for i in range(5):
        for j in range(5):
            if i != j:
                derivative[i, j] = legendre[i] / (legendre[j] * (abscissae[i] - abscissae[j]))
    derivative[0, 0] = -2.5
    derivative[4, 4] = 2.5
    identity = np.eye(5)
    operator = np.concatenate(
        [
            np.kron(np.kron(derivative, identity), identity),
            np.kron(np.kron(identity, derivative), identity),
            np.kron(np.kron(identity, identity), derivative),
        ],
        axis=0,
    )
    weight_cube = weights[:, None, None] * weights[None, :, None] * weights[None, None, :]
    lattice = np.arange(125).reshape(5, 5, 5)
    face_nodes = np.stack(
        [
            lattice[0].ravel(),
            lattice[4].ravel(),
            lattice[:, 0].ravel(),
            lattice[:, 4].ravel(),
            lattice[:, :, 0].ravel(),
            lattice[:, :, 4].ravel(),
        ]
    )
    return (
        operator.astype(np.float32),
        weight_cube.reshape(125, 1).astype(np.float32),
        face_nodes.astype(np.int32),
    )


def stiffness(field_in, speed_sq, operator, weight_cube):
    columns = field_in.shape[-1]
    scaling = weight_cube * speed_sq
    grads = jnp.dot(
        operator, field_in, precision=lax.Precision.HIGHEST, preferred_element_type=jnp.float32
    )
    scaled = (grads.reshape(3, 125, columns) * scaling[None]).reshape(375, columns)
    return jnp.dot(
        operator.T, scaled, precision=lax.Precision.HIGHEST, preferred_element_type=jnp.float32
    )


def general_body(wave_speed, inverse_mass, source_field, source_time, face_links, coupling_links):
    operator_np, weight_np, faces_np = node_tables()
    operator = jnp.asarray(operator_np)
    weight_cube = jnp.asarray(weight_np)
    picker_np = np.zeros((150, 125), np.float32)
    for side_number in range(6):
        for node_number in range(25):
            picker_np[side_number * 25 + node_number, faces_np[side_number, node_number]] = 1.0
    picker = jnp.asarray(picker_np)
    spreader = jnp.asarray(picker_np.T.copy())
    speed_sq = wave_speed[0]
    inverse = inverse_mass[0]
    forcing = source_field[0]
    timing = source_time[0]
    element = face_links[0, 0]
    face_side = face_links[0, 1]
    face_peer = face_links[0, 2]
    blocks = lax.axis_size("blk")
    bit_count = blocks.bit_length() - 1
    myself = lax.axis_index("blk")
    is_box = lax.axis_index("sec") == 0
    records = element.shape[0]
    per_peer = records // 8
    ordinal = jnp.arange(records)
    linked = face_peer != myself
    side_mask = face_side[None, None, :] == jnp.arange(6, dtype=jnp.int32)[:, None, None]
    earlier = ordinal[None, :] < ordinal[:, None]
    face_slot = jnp.sum(
        ((face_peer[:, None] == face_peer[None, :]) & earlier).astype(jnp.int32), axis=1
    )
    offset_bits = jnp.bitwise_xor(face_peer, myself)
    bit_index = jnp.zeros((records,), jnp.int32)
    for bit_number in range(bit_count):
        bit_index = bit_index + bit_number * (offset_bits == 1 << bit_number).astype(jnp.int32)
    pair_column = jnp.where(linked, bit_index * per_peer + face_slot, 0)
    point_element = coupling_links[0]
    point_node = coupling_links[1]
    point_owner = coupling_links[2]
    target_element = coupling_links[3]
    target_node = coupling_links[4]
    in_use = point_owner >= 0
    owner_safe = jnp.maximum(point_owner, 0)
    point_ordinal = jnp.arange(point_owner.shape[0])
    point_earlier = point_ordinal[None, :] < point_ordinal[:, None]
    point_slot = jnp.sum(
        ((point_owner[:, None] == point_owner[None, :]) & point_earlier).astype(jnp.int32), axis=1
    )
    point_column = jnp.where(in_use, point_slot * blocks + owner_safe, 0)
    slot_total = CAPC * blocks
    outbound = jnp.zeros((3, slot_total), jnp.int32)
    outbound = outbound.at[0, point_column].add(jnp.where(in_use, target_element, 0))
    outbound = outbound.at[1, point_column].add(jnp.where(in_use, target_node, 0))
    outbound = outbound.at[2, point_column].add(in_use.astype(jnp.int32))
    inbound = lax.all_to_all(
        outbound.reshape(3, CAPC, blocks), "blk", split_axis=2, concat_axis=2, tiled=True
    ).reshape(3, slot_total)
    remote_element = inbound[0]
    remote_node = inbound[1]
    remote_flag = inbound[2].astype(jnp.float32)
    target_rows = jnp.concatenate([point_node, remote_node])
    target_cols = jnp.concatenate([point_element, remote_element])
    current = jnp.zeros(speed_sq.shape, jnp.float32)
    previous = jnp.zeros(speed_sq.shape, jnp.float32)
    def one_step(moment, state):
        current, previous = state
        internal = stiffness(current, speed_sq, operator, weight_cube)
        stacked = jnp.dot(
            picker,
            internal[:, element],
            precision=lax.Precision.HIGHEST,
            preferred_element_type=jnp.float32,
        ).reshape(6, 25, records)
        payload = jnp.sum(jnp.where(side_mask, stacked, 0.0), axis=0)
        payload = jnp.where(linked[None, :], payload, 0.0)
        outgoing = (
            jnp.zeros((25, bit_count * per_peer), jnp.float32).at[:, pair_column].add(payload)
        )
        arrived = []
        for bit_number in range(bit_count):
            piece = outgoing[:, bit_number * per_peer : (bit_number + 1) * per_peer]
            arrived.append(partner_2(piece, "blk", bit_number))
        partner = jnp.concatenate(arrived, axis=1)[:, pair_column]
        partner = jnp.where(linked[None, :], partner, 0.0)
        masked = jnp.where(side_mask, partner[None], 0.0).reshape(150, records)
        assembled = internal.at[:, element].add(
            jnp.dot(
                spreader,
                masked,
                precision=lax.Precision.HIGHEST,
                preferred_element_type=jnp.float32,
            )
        )
        velocity = current - previous
        traction = assembled[point_node, point_element]
        box_send = (
            jnp.zeros((slot_total,), jnp.float32)
            .at[point_column]
            .add(jnp.where(in_use, traction, 0.0))
        )
        global_send = velocity[remote_node, remote_element] * remote_flag
        dispatch = jnp.where(is_box, box_send, global_send).reshape(CAPC, blocks)
        crossed = partner_2(dispatch, "sec", 0)
        received = lax.all_to_all(crossed, "blk", split_axis=1, concat_axis=1, tiled=True)
        received = received.reshape(slot_total)
        remote_velocity = received[point_column]
        box_terms = jnp.where(
            in_use, PENALTY * (remote_velocity - velocity[point_node, point_element]), 0.0
        )
        values = jnp.concatenate(
            [jnp.where(is_box, box_terms, 0.0), jnp.where(is_box, 0.0, received * remote_flag)]
        )
        driving = timing[moment] * forcing - assembled
        driving = driving.at[target_rows, target_cols].add(values)
        advanced = 2.0 * current - previous + DT_SQUARED * inverse * driving
        return advanced, current

    current, previous = lax.fori_loop(0, STEPS, one_step, (current, previous))
    return (current[None], previous[None])


LANES = 128
HALF = 64
SLOTS = 6
LAGS = 10
PAIRS = LAGS // 2
FREE_ROWS = STEPS // 2
GAIN_ROW = FREE_ROWS
INDEX_ROW = GAIN_ROW + SLOTS * PAIRS
FLAG_ROW = INDEX_ROW + SLOTS // 2
PAYLOAD = FLAG_ROW + 1
NODES = 125
EXACT = lax.Precision.HIGHEST


def line_matrix():
    abscissae = np.array([-1.0, -np.sqrt(3.0 / 7.0), 0.0, np.sqrt(3.0 / 7.0), 1.0])
    legendre = (35.0 * abscissae**4 - 30.0 * abscissae**2 + 3.0) / 8.0
    derivative = np.zeros((5, 5))
    for i in range(5):
        for j in range(5):
            if i != j:
                derivative[i, j] = legendre[i] / (legendre[j] * (abscissae[i] - abscissae[j]))
    derivative[0, 0] = -2.5
    derivative[4, 4] = 2.5
    return derivative


def apply_line(matrix, x):
    odd = [x[0] - x[4], x[1] - x[3]]
    even = [x[0] + x[4], x[1] + x[3]]
    out = [None] * 5
    for i in range(2):
        symmetric = (
            float(0.5 * (matrix[i, 0] - matrix[i, 4])) * odd[0]
            + float(0.5 * (matrix[i, 1] - matrix[i, 3])) * odd[1]
        )
        skew = (
            float(0.5 * (matrix[i, 0] + matrix[i, 4])) * even[0]
            + float(0.5 * (matrix[i, 1] + matrix[i, 3])) * even[1]
            + float(matrix[i, 2]) * x[2]
        )
        out[i] = symmetric + skew
        out[4 - i] = symmetric - skew
    out[2] = float(matrix[2, 0]) * odd[0] + float(matrix[2, 1]) * odd[1]
    return out


def stiffness_lines(x_ref, scale_ref, y_ref):
    forward = line_matrix()
    backward = forward.T.copy()

    def along(index):
        x = [x_ref[k] for k in index]
        grads = apply_line(forward, x)
        scaled = [g * scale_ref[k] for g, k in zip(grads, index)]
        return apply_line(backward, scaled)

    for b in range(5):
        for c in range(5):
            index = [25 * j + 5 * b + c for j in range(5)]
            for k, value in zip(index, along(index)):
                y_ref[k] = value
    for a in range(5):
        total = [y_ref[25 * a + k] for k in range(25)]
        for c in range(5):
            local = [5 * j + c for j in range(5)]
            for k, value in zip(local, along([25 * a + k for k in local])):
                total[k] = total[k] + value
        for b in range(5):
            local = [5 * b + j for j in range(5)]
            for k, value in zip(local, along([25 * a + k for k in local])):
                total[k] = total[k] + value
        for k in range(25):
            y_ref[25 * a + k] = total[k]


def partner_faces(load, side):
    _, _, faces = node_tables()
    masks = [side == q for q in range(6)]
    arrived = []
    for t in range(25):
        value = jnp.zeros(side.shape, jnp.float32)
        for q in range(6):
            value = jnp.where(masks[q], load(int(faces[q, t])), value)
        arrived.append(pltpu.roll(value, HALF, 1))
    extra = [None] * NODES
    for q in range(6):
        for t in range(25):
            node = int(faces[q, t])
            before = extra[node]
            zero = jnp.zeros(side.shape, jnp.float32) if before is None else before
            extra[node] = jnp.where(masks[q], arrived[t], zero)
    return extra


def across(row_values):
    return jnp.broadcast_to(row_values, (LANES, LANES)).T


def rank_among(row_values):
    down = lax.broadcasted_iota(jnp.int32, (LANES, LANES), 0)
    right = lax.broadcasted_iota(jnp.int32, (LANES, LANES), 1)
    same = (across(row_values) == row_values) & (down < right)
    return jnp.sum(jnp.where(same, 1.0, 0.0), axis=0, keepdims=True)


def one_hot(condition):
    return jnp.where(condition, 1.0, 0.0).astype(jnp.bfloat16)


def plain_dot(a, b):
    return jnp.dot(a.astype(jnp.bfloat16), b, preferred_element_type=jnp.float32)


def exact_pick(values, chosen, transposed=False):
    total = None
    rest = values
    for _ in range(3):
        part = rest.astype(jnp.bfloat16)
        if transposed:
            got = lax.dot_general(
                chosen, part, (((1,), (1,)), ((), ())), preferred_element_type=jnp.float32
            )
        else:
            got = jnp.dot(part, chosen, preferred_element_type=jnp.float32)
        total = got if total is None else total + got
        rest = rest - part.astype(jnp.float32)
    return total


def lane_row():
    return lax.broadcasted_iota(jnp.int32, (1, LANES), 1)


def pack_kernel(
    where_ref,
    wave_ref,
    mass_ref,
    source_ref,
    weight_ref,
    face_ref,
    couple_ref,
    links_ref,
    m0_ref,
    m1_ref,
    m2_ref,
    m3_ref,
    count_ref,
):
    me = where_ref[1]
    me_f = me.astype(jnp.float32)
    is_box = where_ref[0] == 0
    down = lax.broadcasted_iota(jnp.int32, (LANES, LANES), 0)
    right = lax.broadcasted_iota(jnp.int32, (LANES, LANES), 1)
    right_f = right.astype(jnp.float32)
    lane = lane_row()

    live = couple_ref[:, 0:LANES].astype(jnp.float32)
    owner = jnp.where(lane < HALF, live[2:3], -1.0)
    slot = jnp.where(owner >= 0.0, owner * CAPC + rank_among(owner), -1.0)
    to_slot = one_hot(across(slot) == right_f)
    named = jnp.concatenate([live[0:2], live[3:5], jnp.full((4, LANES), -1.0)], axis=0) + 1.0
    links = plain_dot(named, to_slot)
    for k in range(links_ref.shape[0]):
        links_ref[k] = links

    faces = face_ref[0]
    peer = faces[2:3]
    linked = peer != me
    distance = peer ^ me
    bit = jnp.zeros((1, LANES), jnp.float32)
    for j in range(1, 4):
        bit = bit + jnp.where(distance == 1 << j, float(j), 0.0)
    face_slot = jnp.where(linked, bit * 16.0 + rank_among(peer.astype(jnp.float32)), -1.0)
    to_record = one_hot(across(face_slot) == right_f)
    facts = jnp.concatenate([faces[0:2].astype(jnp.float32) + 1.0, jnp.zeros((6, LANES))], axis=0)
    record = plain_dot(facts, to_record)

    node_one = lax.broadcasted_iota(jnp.int32, (LANES, LANES), 0).astype(jnp.float32) + 1.0
    own_nodes = one_hot(node_one == links[1:2])
    point_column = across(links[0:1])
    record_column = across(record[0:1])
    side_column = across(record[1:2])
    counts = []
    taken = []
    for g in range(2):
        column_one = right_f + float(g * LANES + 1)
        counts.append(
            jnp.dot(own_nodes, one_hot(point_column == column_one), preferred_element_type=jnp.float32)
        )
        taken.append(one_hot(record_column == column_one)[:HALF])
    count = jnp.concatenate(counts, axis=1) * jnp.where(is_box, 1.0, 0.0)
    count_ref[...] = count
    take = jnp.concatenate(taken, axis=1)
    pad = jnp.zeros((LANES - NODES, 2 * LANES), jnp.float32)
    stiff = jnp.concatenate([weight_ref[...] * wave_ref[0], pad], axis=0)
    mass = jnp.concatenate([DT_SQUARED * mass_ref[0], pad], axis=0)
    source = jnp.concatenate([source_ref[0], pad], axis=0)
    first = exact_pick(stiff, take, True)
    first = jnp.where(right[:HALF] == 125, record_column[:HALF], first)
    first = jnp.where(right[:HALF] == 126, side_column[:HALF], first)
    parts = [
        first,
        exact_pick(mass, take, True),
        exact_pick(source, take, True),
        lax.dot_general(
            take,
            count.astype(jnp.bfloat16),
            (((1,), (1,)), ((), ())),
            preferred_element_type=jnp.float32,
        ),
    ]
    for j, out in enumerate((m0_ref, m1_ref, m2_ref, m3_ref)):
        for k in range(4):
            out[:, k * LANES : (k + 1) * LANES] = parts[k][16 * j : 16 * j + 16]


def point_tables(where_ref, every_ref):
    me = where_ref[1]
    is_box = where_ref[0] == 0
    lane = lane_row()
    low = lane < HALF
    blocks = every_ref.shape[0]
    down = lax.broadcasted_iota(jnp.int32, (blocks, LANES), 0)
    right = lax.broadcasted_iota(jnp.int32, (blocks, LANES), 1)
    mine = right // CAPC == down
    tables = []
    for offset in (0, 1, 2, 4, 8):
        beta = me ^ offset
        at = beta * CAPC + right % CAPC
        rows = []
        for f in range(2):
            direct = every_ref[beta, f : f + 1, :]
            column = every_ref[:, 2 + f, :]
            picked = jnp.concatenate(
                [
                    jnp.take_along_axis(column[8 * h : 8 * h + 8], at[8 * h : 8 * h + 8], axis=1,
                                        mode="promise_in_bounds")
                    for h in range(blocks // 8)
                ],
                axis=0,
            )
            turned = jnp.sum(jnp.where(mine, picked, 0.0), axis=0, keepdims=True)
            row = jnp.where(is_box, direct, turned)
            rows.append(jnp.where(low, row, 0.0))
        inputs = lane // CAPC * HALF + beta * CAPC + lane % CAPC
        rows.append(jnp.where(low, inputs, 0).astype(jnp.float32))
        tables.append(rows)
    tables.append([jnp.zeros((1, LANES), jnp.float32)] * 3)
    chunks = []
    for c in range(3):
        chunks.append(
            [
                jnp.where(low, tables[2 * c][f], pltpu.roll(tables[2 * c + 1][f], HALF, 1))
                for f in range(3)
            ]
        )
    keys = []
    for c in range(3):
        table = jnp.where(low, float(2 * c), float(2 * c + 1))
        element, node, _ = chunks[c]
        keys.append(jnp.where(node > 0.0, table * 256.0 + element - 1.0, -1.0))
    return chunks, keys


def response_kernel(
    where_ref,
    coef_ref,
    wave_ref,
    mass_ref,
    source_ref,
    weight_ref,
    count_ref,
    m0_ref,
    m1_ref,
    m2_ref,
    m3_ref,
    g0_ref,
    g1_ref,
    g2_ref,
    g3_ref,
    every_ref,
    out_ref,
    pair_ref,
    note_ref,
    data_ref,
    scale_ref,
    x_ref,
    h_ref,
    y_ref,
    t_ref,
    in_ref,
    rec_ref,
    seen_ref,
):
    down = lax.broadcasted_iota(jnp.int32, (LANES, LANES), 0)
    right = lax.broadcasted_iota(jnp.int32, (LANES, LANES), 1)
    right_f = right.astype(jnp.float32)
    lane = lane_row()
    lane_low = lane < HALF
    lane_f = lane.astype(jnp.float32)

    stacked = jnp.concatenate(
        [r[...] for r in (m0_ref, m1_ref, m2_ref, m3_ref, g0_ref, g1_ref, g2_ref, g3_ref)], axis=0
    )
    pair = [stacked[:, k * LANES : (k + 1) * LANES].T for k in range(4)]
    for k in range(4):
        pair_ref[k] = pair[k]
    pair_element = pair[0][125:126]
    pair_side = pair[0][126:127]
    own_column = jnp.broadcast_to(stacked[:HALF, 125:126], (HALF, LANES))
    own_column = jnp.concatenate([own_column, own_column], axis=0)

    chunks, keys = point_tables(where_ref, every_ref)
    element, node, _ = chunks[0]
    element_both = jnp.where(lane_low, element, pltpu.roll(element, HALF, 1))
    node_low = jnp.where(lane_low, node, 0.0)
    present = element_both > 0.0
    same_half = (down < HALF) == (right < HALF)
    of_record = (own_column == element_both) & present & same_half
    facts_matrix = one_hot(of_record)
    partner_matrix = one_hot(of_record & (down >= HALF))
    table_row = jnp.where(lane_low, 0.0, (1 + (lane - HALF) // 16).astype(jnp.float32))
    facts = plain_dot(
        jnp.concatenate([pair_side, pair_element, table_row, jnp.zeros((5, LANES))], axis=0),
        facts_matrix,
    )
    side_row = facts[0:1].astype(jnp.int32) - 1
    partner = pltpu.roll(facts, HALF, 1)
    ghost_key = jnp.where(partner[1:2] > 0.0, partner[2:3] * 256.0 + partner[1:2] - 1.0, -5.0)
    own_key = jnp.where(element > 0.0, element - 1.0, -5.0)
    own_key = jnp.where(lane_low, own_key, -5.0)
    ghost_key = jnp.where(lane_low, ghost_key, -5.0)

    match = [(across(keys[c]) == own_key) | (across(keys[c]) == ghost_key) for c in range(3)]
    matched = [jnp.where(m, 1.0, 0.0) for m in match]
    lower = one_hot(right < down)
    before = jnp.zeros((1, LANES), jnp.float32)
    lists = [jnp.zeros((8, LANES), jnp.float32)] * SLOTS
    for c in range(3):
        place = jnp.dot(lower, matched[c].astype(jnp.bfloat16), preferred_element_type=jnp.float32)
        place = jnp.where(match[c], place + before, -1.0)
        before = before + jnp.sum(matched[c], axis=0, keepdims=True)
        _, node_c, gid_c = chunks[c]
        gid_high = jnp.floor(gid_c * (1.0 / 256.0))
        table_c = jnp.where(lane_low, float(2 * c), float(2 * c + 1))
        described = jnp.concatenate(
            [node_c, gid_high, gid_c - 256.0 * gid_high, table_c, jnp.zeros((4, LANES))], axis=0
        )
        for q in range(SLOTS):
            lists[q] = lists[q] + plain_dot(described, one_hot(place == float(q)))
    too_long = jnp.max(before) > float(SLOTS)
    wanted_rows = []
    gids = []
    for q in range(SLOTS):
        node_q = lists[q][0:1] - 1.0
        there = lists[q][3:4] > 0.0
        gids.append(lists[q][1:2] * 256.0 + lists[q][2:3])
        wanted_rows.append(
            jnp.where(
                lane_low,
                jnp.where(there, -1.0, node_q),
                pltpu.roll(jnp.where(there, node_q, -1.0), HALF, 1),
            )
        )
    own_node = jnp.where(lane_low, node - 1.0, -1.0)
    wanted_rows.append(own_node)
    wanted_rows.append(jnp.full((1, LANES), -1.0))
    wanted = jnp.concatenate(wanted_rows, axis=0).astype(jnp.int32)

    take = [
        one_hot((down.astype(jnp.float32) + float(g * LANES + 1) == element_both) & (right < HALF))
        for g in range(2)
    ]
    take = jnp.concatenate(take, axis=0)
    own_fields = [
        weight_ref[...] * wave_ref[0],
        DT_SQUARED * mass_ref[0],
        source_ref[0],
        count_ref[...][:NODES],
    ]
    for k in range(4):
        copy = exact_pick(own_fields[k], take) + exact_pick(pair[k], partner_matrix)[:NODES]
        data_ref[k, 0:NODES] = PENALTY * copy if k == 3 else copy

    home = []
    for g in range(2):
        hit = one_hot(own_column[:HALF] == right_f[:HALF] + float(g * LANES + 1))
        home.append(
            jnp.dot(
                jnp.broadcast_to(lane_f[:, :HALF] + 1.0, (8, HALF)).astype(jnp.bfloat16),
                hit,
                preferred_element_type=jnp.float32,
            )[0:1]
            - 1.0
        )
    pair_key = jnp.where(pair_element > 0.0, table_row * 256.0 + pair_element - 1.0, -3.0)
    notes = (
        [chunks[c][2] for c in range(3)]
        + [chunks[c][1] - 1.0 for c in range(3)]
        + keys
        + [pair_key, lane_f, lane_f + float(LANES)]
        + [pair_side - 1.0]
        + home
        + [jnp.zeros((1, LANES), jnp.float32)]
    )
    note_ref[...] = jnp.concatenate(notes, axis=0)

    row = lax.broadcasted_iota(jnp.int32, (8, LANES), 0)
    low = lax.broadcasted_iota(jnp.int32, (8, LANES), 1) < HALF
    first = row == 0
    side = jnp.where(row < 2, jnp.broadcast_to(side_row, (8, LANES)), -1)
    forced = row == SLOTS
    shape = (8, LANES)
    start_node = own_node.astype(jnp.int32)

    def tile(k, n):
        return jnp.broadcast_to(data_ref[k, n : n + 1], shape)

    for n in range(NODES):
        x_ref[n] = jnp.where((row == 1) & (start_node == n), 1.0, 0.0)
        h_ref[n] = jnp.zeros(shape, jnp.float32)
        y_ref[n] = jnp.zeros(shape, jnp.float32)
        scale_ref[n] = tile(0, n)

    is_box = jnp.where(where_ref[0] == 0, 1.0, 0.0)

    def step(moment, _):
        drive = coef_ref[0, moment]
        keep = jnp.where(moment > 0, 1.0, 0.0)
        stiff = jnp.where(moment > 0, -1.0, is_box)
        begin = jnp.where(moment > 0, 0.0, 1.0 - is_box)
        for n in range(NODES):
            t_ref[n] = jnp.where(first, y_ref[n], x_ref[n])
        extra = partner_faces(lambda k: t_ref[k], side)
        for n in range(NODES):
            assembled = t_ref[n] if extra[n] is None else t_ref[n] + extra[n]
            inverse = tile(1, n)
            force = tile(2, n)
            damp = tile(3, n)
            x = x_ref[n]
            h = h_ref[n]
            advanced = 2.0 * x - h + inverse * (drive * force - assembled - damp * x)
            in_ref[n] = jnp.where(first, advanced, assembled)
            rec_ref[n] = is_box * assembled + (1.0 - is_box) * (x - h)
        stiffness_lines(in_ref, scale_ref, y_ref)
        seen = jnp.zeros(shape, jnp.float32)
        for n in range(NODES):
            inverse = tile(1, n)
            damp = tile(3, n)
            x = x_ref[n]
            h = h_ref[n]
            dx = damp * x
            adjoint = 2.0 * keep * x - h + inverse * (stiff * y_ref[n] - keep * dx + begin * x)
            x_ref[n] = jnp.where(first, in_ref[n], adjoint)
            h_ref[n] = keep * (x - inverse * dx) + begin * (inverse * x)
            source = jnp.where(
                forced,
                jnp.broadcast_to(rec_ref[n][0:1], shape),
                jnp.broadcast_to(adjoint[1:2], shape),
            )
            seen = seen + jnp.where(wanted == n, source, 0.0)
        seen_ref[moment] = seen + pltpu.roll(seen, HALF, 1)
        return 0

    lax.fori_loop(0, STEPS, step, 0)
    for k in range(FREE_ROWS):
        out_ref[0, k : k + 1] = jnp.where(
            lane_low,
            seen_ref[2 * k][SLOTS : SLOTS + 1],
            seen_ref[2 * k + 1][SLOTS : SLOTS + 1],
        )
    for q in range(SLOTS):
        for k in range(PAIRS):
            r = GAIN_ROW + q * PAIRS + k
            out_ref[0, r : r + 1] = jnp.where(
                lane_low, seen_ref[2 * k][q : q + 1], seen_ref[2 * k + 1][q : q + 1]
            )
    for q in range(0, SLOTS, 2):
        r = INDEX_ROW + q // 2
        out_ref[0, r : r + 1] = jnp.where(lane_low, gids[q], pltpu.roll(gids[q + 1], HALF, 1))
    out_ref[0, FLAG_ROW : FLAG_ROW + 1] = jnp.full((1, LANES), jnp.where(too_long, 1.0, 0.0))
    for k in range(1, out_ref.shape[0]):
        out_ref[k] = out_ref[0]


def gather_packed(packed, at):
    rows = at // LANES
    lanes = at % LANES
    out = jnp.zeros(at.shape, jnp.float32)
    for k in range(8):
        source = jnp.broadcast_to(packed[k : k + 1], at.shape)
        picked = jnp.take_along_axis(source, lanes, axis=1, mode="promise_in_bounds")
        out = jnp.where(rows == k, picked, out)
    return out


def final_kernel(
    where_ref,
    time_ref,
    mine_ref,
    other_ref,
    wave_ref,
    mass_ref,
    source_ref,
    weight_ref,
    count_ref,
    pair_ref,
    note_ref,
    now_ref,
    before_ref,
    both_ref,
    spread_ref,
    input_ref,
    data_ref,
    x_ref,
    h_ref,
    y_ref,
    kick_ref,
    flat_ref,
):
    is_box = where_ref[0] == 0
    parity = where_ref[1] % 2
    both_ref[parity] = mine_ref[...]
    both_ref[1 - parity] = other_ref[...]
    low = lax.broadcasted_iota(jnp.int32, (8, LANES), 1) < HALF

    def rows(section, core, r):
        return both_ref[core, section * 8 : section * 8 + 8, r, :]

    index = {}
    for s in range(2):
        for p in range(2):
            for k in range(SLOTS // 2):
                pair = rows(s, p, INDEX_ROW + k).astype(jnp.int32)
                turned = pltpu.roll(pair, HALF, 1)
                index[s, p, 2 * k] = jnp.where(low, pair, turned)
                index[s, p, 2 * k + 1] = jnp.where(low, turned, pair)
    note = note_ref[...]
    at = jnp.where(lax.broadcasted_iota(jnp.int32, (8, LANES), 0) < 3, note[0:8], 0.0).astype(jnp.int32)
    packed = {}
    pairs = {}
    last = {}
    zero = jnp.zeros((8, LANES), jnp.float32)
    for n in range(1, STEPS):
        value = {}
        for s in range(2):
            for p in range(2):
                free = rows(s, p, n // 2)
                total = jnp.where(low, free, 0.0) if n % 2 == 0 else jnp.where(low, 0.0, free)
                for q in range(SLOTS):
                    for k in range(PAIRS):
                        m = n - 2 * k - 1
                        if m >= 1:
                            total = total + rows(s, p, GAIN_ROW + q * PAIRS + k) * pairs[s, p, q, m]
                value[s, p] = total + pltpu.roll(total, HALF, 1)
        for s in range(2):
            packed[s] = jnp.where(low, value[s, 0], value[s, 1])
        packed[1] = PENALTY * packed[1]
        input_ref[n] = gather_packed(jnp.where(is_box, packed[1], packed[0]), at)
        if n < STEPS - 1:
            for s in range(2):
                for p in range(2):
                    for q in range(SLOTS):
                        got = gather_packed(packed[1 - s], index[s, p, q])
                        pairs[s, p, q, n] = jnp.where(low, got, last.get((s, p, q), zero))
                        last[s, p, q] = got
    input_ref[0] = zero
    for c in range(3):
        point_key = across(note[6 + c : 7 + c])
        for g in range(3):
            spread_ref[c, :, g * LANES : (g + 1) * LANES] = one_hot(
                point_key == note[9 + g : 10 + g]
            )
    group = lax.broadcasted_iota(jnp.int32, (3, LANES), 0)
    side = jnp.where(group == 0, note[12:13].astype(jnp.int32), -1)
    own_fields = [
        weight_ref[...] * wave_ref[0],
        DT_SQUARED * mass_ref[0],
        source_ref[0],
        count_ref[...][:NODES],
    ]
    for k in range(4):
        flat_ref[0:LANES] = pair_ref[k]
        flat_ref[LANES : LANES + NODES] = own_fields[k][:, :LANES]
        flat_ref[2 * LANES : 2 * LANES + NODES] = own_fields[k][:, LANES:]
        for n in range(NODES):
            value = flat_ref[pl.ds(n, 3, stride=LANES)]
            data_ref[k, n] = PENALTY * value if k == 3 else value
    for n in range(NODES):
        x_ref[n] = zero[:3]
        h_ref[n] = zero[:3]
        y_ref[n] = zero[:3]
    point_node = note[3:6].astype(jnp.int32)
    node_row = lax.broadcasted_iota(jnp.int32, (LANES, LANES), 0)

    def step(moment, _):
        drive = time_ref[0, moment]
        inputs = input_ref[moment]
        kick = jnp.zeros((LANES, 3 * LANES), jnp.float32)
        for c in range(3):
            chosen = jnp.where(node_row == point_node[c : c + 1], inputs[c : c + 1], 0.0)
            for _ in range(3):
                part = chosen.astype(jnp.bfloat16)
                kick = kick + jnp.dot(part, spread_ref[c], preferred_element_type=jnp.float32)
                chosen = chosen - part.astype(jnp.float32)
        for c in range(3):
            kick_ref[c * LANES : (c + 1) * LANES] = kick[:, c * LANES : (c + 1) * LANES]
        extra = partner_faces(lambda k: y_ref[k], side)
        for n in range(NODES):
            assembled = y_ref[n] if extra[n] is None else y_ref[n] + extra[n]
            inverse = data_ref[1, n]
            damp = data_ref[3, n]
            x = x_ref[n]
            h = h_ref[n]
            arrived = kick_ref[pl.ds(n, 3, stride=LANES)]
            dx = damp * x
            advanced = 2.0 * x - h + inverse * (drive * data_ref[2, n] - assembled - dx + arrived)
            h_ref[n] = x - inverse * dx
            flat_ref[pl.ds(n, 3, stride=LANES)] = x
            x_ref[n] = advanced
        stiffness_lines(x_ref, data_ref.at[0], y_ref)
        return 0

    lax.fori_loop(0, STEPS, step, 0)
    home = jnp.concatenate([note[13:14], note[14:15]], axis=1).astype(jnp.int32)
    linked = jnp.where(
        home == lax.broadcasted_iota(jnp.int32, (LANES, 2 * LANES), 0), 1.0, 0.0
    ).astype(jnp.bfloat16)
    alone = home < 0

    def put(out_ref):
        rest = flat_ref[0:LANES]
        moved = jnp.zeros((LANES, 2 * LANES), jnp.float32)
        for _ in range(3):
            part = rest.astype(jnp.bfloat16)
            moved = moved + jnp.dot(part, linked, preferred_element_type=jnp.float32)
            rest = rest - part.astype(jnp.float32)
        for g in range(2):
            own = flat_ref[(g + 1) * LANES : (g + 2) * LANES]
            cut = slice(g * LANES, (g + 1) * LANES)
            merged = jnp.where(alone[:, cut], own, moved[:, cut])
            out_ref[0, :, cut] = merged[:NODES]

    put(before_ref)
    for n in range(NODES):
        flat_ref[pl.ds(n, 3, stride=LANES)] = x_ref[n]
    put(now_ref)


def fast_body(wave_speed, inverse_mass, source_field, source_time, face_links, coupling_links):
    _, weight_np, _ = node_tables()
    weight = jnp.asarray(weight_np).reshape(NODES, 1)
    blocks = lax.axis_size("blk")
    columns = wave_speed.shape[-1]
    me = lax.axis_index("blk")
    place = jnp.stack([lax.axis_index("sec"), me]).astype(jnp.int32)
    vmem = pl.BlockSpec(memory_space=pltpu.VMEM)
    smem = pl.BlockSpec(memory_space=pltpu.SMEM)

    def shape(*dims):
        return jax.ShapeDtypeStruct(dims, jnp.float32)

    links, m0, m1, m2, m3, count = pl.pallas_call(
        pack_kernel,
        out_shape=[shape(blocks, 8, LANES)] + [shape(16, 4 * LANES)] * 4 + [shape(LANES, columns)],
        in_specs=[smem] + [vmem] * 6,
        out_specs=[vmem] * 6,
    )(place, wave_speed, inverse_mass, source_field, weight, face_links, coupling_links)
    every = lax.all_to_all(links, "blk", 0, 0, tiled=True)
    mine = [m0, m1, m2, m3]
    ghost = [partner_2(part, "blk", j) for j, part in enumerate(mine)]
    full = pltpu.VMEM((NODES, 8, LANES), jnp.float32)
    payload, pair, note = pl.pallas_call(
        response_kernel,
        out_shape=[shape(blocks, PAYLOAD, LANES), shape(4, LANES, LANES), shape(16, LANES)],
        in_specs=[smem] * 2 + [vmem] * 14,
        out_specs=[vmem] * 3,
        scratch_shapes=[pltpu.VMEM((4, LANES, LANES), jnp.float32)]
        + [full] * 7
        + [pltpu.VMEM((STEPS, 8, LANES), jnp.float32)],
    )(
        place,
        source_time,
        wave_speed,
        inverse_mass,
        source_field,
        weight,
        count,
        *mine,
        *ghost,
        every,
    )

    same_core = [[c + 2 * i for i in range(blocks)] for c in range(2)]
    received = lax.all_to_all(
        payload, ("sec", "blk"), 0, 0, axis_index_groups=same_core, tiled=True
    )
    sibling = partner_2(received, "blk", 0)
    overflow = jnp.max(
        jnp.maximum(received[:, FLAG_ROW, 0], sibling[:, FLAG_ROW, 0])
    ) > 0
    three = pltpu.VMEM((NODES, 3, LANES), jnp.float32)

    def quick(_):
        return tuple(
            pl.pallas_call(
                final_kernel,
                out_shape=[shape(1, NODES, columns)] * 2,
                in_specs=[smem] * 2 + [vmem] * 9,
                out_specs=[vmem] * 2,
                scratch_shapes=[
                    pltpu.VMEM((2, blocks, PAYLOAD, LANES), jnp.float32),
                    pltpu.VMEM((3, LANES, 3 * LANES), jnp.bfloat16),
                    pltpu.VMEM((STEPS, 8, LANES), jnp.float32),
                    pltpu.VMEM((4, NODES, 3, LANES), jnp.float32),
                    three,
                    three,
                    three,
                    pltpu.VMEM((3 * LANES, LANES), jnp.float32),
                    pltpu.VMEM((3 * LANES, LANES), jnp.float32),
                ],
            )(
                place,
                source_time,
                received,
                sibling,
                wave_speed,
                inverse_mass,
                source_field,
                weight,
                count,
                pair,
                note,
            )
        )

    def slow(_):
        return general_body(
            wave_speed, inverse_mass, source_field, source_time, face_links, coupling_links
        )

    return lax.cond(overflow, slow, quick, 0)


def body(*arguments):
    wave_speed, _, _, _, face_links, coupling_links = arguments
    fits = (
        lax.axis_size("blk") == 16
        and lax.axis_size("sec") == 2
        and wave_speed.shape[1:] == (NODES, 2 * LANES)
        and face_links.shape[-1] == LANES
        and coupling_links.shape[-1] >= CAPC * 16
    )
    return fast_body(*arguments) if fits else general_body(*arguments)


def solution(mesh):
    in_specs = (
        P("sec", None, "blk"),
        P("sec", None, "blk"),
        P("sec", None, "blk"),
        P("sec", None),
        P("sec", None, "blk"),
        P(None, "blk"),
    )
    out_specs = (P("sec", None, "blk"), P("sec", None, "blk"))
    return jax.shard_map(body, mesh=mesh, in_specs=in_specs, out_specs=out_specs, check_vma=False)
```

```python
import jax
import jax.numpy as jnp
import numpy as np
from jax import lax
from jax.experimental import pallas as pl
from jax.experimental.pallas import tpu as pltpu
from jax.sharding import PartitionSpec as P

CAPC = 4
STEPS = 12


DT_SQUARED = 0.05
PENALTY = 10.0


def partner_2(value, axis, stride):
    return lax.ppermute(value, axis, [(i, i ^ 1 << stride) for i in range(lax.axis_size(axis))])


def node_tables():
    abscissae = np.array([-1.0, -np.sqrt(3.0 / 7.0), 0.0, np.sqrt(3.0 / 7.0), 1.0])
    weights = np.array([0.1, 49.0 / 90.0, 32.0 / 45.0, 49.0 / 90.0, 0.1])
    legendre = (35.0 * abscissae**4 - 30.0 * abscissae**2 + 3.0) / 8.0
    derivative = np.zeros((5, 5))
    for i in range(5):
        for j in range(5):
            if i != j:
                derivative[i, j] = legendre[i] / (legendre[j] * (abscissae[i] - abscissae[j]))
    derivative[0, 0] = -2.5
    derivative[4, 4] = 2.5
    identity = np.eye(5)
    operator = np.concatenate(
        [
            np.kron(np.kron(derivative, identity), identity),
            np.kron(np.kron(identity, derivative), identity),
            np.kron(np.kron(identity, identity), derivative),
        ],
        axis=0,
    )
    weight_cube = weights[:, None, None] * weights[None, :, None] * weights[None, None, :]
    lattice = np.arange(125).reshape(5, 5, 5)
    face_nodes = np.stack(
        [
            lattice[0].ravel(),
            lattice[4].ravel(),
            lattice[:, 0].ravel(),
            lattice[:, 4].ravel(),
            lattice[:, :, 0].ravel(),
            lattice[:, :, 4].ravel(),
        ]
    )
    return (
        operator.astype(np.float32),
        weight_cube.reshape(125, 1).astype(np.float32),
        face_nodes.astype(np.int32),
    )


def stiffness(field_in, speed_sq, operator, weight_cube):
    columns = field_in.shape[-1]
    scaling = weight_cube * speed_sq
    grads = jnp.dot(
        operator, field_in, precision=lax.Precision.HIGHEST, preferred_element_type=jnp.float32
    )
    scaled = (grads.reshape(3, 125, columns) * scaling[None]).reshape(375, columns)
    return jnp.dot(
        operator.T, scaled, precision=lax.Precision.HIGHEST, preferred_element_type=jnp.float32
    )


def general_body(wave_speed, inverse_mass, source_field, source_time, face_links, coupling_links):
    operator_np, weight_np, faces_np = node_tables()
    operator = jnp.asarray(operator_np)
    weight_cube = jnp.asarray(weight_np)
    picker_np = np.zeros((150, 125), np.float32)
    for side_number in range(6):
        for node_number in range(25):
            picker_np[side_number * 25 + node_number, faces_np[side_number, node_number]] = 1.0
    picker = jnp.asarray(picker_np)
    spreader = jnp.asarray(picker_np.T.copy())
    speed_sq = wave_speed[0]
    inverse = inverse_mass[0]
    forcing = source_field[0]
    timing = source_time[0]
    element = face_links[0, 0]
    face_side = face_links[0, 1]
    face_peer = face_links[0, 2]
    blocks = lax.axis_size("blk")
    bit_count = blocks.bit_length() - 1
    myself = lax.axis_index("blk")
    is_box = lax.axis_index("sec") == 0
    records = element.shape[0]
    per_peer = records // 8
    ordinal = jnp.arange(records)
    linked = face_peer != myself
    side_mask = face_side[None, None, :] == jnp.arange(6, dtype=jnp.int32)[:, None, None]
    earlier = ordinal[None, :] < ordinal[:, None]
    face_slot = jnp.sum(
        ((face_peer[:, None] == face_peer[None, :]) & earlier).astype(jnp.int32), axis=1
    )
    offset_bits = jnp.bitwise_xor(face_peer, myself)
    bit_index = jnp.zeros((records,), jnp.int32)
    for bit_number in range(bit_count):
        bit_index = bit_index + bit_number * (offset_bits == 1 << bit_number).astype(jnp.int32)
    pair_column = jnp.where(linked, bit_index * per_peer + face_slot, 0)
    point_element = coupling_links[0]
    point_node = coupling_links[1]
    point_owner = coupling_links[2]
    target_element = coupling_links[3]
    target_node = coupling_links[4]
    in_use = point_owner >= 0
    owner_safe = jnp.maximum(point_owner, 0)
    point_ordinal = jnp.arange(point_owner.shape[0])
    point_earlier = point_ordinal[None, :] < point_ordinal[:, None]
    point_slot = jnp.sum(
        ((point_owner[:, None] == point_owner[None, :]) & point_earlier).astype(jnp.int32), axis=1
    )
    point_column = jnp.where(in_use, point_slot * blocks + owner_safe, 0)
    slot_total = CAPC * blocks
    outbound = jnp.zeros((3, slot_total), jnp.int32)
    outbound = outbound.at[0, point_column].add(jnp.where(in_use, target_element, 0))
    outbound = outbound.at[1, point_column].add(jnp.where(in_use, target_node, 0))
    outbound = outbound.at[2, point_column].add(in_use.astype(jnp.int32))
    inbound = lax.all_to_all(
        outbound.reshape(3, CAPC, blocks), "blk", split_axis=2, concat_axis=2, tiled=True
    ).reshape(3, slot_total)
    remote_element = inbound[0]
    remote_node = inbound[1]
    remote_flag = inbound[2].astype(jnp.float32)
    target_rows = jnp.concatenate([point_node, remote_node])
    target_cols = jnp.concatenate([point_element, remote_element])
    current = jnp.zeros(speed_sq.shape, jnp.float32)
    previous = jnp.zeros(speed_sq.shape, jnp.float32)
    def one_step(moment, state):
        current, previous = state
        internal = stiffness(current, speed_sq, operator, weight_cube)
        stacked = jnp.dot(
            picker,
            internal[:, element],
            precision=lax.Precision.HIGHEST,
            preferred_element_type=jnp.float32,
        ).reshape(6, 25, records)
        payload = jnp.sum(jnp.where(side_mask, stacked, 0.0), axis=0)
        payload = jnp.where(linked[None, :], payload, 0.0)
        outgoing = (
            jnp.zeros((25, bit_count * per_peer), jnp.float32).at[:, pair_column].add(payload)
        )
        arrived = []
        for bit_number in range(bit_count):
            piece = outgoing[:, bit_number * per_peer : (bit_number + 1) * per_peer]
            arrived.append(partner_2(piece, "blk", bit_number))
        partner = jnp.concatenate(arrived, axis=1)[:, pair_column]
        partner = jnp.where(linked[None, :], partner, 0.0)
        masked = jnp.where(side_mask, partner[None], 0.0).reshape(150, records)
        assembled = internal.at[:, element].add(
            jnp.dot(
                spreader,
                masked,
                precision=lax.Precision.HIGHEST,
                preferred_element_type=jnp.float32,
            )
        )
        velocity = current - previous
        traction = assembled[point_node, point_element]
        box_send = (
            jnp.zeros((slot_total,), jnp.float32)
            .at[point_column]
            .add(jnp.where(in_use, traction, 0.0))
        )
        global_send = velocity[remote_node, remote_element] * remote_flag
        dispatch = jnp.where(is_box, box_send, global_send).reshape(CAPC, blocks)
        crossed = partner_2(dispatch, "sec", 0)
        received = lax.all_to_all(crossed, "blk", split_axis=1, concat_axis=1, tiled=True)
        received = received.reshape(slot_total)
        remote_velocity = received[point_column]
        box_terms = jnp.where(
            in_use, PENALTY * (remote_velocity - velocity[point_node, point_element]), 0.0
        )
        values = jnp.concatenate(
            [jnp.where(is_box, box_terms, 0.0), jnp.where(is_box, 0.0, received * remote_flag)]
        )
        driving = timing[moment] * forcing - assembled
        driving = driving.at[target_rows, target_cols].add(values)
        advanced = 2.0 * current - previous + DT_SQUARED * inverse * driving
        return advanced, current

    current, previous = lax.fori_loop(0, STEPS, one_step, (current, previous))
    return (current[None], previous[None])


LANES = 128
HALF = 64
SLOTS = 6
LAGS = 10
PAIRS = LAGS // 2
FREE_ROWS = STEPS // 2
GAIN_ROW = FREE_ROWS
INDEX_ROW = GAIN_ROW + SLOTS * PAIRS
FLAG_ROW = INDEX_ROW + SLOTS // 2
PAYLOAD = FLAG_ROW + 1
NODES = 125
EXACT = lax.Precision.HIGHEST


def line_matrix():
    abscissae = np.array([-1.0, -np.sqrt(3.0 / 7.0), 0.0, np.sqrt(3.0 / 7.0), 1.0])
    legendre = (35.0 * abscissae**4 - 30.0 * abscissae**2 + 3.0) / 8.0
    derivative = np.zeros((5, 5))
    for i in range(5):
        for j in range(5):
            if i != j:
                derivative[i, j] = legendre[i] / (legendre[j] * (abscissae[i] - abscissae[j]))
    derivative[0, 0] = -2.5
    derivative[4, 4] = 2.5
    return derivative


def apply_line(matrix, x):
    odd = [x[0] - x[4], x[1] - x[3]]
    even = [x[0] + x[4], x[1] + x[3]]
    out = [None] * 5
    for i in range(2):
        symmetric = (
            float(0.5 * (matrix[i, 0] - matrix[i, 4])) * odd[0]
            + float(0.5 * (matrix[i, 1] - matrix[i, 3])) * odd[1]
        )
        skew = (
            float(0.5 * (matrix[i, 0] + matrix[i, 4])) * even[0]
            + float(0.5 * (matrix[i, 1] + matrix[i, 3])) * even[1]
            + float(matrix[i, 2]) * x[2]
        )
        out[i] = symmetric + skew
        out[4 - i] = symmetric - skew
    out[2] = float(matrix[2, 0]) * odd[0] + float(matrix[2, 1]) * odd[1]
    return out


def line_tiles():
    row = lax.broadcasted_iota(jnp.int32, (8, LANES), 0)
    tiles = []
    for matrix in (line_matrix(), line_matrix().T):
        columns = []
        for j in range(5):
            tile = jnp.zeros((8, LANES), jnp.float32)
            for i in range(5):
                tile = jnp.where(row == i, float(matrix[i, j]), tile)
            columns.append(tile)
        tiles.append(columns)
    return tiles


def tile_of(ref, bc, group=0, groups=1):
    start = (bc * groups + group) * 8
    return ref[start : start + 8, :]


def set_tile(ref, value, bc, group=0, groups=1):
    start = (bc * groups + group) * 8
    ref[start : start + 8, :] = value


def repeat_row(ref, row):
    return jnp.broadcast_to(ref[row : row + 1, :], (8, LANES))


def stiffness_tiles(x_ref, scale_ref, y_ref, grad_ref, groups, shared):
    forward = line_matrix()
    backward = forward.T.copy()
    to_grad, to_node = line_tiles()

    for g in range(groups):

        def scale(bc):
            return tile_of(scale_ref, bc) if shared else tile_of(scale_ref, bc, g, groups)

        def along(index):
            grads = apply_line(forward, [tile_of(x_ref, k, g, groups) for k in index])
            return apply_line(backward, [v * scale(k) for v, k in zip(grads, index)])

        for bc in range(25):
            start = (bc * groups + g) * 8
            total = to_grad[0] * repeat_row(x_ref, start)
            for j in range(1, 5):
                total = total + to_grad[j] * repeat_row(x_ref, start + j)
            grad_ref[start : start + 8, :] = total * scale(bc)
        total = [None] * 25
        for c in range(5):
            index = [5 * j + c for j in range(5)]
            for k, value in zip(index, along(index)):
                total[k] = value
        for b in range(5):
            index = [5 * b + j for j in range(5)]
            for k, value in zip(index, along(index)):
                total[k] = total[k] + value
        for bc in range(25):
            start = (bc * groups + g) * 8
            value = total[bc]
            for j in range(5):
                value = value + to_node[j] * repeat_row(grad_ref, start + j)
            set_tile(y_ref, value, bc, g, groups)


def partner_faces(ref, face_ref, side, group=0, groups=1):
    row = lax.broadcasted_iota(jnp.int32, (8, LANES), 0)
    is_side = [side == q for q in range(6)]
    on_a = (is_side[0] & (row == 0)) | (is_side[1] & (row == 4))
    arrived = []
    for t in range(5):
        first = ref[pl.ds((t * groups + group) * 8, 8, stride=40 * groups), :]
        last = ref[pl.ds((t * groups + group) * 8 + 4, 8, stride=40 * groups), :]
        value = jnp.where(is_side[1], last, first)
        value = jnp.where(is_side[2], tile_of(ref, t, group, groups), value)
        value = jnp.where(is_side[3], tile_of(ref, 20 + t, group, groups), value)
        value = jnp.where(is_side[4], tile_of(ref, 5 * t, group, groups), value)
        value = jnp.where(is_side[5], tile_of(ref, 5 * t + 4, group, groups), value)
        value = pltpu.roll(value, HALF, 1)
        arrived.append(value)
        set_tile(face_ref, value, t)
    extra = []
    for b in range(5):
        for c in range(5):
            value = jnp.where(on_a, repeat_row(face_ref, 8 * c + b), 0.0)
            if b == 0:
                value = jnp.where(is_side[2], arrived[c], value)
            if b == 4:
                value = jnp.where(is_side[3], arrived[c], value)
            if c == 0:
                value = jnp.where(is_side[4], arrived[b], value)
            if c == 4:
                value = jnp.where(is_side[5], arrived[b], value)
            extra.append(value)
    return extra


def load_tiles(flat_ref, out_ref, factor=None, group=0, groups=1, start=0):
    for bc in range(25):
        value = flat_ref[pl.ds(start + bc, 8, stride=25), :]
        set_tile(out_ref, value if factor is None else factor * value, bc, group, groups)


def across(row_values):
    return jnp.broadcast_to(row_values, (LANES, LANES)).T


def rank_among(row_values):
    down = lax.broadcasted_iota(jnp.int32, (LANES, LANES), 0)
    right = lax.broadcasted_iota(jnp.int32, (LANES, LANES), 1)
    same = (across(row_values) == row_values) & (down < right)
    return jnp.sum(jnp.where(same, 1.0, 0.0), axis=0, keepdims=True)


def one_hot(condition):
    return jnp.where(condition, 1.0, 0.0).astype(jnp.bfloat16)


def plain_dot(a, b):
    return jnp.dot(a.astype(jnp.bfloat16), b, preferred_element_type=jnp.float32)


def exact_pick(values, chosen, transposed=False):
    total = None
    rest = values
    for _ in range(3):
        part = rest.astype(jnp.bfloat16)
        if transposed:
            got = lax.dot_general(
                chosen, part, (((1,), (1,)), ((), ())), preferred_element_type=jnp.float32
            )
        else:
            got = jnp.dot(part, chosen, preferred_element_type=jnp.float32)
        total = got if total is None else total + got
        rest = rest - part.astype(jnp.float32)
    return total


def lane_row():
    return lax.broadcasted_iota(jnp.int32, (1, LANES), 1)


def pack_kernel(
    where_ref,
    wave_ref,
    mass_ref,
    source_ref,
    weight_ref,
    face_ref,
    couple_ref,
    links_ref,
    m0_ref,
    m1_ref,
    m2_ref,
    m3_ref,
    count_ref,
):
    me = where_ref[1]
    me_f = me.astype(jnp.float32)
    is_box = where_ref[0] == 0
    down = lax.broadcasted_iota(jnp.int32, (LANES, LANES), 0)
    right = lax.broadcasted_iota(jnp.int32, (LANES, LANES), 1)
    right_f = right.astype(jnp.float32)
    lane = lane_row()

    live = couple_ref[:, 0:LANES].astype(jnp.float32)
    owner = jnp.where(lane < HALF, live[2:3], -1.0)
    slot = jnp.where(owner >= 0.0, owner * CAPC + rank_among(owner), -1.0)
    to_slot = one_hot(across(slot) == right_f)
    named = jnp.concatenate([live[0:2], live[3:5], jnp.full((4, LANES), -1.0)], axis=0) + 1.0
    links = plain_dot(named, to_slot)
    for k in range(links_ref.shape[0]):
        links_ref[k] = links

    faces = face_ref[:, 0, :]
    peer = faces[2:3]
    linked = peer != me
    distance = peer ^ me
    bit = jnp.zeros((1, LANES), jnp.float32)
    for j in range(1, 4):
        bit = bit + jnp.where(distance == 1 << j, float(j), 0.0)
    face_slot = jnp.where(linked, bit * 16.0 + rank_among(peer.astype(jnp.float32)), -1.0)
    to_record = one_hot(across(face_slot) == right_f)
    facts = jnp.concatenate([faces[0:2].astype(jnp.float32) + 1.0, jnp.zeros((6, LANES))], axis=0)
    record = plain_dot(facts, to_record)

    node_one = lax.broadcasted_iota(jnp.int32, (LANES, LANES), 0).astype(jnp.float32) + 1.0
    own_nodes = one_hot(node_one == links[1:2])
    point_column = across(links[0:1])
    record_column = across(record[0:1])
    side_column = across(record[1:2])
    counts = []
    taken = []
    for g in range(2):
        column_one = right_f + float(g * LANES + 1)
        counts.append(
            jnp.dot(own_nodes, one_hot(point_column == column_one), preferred_element_type=jnp.float32)
        )
        taken.append(one_hot(record_column == column_one)[:HALF])
    count = jnp.concatenate(counts, axis=1) * jnp.where(is_box, 1.0, 0.0)
    count_ref[...] = count
    take = jnp.concatenate(taken, axis=1)
    pad = jnp.zeros((LANES - NODES, 2 * LANES), jnp.float32)
    stiff = jnp.concatenate([weight_ref[...] * wave_ref[:, 0, :], pad], axis=0)
    mass = jnp.concatenate([DT_SQUARED * mass_ref[:, 0, :], pad], axis=0)
    source = jnp.concatenate([source_ref[:, 0, :], pad], axis=0)
    first = exact_pick(stiff, take, True)
    first = jnp.where(right[:HALF] == 125, record_column[:HALF], first)
    first = jnp.where(right[:HALF] == 126, side_column[:HALF], first)
    parts = [
        first,
        exact_pick(mass, take, True),
        exact_pick(source, take, True),
        lax.dot_general(
            take,
            count.astype(jnp.bfloat16),
            (((1,), (1,)), ((), ())),
            preferred_element_type=jnp.float32,
        ),
    ]
    for j, out in enumerate((m0_ref, m1_ref, m2_ref, m3_ref)):
        for k in range(4):
            out[:, k * LANES : (k + 1) * LANES] = parts[k][16 * j : 16 * j + 16]


def point_tables(where_ref, every_ref):
    me = where_ref[1]
    is_box = where_ref[0] == 0
    lane = lane_row()
    low = lane < HALF
    blocks = every_ref.shape[0]
    down = lax.broadcasted_iota(jnp.int32, (blocks, LANES), 0)
    right = lax.broadcasted_iota(jnp.int32, (blocks, LANES), 1)
    mine = right // CAPC == down
    tables = []
    for offset in (0, 1, 2, 4, 8):
        beta = me ^ offset
        at = beta * CAPC + right % CAPC
        rows = []
        for f in range(2):
            direct = every_ref[beta, f : f + 1, :]
            column = every_ref[:, 2 + f, :]
            picked = jnp.concatenate(
                [
                    jnp.take_along_axis(column[8 * h : 8 * h + 8], at[8 * h : 8 * h + 8], axis=1,
                                        mode="promise_in_bounds")
                    for h in range(blocks // 8)
                ],
                axis=0,
            )
            turned = jnp.sum(jnp.where(mine, picked, 0.0), axis=0, keepdims=True)
            row = jnp.where(is_box, direct, turned)
            rows.append(jnp.where(low, row, 0.0))
        inputs = lane // CAPC * HALF + beta * CAPC + lane % CAPC
        rows.append(jnp.where(low, inputs, 0).astype(jnp.float32))
        tables.append(rows)
    tables.append([jnp.zeros((1, LANES), jnp.float32)] * 3)
    chunks = []
    for c in range(3):
        chunks.append(
            [
                jnp.where(low, tables[2 * c][f], pltpu.roll(tables[2 * c + 1][f], HALF, 1))
                for f in range(3)
            ]
        )
    keys = []
    for c in range(3):
        table = jnp.where(low, float(2 * c), float(2 * c + 1))
        element, node, _ = chunks[c]
        keys.append(jnp.where(node > 0.0, table * 256.0 + element - 1.0, -1.0))
    return chunks, keys


def response_kernel(
    where_ref,
    coef_ref,
    wave_ref,
    mass_ref,
    source_ref,
    weight_ref,
    count_ref,
    m0_ref,
    m1_ref,
    m2_ref,
    m3_ref,
    g0_ref,
    g1_ref,
    g2_ref,
    g3_ref,
    every_ref,
    out_ref,
    pair_ref,
    note_ref,
    flat_ref,
    scale_ref,
    inverse_ref,
    force_ref,
    damp_ref,
    state_ref,
    z_ref,
    hc_ref,
    hz_ref,
    y_ref,
    grad_ref,
    face_ref,
    code_ref,
    seen_ref,
):
    down = lax.broadcasted_iota(jnp.int32, (LANES, LANES), 0)
    right = lax.broadcasted_iota(jnp.int32, (LANES, LANES), 1)
    right_f = right.astype(jnp.float32)
    lane = lane_row()
    lane_low = lane < HALF
    lane_f = lane.astype(jnp.float32)

    stacked = jnp.concatenate(
        [r[...] for r in (m0_ref, m1_ref, m2_ref, m3_ref, g0_ref, g1_ref, g2_ref, g3_ref)], axis=0
    )
    pair = [stacked[:, k * LANES : (k + 1) * LANES].T for k in range(4)]
    for k in range(4):
        pair_ref[k] = pair[k]
    pair_element = pair[0][125:126]
    pair_side = pair[0][126:127]
    own_column = jnp.broadcast_to(stacked[:HALF, 125:126], (HALF, LANES))
    own_column = jnp.concatenate([own_column, own_column], axis=0)

    chunks, keys = point_tables(where_ref, every_ref)
    element, node, _ = chunks[0]
    element_both = jnp.where(lane_low, element, pltpu.roll(element, HALF, 1))
    node_low = jnp.where(lane_low, node, 0.0)
    present = element_both > 0.0
    same_half = (down < HALF) == (right < HALF)
    of_record = (own_column == element_both) & present & same_half
    facts_matrix = one_hot(of_record)
    partner_matrix = one_hot(of_record & (down >= HALF))
    table_row = jnp.where(lane_low, 0.0, (1 + (lane - HALF) // 16).astype(jnp.float32))
    facts = plain_dot(
        jnp.concatenate([pair_side, pair_element, table_row, jnp.zeros((5, LANES))], axis=0),
        facts_matrix,
    )
    side_row = facts[0:1].astype(jnp.int32) - 1
    partner = pltpu.roll(facts, HALF, 1)
    ghost_key = jnp.where(partner[1:2] > 0.0, partner[2:3] * 256.0 + partner[1:2] - 1.0, -5.0)
    own_key = jnp.where(element > 0.0, element - 1.0, -5.0)
    own_key = jnp.where(lane_low, own_key, -5.0)
    ghost_key = jnp.where(lane_low, ghost_key, -5.0)

    match = [(across(keys[c]) == own_key) | (across(keys[c]) == ghost_key) for c in range(3)]
    matched = [jnp.where(m, 1.0, 0.0) for m in match]
    lower = one_hot(right < down)
    before = jnp.zeros((1, LANES), jnp.float32)
    lists = [jnp.zeros((8, LANES), jnp.float32)] * SLOTS
    for c in range(3):
        place = jnp.dot(lower, matched[c].astype(jnp.bfloat16), preferred_element_type=jnp.float32)
        place = jnp.where(match[c], place + before, -1.0)
        before = before + jnp.sum(matched[c], axis=0, keepdims=True)
        _, node_c, gid_c = chunks[c]
        gid_high = jnp.floor(gid_c * (1.0 / 256.0))
        table_c = jnp.where(lane_low, float(2 * c), float(2 * c + 1))
        described = jnp.concatenate(
            [node_c, gid_high, gid_c - 256.0 * gid_high, table_c, jnp.zeros((4, LANES))], axis=0
        )
        for q in range(SLOTS):
            lists[q] = lists[q] + plain_dot(described, one_hot(place == float(q)))
    too_long = jnp.max(before) > float(SLOTS)
    wanted_rows = []
    gids = []
    for q in range(SLOTS):
        node_q = lists[q][0:1] - 1.0
        there = lists[q][3:4] > 0.0
        gids.append(lists[q][1:2] * 256.0 + lists[q][2:3])
        wanted_rows.append(
            jnp.where(
                lane_low,
                jnp.where(there, -1.0, node_q),
                pltpu.roll(jnp.where(there, node_q, -1.0), HALF, 1),
            )
        )
    own_node = jnp.where(lane_low, node - 1.0, -1.0)
    wanted_rows.append(own_node)
    wanted_rows.append(jnp.full((1, LANES), -1.0))
    wanted = jnp.concatenate(wanted_rows, axis=0).astype(jnp.int32)

    take = [
        one_hot((down.astype(jnp.float32) + float(g * LANES + 1) == element_both) & (right < HALF))
        for g in range(2)
    ]
    take = jnp.concatenate(take, axis=0)
    own_fields = [
        weight_ref[...] * wave_ref[:, 0, :],
        DT_SQUARED * mass_ref[:, 0, :],
        source_ref[:, 0, :],
        count_ref[...][:NODES],
    ]
    flat_ref[...] = jnp.zeros(flat_ref.shape, jnp.float32)
    for k, out in enumerate((scale_ref, inverse_ref, force_ref, damp_ref)):
        flat_ref[0:NODES] = (
            exact_pick(own_fields[k], take) + exact_pick(pair[k], partner_matrix)[:NODES]
        )
        load_tiles(flat_ref, out, PENALTY if k == 3 else None)

    home = []
    for g in range(2):
        hit = one_hot(own_column[:HALF] == right_f[:HALF] + float(g * LANES + 1))
        home.append(
            jnp.dot(
                jnp.broadcast_to(lane_f[:, :HALF] + 1.0, (8, HALF)).astype(jnp.bfloat16),
                hit,
                preferred_element_type=jnp.float32,
            )[0:1]
            - 1.0
        )
    pair_key = jnp.where(pair_element > 0.0, table_row * 256.0 + pair_element - 1.0, -3.0)
    notes = (
        [chunks[c][2] for c in range(3)]
        + [chunks[c][1] - 1.0 for c in range(3)]
        + keys
        + [pair_key, lane_f, lane_f + float(LANES)]
        + [pair_side - 1.0]
        + home
        + [jnp.zeros((1, LANES), jnp.float32)]
    )
    note_ref[...] = jnp.concatenate(notes, axis=0)

    row = lax.broadcasted_iota(jnp.int32, (8, LANES), 0)
    side = jnp.broadcast_to(side_row, (8, LANES))
    own_here = jnp.broadcast_to(own_node.astype(jnp.int32), (8, LANES))
    zero = jnp.zeros((8, LANES), jnp.float32)
    for q in range(SLOTS + 1):
        node_q = jnp.broadcast_to(wanted[q : q + 1], (8, LANES))
        code_ref[q] = jnp.where((node_q >= 0) & (node_q // 25 == row), node_q % 25, -1)
    for bc in range(25):
        set_tile(z_ref, jnp.where(own_here == 25 * row + bc, jnp.where(row < 5, 1.0, 0.0), 0.0), bc)
        set_tile(hc_ref, zero, bc)
        set_tile(hz_ref, zero, bc)
        set_tile(state_ref, zero, bc, 0, 2)
        set_tile(y_ref, zero, bc, 0, 2)
    for bc in range(25, 40):
        set_tile(z_ref, zero, bc)
        set_tile(y_ref, zero, bc, 0, 2)
        set_tile(y_ref, zero, bc, 1, 2)

    is_box = jnp.where(where_ref[0] == 0, 1.0, 0.0)

    def step(moment, _):
        drive = coef_ref[0, moment]
        keep = jnp.where(moment > 0, 1.0, 0.0)
        stiff = jnp.where(moment > 0, -1.0, is_box)
        begin = jnp.where(moment > 0, 0.0, 1.0 - is_box)
        extra = partner_faces(y_ref, face_ref, side, 0, 2)
        code = code_ref[SLOTS]
        seen = zero
        for bc in range(25):
            assembled = tile_of(y_ref, bc, 0, 2) + extra[bc]
            inverse = tile_of(inverse_ref, bc)
            x = tile_of(state_ref, bc, 0, 2)
            h = tile_of(hc_ref, bc)
            dx = tile_of(damp_ref, bc) * x
            advanced = 2.0 * x - h + inverse * (drive * tile_of(force_ref, bc) - assembled - dx)
            set_tile(state_ref, advanced, bc, 0, 2)
            set_tile(hc_ref, x - inverse * dx, bc)
            noted = is_box * assembled + (1.0 - is_box) * (x - h)
            seen = seen + jnp.where(code == bc, noted, 0.0)
        seen_ref[moment, SLOTS : SLOTS + 1] = jnp.sum(seen, axis=0, keepdims=True)
        extra = partner_faces(z_ref, face_ref, side)
        for bc in range(25):
            set_tile(state_ref, tile_of(z_ref, bc) + extra[bc], bc, 1, 2)
        stiffness_tiles(state_ref, scale_ref, y_ref, grad_ref, 2, True)
        codes = [code_ref[q] for q in range(SLOTS)]
        seen = [zero] * SLOTS
        for bc in range(25):
            inverse = tile_of(inverse_ref, bc)
            x = tile_of(z_ref, bc)
            h = tile_of(hz_ref, bc)
            dx = tile_of(damp_ref, bc) * x
            adjoint = (2.0 * keep) * x - h + inverse * (
                stiff * tile_of(y_ref, bc, 1, 2) - keep * dx + begin * x
            )
            set_tile(z_ref, adjoint, bc)
            set_tile(hz_ref, keep * (x - inverse * dx) + begin * (inverse * x), bc)
            for q in range(SLOTS):
                seen[q] = seen[q] + jnp.where(codes[q] == bc, adjoint, 0.0)
        for q in range(SLOTS):
            seen_ref[moment, q : q + 1] = jnp.sum(seen[q], axis=0, keepdims=True)
        return 0

    lax.fori_loop(0, STEPS, step, 0)
    for n in range(STEPS):
        rows = seen_ref[n]
        seen_ref[n] = rows + pltpu.roll(rows, HALF, 1)
    for k in range(FREE_ROWS):
        out_ref[0, k : k + 1] = jnp.where(
            lane_low,
            seen_ref[2 * k][SLOTS : SLOTS + 1],
            seen_ref[2 * k + 1][SLOTS : SLOTS + 1],
        )
    for q in range(SLOTS):
        for k in range(PAIRS):
            r = GAIN_ROW + q * PAIRS + k
            out_ref[0, r : r + 1] = jnp.where(
                lane_low, seen_ref[2 * k][q : q + 1], seen_ref[2 * k + 1][q : q + 1]
            )
    for q in range(0, SLOTS, 2):
        r = INDEX_ROW + q // 2
        out_ref[0, r : r + 1] = jnp.where(lane_low, gids[q], pltpu.roll(gids[q + 1], HALF, 1))
    out_ref[0, FLAG_ROW : FLAG_ROW + 1] = jnp.full((1, LANES), jnp.where(too_long, 1.0, 0.0))
    for k in range(1, out_ref.shape[0]):
        out_ref[k] = out_ref[0]


def gather_packed(packed, at):
    rows = at // LANES
    lanes = at % LANES
    out = jnp.zeros(at.shape, jnp.float32)
    for k in range(8):
        source = jnp.broadcast_to(packed[k : k + 1], at.shape)
        picked = jnp.take_along_axis(source, lanes, axis=1, mode="promise_in_bounds")
        out = jnp.where(rows == k, picked, out)
    return out


def final_kernel(
    where_ref,
    time_ref,
    mine_ref,
    other_ref,
    wave_ref,
    mass_ref,
    source_ref,
    weight_ref,
    count_ref,
    pair_ref,
    note_ref,
    now_ref,
    before_ref,
    both_ref,
    spread_ref,
    input_ref,
    scale_ref,
    inverse_ref,
    force_ref,
    damp_ref,
    x_ref,
    old_ref,
    h_ref,
    y_ref,
    grad_ref,
    face_ref,
    kick_ref,
):
    is_box = where_ref[0] == 0
    parity = where_ref[1] % 2
    both_ref[parity] = mine_ref[...]
    both_ref[1 - parity] = other_ref[...]
    low = lax.broadcasted_iota(jnp.int32, (8, LANES), 1) < HALF

    def rows(section, core, r):
        return both_ref[core, section * 8 : section * 8 + 8, r, :]

    index = {}
    for s in range(2):
        for p in range(2):
            for k in range(SLOTS // 2):
                pair = rows(s, p, INDEX_ROW + k).astype(jnp.int32)
                turned = pltpu.roll(pair, HALF, 1)
                index[s, p, 2 * k] = jnp.where(low, pair, turned)
                index[s, p, 2 * k + 1] = jnp.where(low, turned, pair)
    note = note_ref[...]
    at = jnp.where(lax.broadcasted_iota(jnp.int32, (8, LANES), 0) < 3, note[0:8], 0.0).astype(jnp.int32)
    packed = {}
    pairs = {}
    last = {}
    zero = jnp.zeros((8, LANES), jnp.float32)
    for n in range(1, STEPS):
        value = {}
        for s in range(2):
            for p in range(2):
                free = rows(s, p, n // 2)
                total = jnp.where(low, free, 0.0) if n % 2 == 0 else jnp.where(low, 0.0, free)
                for q in range(SLOTS):
                    for k in range(PAIRS):
                        m = n - 2 * k - 1
                        if m >= 1:
                            total = total + rows(s, p, GAIN_ROW + q * PAIRS + k) * pairs[s, p, q, m]
                value[s, p] = total + pltpu.roll(total, HALF, 1)
        for s in range(2):
            packed[s] = jnp.where(low, value[s, 0], value[s, 1])
        packed[1] = PENALTY * packed[1]
        input_ref[n] = gather_packed(jnp.where(is_box, packed[1], packed[0]), at)
        if n < STEPS - 1:
            for s in range(2):
                for p in range(2):
                    for q in range(SLOTS):
                        got = gather_packed(packed[1 - s], index[s, p, q])
                        pairs[s, p, q, n] = jnp.where(low, got, last.get((s, p, q), zero))
                        last[s, p, q] = got
    input_ref[0] = zero
    for c in range(3):
        point_key = across(note[6 + c : 7 + c])
        for g in range(3):
            matrix = one_hot(point_key == note[9 + g : 10 + g])
            spread_ref[c * LANES : (c + 1) * LANES, g * LANES : (g + 1) * LANES] = matrix
            spread_ref[(c + 3) * LANES : (c + 4) * LANES, g * LANES : (g + 1) * LANES] = matrix
    side = jnp.broadcast_to(note[12:13].astype(jnp.int32), (8, LANES))
    own_fields = [
        weight_ref[...] * wave_ref[:, 0, :],
        DT_SQUARED * mass_ref[:, 0, :],
        source_ref[:, 0, :],
        count_ref[...][:NODES],
    ]
    kick_ref[...] = jnp.zeros(kick_ref.shape, jnp.float32)
    for k, out in enumerate((scale_ref, inverse_ref, force_ref, damp_ref)):
        kick_ref[0:NODES] = pair_ref[k][:NODES]
        kick_ref[200 : 200 + NODES] = own_fields[k][:, :LANES]
        kick_ref[400 : 400 + NODES] = own_fields[k][:, LANES:]
        for g in range(3):
            load_tiles(kick_ref, out, PENALTY if k == 3 else None, g, 3, 200 * g)
    for g in range(3):
        for bc in range(40):
            set_tile(y_ref, zero, bc, g, 3)
        for bc in range(25):
            set_tile(x_ref, zero, bc, g, 3)
            set_tile(h_ref, zero, bc, g, 3)
    point_node = note[3:6].astype(jnp.int32)
    node_row = lax.broadcasted_iota(jnp.int32, (LANES, LANES), 0)

    def step(moment, _):
        drive = time_ref[0, moment]
        inputs = input_ref[moment]
        chosen = [
            jnp.where(node_row == point_node[c : c + 1], inputs[c : c + 1], 0.0) for c in range(3)
        ]
        high = [part.astype(jnp.bfloat16) for part in chosen]
        rest = [
            (part - top.astype(jnp.float32)).astype(jnp.bfloat16) for part, top in zip(chosen, high)
        ]
        kick = jnp.dot(
            jnp.concatenate(high + rest, axis=1), spread_ref[...], preferred_element_type=jnp.float32
        )
        for g in range(3):
            kick_ref[200 * g : 200 * g + LANES] = kick[:, g * LANES : (g + 1) * LANES]
        extra = partner_faces(y_ref, face_ref, side, 0, 3)
        for g in range(3):
            for bc in range(25):
                assembled = tile_of(y_ref, bc, g, 3)
                if g == 0:
                    assembled = assembled + extra[bc]
                inverse = tile_of(inverse_ref, bc, g, 3)
                x = tile_of(x_ref, bc, g, 3)
                h = tile_of(h_ref, bc, g, 3)
                arrived = kick_ref[pl.ds(200 * g + bc, 8, stride=25), :]
                dx = tile_of(damp_ref, bc, g, 3) * x
                advanced = 2.0 * x - h + inverse * (
                    drive * tile_of(force_ref, bc, g, 3) - assembled - dx + arrived
                )
                set_tile(h_ref, x - inverse * dx, bc, g, 3)
                set_tile(old_ref, x, bc, g, 3)
                set_tile(x_ref, advanced, bc, g, 3)
        stiffness_tiles(x_ref, scale_ref, y_ref, grad_ref, 3, False)
        return 0

    lax.fori_loop(0, STEPS, step, 0)
    home = jnp.concatenate([note[13:14], note[14:15]], axis=1).astype(jnp.int32)
    linked = jnp.where(
        home == lax.broadcasted_iota(jnp.int32, (LANES, 2 * LANES), 0), 1.0, 0.0
    ).astype(jnp.bfloat16)
    alone = home < 0

    for tiles_ref, out_ref in ((old_ref, before_ref), (x_ref, now_ref)):
        for g in range(3):
            for bc in range(25):
                kick_ref[pl.ds(200 * g + bc, 8, stride=25), :] = tile_of(tiles_ref, bc, g, 3)
        moved = exact_pick(kick_ref[0:LANES], linked)
        for g in range(2):
            own = kick_ref[200 * (g + 1) : 200 * (g + 1) + LANES]
            cut = slice(g * LANES, (g + 1) * LANES)
            out_ref[:, 0, cut] = jnp.where(alone[:, cut], own, moved[:, cut])[:NODES]


def fast_body(wave_speed, inverse_mass, source_field, source_time, face_links, coupling_links):
    _, weight_np, _ = node_tables()
    weight = jnp.asarray(weight_np).reshape(NODES, 1)
    wave, mass, source = [
        jnp.transpose(field, (1, 0, 2)) for field in (wave_speed, inverse_mass, source_field)
    ]
    faces = jnp.transpose(face_links, (1, 0, 2))
    blocks = lax.axis_size("blk")
    columns = wave_speed.shape[-1]
    me = lax.axis_index("blk")
    place = jnp.stack([lax.axis_index("sec"), me]).astype(jnp.int32)
    vmem = pl.BlockSpec(memory_space=pltpu.VMEM)
    smem = pl.BlockSpec(memory_space=pltpu.SMEM)

    def shape(*dims):
        return jax.ShapeDtypeStruct(dims, jnp.float32)

    links, m0, m1, m2, m3, count = pl.pallas_call(
        pack_kernel,
        out_shape=[shape(blocks, 8, LANES)] + [shape(16, 4 * LANES)] * 4 + [shape(LANES, columns)],
        in_specs=[smem] + [vmem] * 6,
        out_specs=[vmem] * 6,
    )(place, wave, mass, source, weight, faces, coupling_links)
    every = lax.all_to_all(links, "blk", 0, 0, tiled=True)
    mine = [m0, m1, m2, m3]
    ghost = [partner_2(part, "blk", j) for j, part in enumerate(mine)]

    def tiles(count):
        return pltpu.VMEM((8 * count, LANES), jnp.float32)

    payload, pair, note = pl.pallas_call(
        response_kernel,
        out_shape=[shape(blocks, PAYLOAD, LANES), shape(4, LANES, LANES), shape(16, LANES)],
        in_specs=[smem] * 2 + [vmem] * 14,
        out_specs=[vmem] * 3,
        scratch_shapes=[tiles(25)] * 5
        + [tiles(50), tiles(40), tiles(25), tiles(25), tiles(80), tiles(50), tiles(5)]
        + [pltpu.VMEM((8, 8, LANES), jnp.int32), pltpu.VMEM((STEPS, 8, LANES), jnp.float32)],
    )(
        place,
        source_time,
        wave,
        mass,
        source,
        weight,
        count,
        *mine,
        *ghost,
        every,
    )

    same_core = [[c + 2 * i for i in range(blocks)] for c in range(2)]
    received = lax.all_to_all(
        payload, ("sec", "blk"), 0, 0, axis_index_groups=same_core, tiled=True
    )
    sibling = partner_2(received, "blk", 0)
    overflow = jnp.max(
        jnp.maximum(received[:, FLAG_ROW, 0], sibling[:, FLAG_ROW, 0])
    ) > 0

    def quick(_):
        return tuple(
            pl.pallas_call(
                final_kernel,
                out_shape=[shape(NODES, 1, columns)] * 2,
                in_specs=[smem] * 2 + [vmem] * 9,
                out_specs=[vmem] * 2,
                scratch_shapes=[
                    pltpu.VMEM((2, blocks, PAYLOAD, LANES), jnp.float32),
                    pltpu.VMEM((6 * LANES, 3 * LANES), jnp.bfloat16),
                    pltpu.VMEM((STEPS, 8, LANES), jnp.float32),
                ]
                + [tiles(75)] * 7
                + [tiles(120), tiles(75), tiles(5), tiles(75)],
            )(
                place,
                source_time,
                received,
                sibling,
                wave,
                mass,
                source,
                weight,
                count,
                pair,
                note,
            )
        )

    def slow(_):
        results = general_body(
            wave_speed, inverse_mass, source_field, source_time, face_links, coupling_links
        )
        return tuple(jnp.transpose(field, (1, 0, 2)) for field in results)

    now, before = lax.cond(overflow, slow, quick, 0)
    return (jnp.transpose(now, (1, 0, 2)), jnp.transpose(before, (1, 0, 2)))


def body(*arguments):
    wave_speed, _, _, _, face_links, coupling_links = arguments
    fits = (
        lax.axis_size("blk") == 16
        and lax.axis_size("sec") == 2
        and wave_speed.shape[1:] == (NODES, 2 * LANES)
        and face_links.shape[-1] == LANES
        and coupling_links.shape[-1] >= CAPC * 16
    )
    return fast_body(*arguments) if fits else general_body(*arguments)


def solution(mesh):
    in_specs = (
        P("sec", None, "blk"),
        P("sec", None, "blk"),
        P("sec", None, "blk"),
        P("sec", None),
        P("sec", None, "blk"),
        P(None, "blk"),
    )
    out_specs = (P("sec", None, "blk"), P("sec", None, "blk"))
    return jax.shard_map(body, mesh=mesh, in_specs=in_specs, out_specs=out_specs, check_vma=False)
```

```python
import jax
import jax.numpy as jnp
import numpy as np
from jax import lax
from jax.experimental import pallas as pl
from jax.experimental.pallas import tpu as pltpu
from jax.sharding import PartitionSpec as P

CAPC = 4
STEPS = 12


DT_SQUARED = 0.05
PENALTY = 10.0


def partner_2(value, axis, stride):
    return lax.ppermute(value, axis, [(i, i ^ 1 << stride) for i in range(lax.axis_size(axis))])


def node_tables():
    abscissae = np.array([-1.0, -np.sqrt(3.0 / 7.0), 0.0, np.sqrt(3.0 / 7.0), 1.0])
    weights = np.array([0.1, 49.0 / 90.0, 32.0 / 45.0, 49.0 / 90.0, 0.1])
    legendre = (35.0 * abscissae**4 - 30.0 * abscissae**2 + 3.0) / 8.0
    derivative = np.zeros((5, 5))
    for i in range(5):
        for j in range(5):
            if i != j:
                derivative[i, j] = legendre[i] / (legendre[j] * (abscissae[i] - abscissae[j]))
    derivative[0, 0] = -2.5
    derivative[4, 4] = 2.5
    identity = np.eye(5)
    operator = np.concatenate(
        [
            np.kron(np.kron(derivative, identity), identity),
            np.kron(np.kron(identity, derivative), identity),
            np.kron(np.kron(identity, identity), derivative),
        ],
        axis=0,
    )
    weight_cube = weights[:, None, None] * weights[None, :, None] * weights[None, None, :]
    lattice = np.arange(125).reshape(5, 5, 5)
    face_nodes = np.stack(
        [
            lattice[0].ravel(),
            lattice[4].ravel(),
            lattice[:, 0].ravel(),
            lattice[:, 4].ravel(),
            lattice[:, :, 0].ravel(),
            lattice[:, :, 4].ravel(),
        ]
    )
    return (
        operator.astype(np.float32),
        weight_cube.reshape(125, 1).astype(np.float32),
        face_nodes.astype(np.int32),
    )


def stiffness(field_in, speed_sq, operator, weight_cube):
    columns = field_in.shape[-1]
    scaling = weight_cube * speed_sq
    grads = jnp.dot(
        operator, field_in, precision=lax.Precision.HIGHEST, preferred_element_type=jnp.float32
    )
    scaled = (grads.reshape(3, 125, columns) * scaling[None]).reshape(375, columns)
    return jnp.dot(
        operator.T, scaled, precision=lax.Precision.HIGHEST, preferred_element_type=jnp.float32
    )


def general_body(wave_speed, inverse_mass, source_field, source_time, face_links, coupling_links):
    operator_np, weight_np, faces_np = node_tables()
    operator = jnp.asarray(operator_np)
    weight_cube = jnp.asarray(weight_np)
    picker_np = np.zeros((150, 125), np.float32)
    for side_number in range(6):
        for node_number in range(25):
            picker_np[side_number * 25 + node_number, faces_np[side_number, node_number]] = 1.0
    picker = jnp.asarray(picker_np)
    spreader = jnp.asarray(picker_np.T.copy())
    speed_sq = wave_speed[0]
    inverse = inverse_mass[0]
    forcing = source_field[0]
    timing = source_time[0]
    element = face_links[0, 0]
    face_side = face_links[0, 1]
    face_peer = face_links[0, 2]
    blocks = lax.axis_size("blk")
    bit_count = blocks.bit_length() - 1
    myself = lax.axis_index("blk")
    is_box = lax.axis_index("sec") == 0
    records = element.shape[0]
    per_peer = records // 8
    ordinal = jnp.arange(records)
    linked = face_peer != myself
    side_mask = face_side[None, None, :] == jnp.arange(6, dtype=jnp.int32)[:, None, None]
    earlier = ordinal[None, :] < ordinal[:, None]
    face_slot = jnp.sum(
        ((face_peer[:, None] == face_peer[None, :]) & earlier).astype(jnp.int32), axis=1
    )
    offset_bits = jnp.bitwise_xor(face_peer, myself)
    bit_index = jnp.zeros((records,), jnp.int32)
    for bit_number in range(bit_count):
        bit_index = bit_index + bit_number * (offset_bits == 1 << bit_number).astype(jnp.int32)
    pair_column = jnp.where(linked, bit_index * per_peer + face_slot, 0)
    point_element = coupling_links[0]
    point_node = coupling_links[1]
    point_owner = coupling_links[2]
    target_element = coupling_links[3]
    target_node = coupling_links[4]
    in_use = point_owner >= 0
    owner_safe = jnp.maximum(point_owner, 0)
    point_ordinal = jnp.arange(point_owner.shape[0])
    point_earlier = point_ordinal[None, :] < point_ordinal[:, None]
    point_slot = jnp.sum(
        ((point_owner[:, None] == point_owner[None, :]) & point_earlier).astype(jnp.int32), axis=1
    )
    point_column = jnp.where(in_use, point_slot * blocks + owner_safe, 0)
    slot_total = CAPC * blocks
    outbound = jnp.zeros((3, slot_total), jnp.int32)
    outbound = outbound.at[0, point_column].add(jnp.where(in_use, target_element, 0))
    outbound = outbound.at[1, point_column].add(jnp.where(in_use, target_node, 0))
    outbound = outbound.at[2, point_column].add(in_use.astype(jnp.int32))
    inbound = lax.all_to_all(
        outbound.reshape(3, CAPC, blocks), "blk", split_axis=2, concat_axis=2, tiled=True
    ).reshape(3, slot_total)
    remote_element = inbound[0]
    remote_node = inbound[1]
    remote_flag = inbound[2].astype(jnp.float32)
    target_rows = jnp.concatenate([point_node, remote_node])
    target_cols = jnp.concatenate([point_element, remote_element])
    current = jnp.zeros(speed_sq.shape, jnp.float32)
    previous = jnp.zeros(speed_sq.shape, jnp.float32)
    def one_step(moment, state):
        current, previous = state
        internal = stiffness(current, speed_sq, operator, weight_cube)
        stacked = jnp.dot(
            picker,
            internal[:, element],
            precision=lax.Precision.HIGHEST,
            preferred_element_type=jnp.float32,
        ).reshape(6, 25, records)
        payload = jnp.sum(jnp.where(side_mask, stacked, 0.0), axis=0)
        payload = jnp.where(linked[None, :], payload, 0.0)
        outgoing = (
            jnp.zeros((25, bit_count * per_peer), jnp.float32).at[:, pair_column].add(payload)
        )
        arrived = []
        for bit_number in range(bit_count):
            piece = outgoing[:, bit_number * per_peer : (bit_number + 1) * per_peer]
            arrived.append(partner_2(piece, "blk", bit_number))
        partner = jnp.concatenate(arrived, axis=1)[:, pair_column]
        partner = jnp.where(linked[None, :], partner, 0.0)
        masked = jnp.where(side_mask, partner[None], 0.0).reshape(150, records)
        assembled = internal.at[:, element].add(
            jnp.dot(
                spreader,
                masked,
                precision=lax.Precision.HIGHEST,
                preferred_element_type=jnp.float32,
            )
        )
        velocity = current - previous
        traction = assembled[point_node, point_element]
        box_send = (
            jnp.zeros((slot_total,), jnp.float32)
            .at[point_column]
            .add(jnp.where(in_use, traction, 0.0))
        )
        global_send = velocity[remote_node, remote_element] * remote_flag
        dispatch = jnp.where(is_box, box_send, global_send).reshape(CAPC, blocks)
        crossed = partner_2(dispatch, "sec", 0)
        received = lax.all_to_all(crossed, "blk", split_axis=1, concat_axis=1, tiled=True)
        received = received.reshape(slot_total)
        remote_velocity = received[point_column]
        box_terms = jnp.where(
            in_use, PENALTY * (remote_velocity - velocity[point_node, point_element]), 0.0
        )
        values = jnp.concatenate(
            [jnp.where(is_box, box_terms, 0.0), jnp.where(is_box, 0.0, received * remote_flag)]
        )
        driving = timing[moment] * forcing - assembled
        driving = driving.at[target_rows, target_cols].add(values)
        advanced = 2.0 * current - previous + DT_SQUARED * inverse * driving
        return advanced, current

    current, previous = lax.fori_loop(0, STEPS, one_step, (current, previous))
    return (current[None], previous[None])


LANES = 128
HALF = 64
OTHERS = 5
LAGS = 10
PAIRS = LAGS // 2
FREE_ROWS = STEPS // 2
GAIN_ROW = FREE_ROWS
EXTRA_ROW = GAIN_ROW + PAIRS
INDEX_ROW = EXTRA_ROW + PAIRS
PAYLOAD = INDEX_ROW + 1
NODES = 125
EXACT = lax.Precision.HIGHEST


def line_matrix():
    abscissae = np.array([-1.0, -np.sqrt(3.0 / 7.0), 0.0, np.sqrt(3.0 / 7.0), 1.0])
    legendre = (35.0 * abscissae**4 - 30.0 * abscissae**2 + 3.0) / 8.0
    derivative = np.zeros((5, 5))
    for i in range(5):
        for j in range(5):
            if i != j:
                derivative[i, j] = legendre[i] / (legendre[j] * (abscissae[i] - abscissae[j]))
    derivative[0, 0] = -2.5
    derivative[4, 4] = 2.5
    return derivative


def apply_line(matrix, x):
    odd = [x[0] - x[4], x[1] - x[3]]
    even = [x[0] + x[4], x[1] + x[3]]
    out = [None] * 5
    for i in range(2):
        symmetric = (
            float(0.5 * (matrix[i, 0] - matrix[i, 4])) * odd[0]
            + float(0.5 * (matrix[i, 1] - matrix[i, 3])) * odd[1]
        )
        skew = (
            float(0.5 * (matrix[i, 0] + matrix[i, 4])) * even[0]
            + float(0.5 * (matrix[i, 1] + matrix[i, 3])) * even[1]
            + float(matrix[i, 2]) * x[2]
        )
        out[i] = symmetric + skew
        out[4 - i] = symmetric - skew
    out[2] = float(matrix[2, 0]) * odd[0] + float(matrix[2, 1]) * odd[1]
    return out


def line_tiles():
    row = lax.broadcasted_iota(jnp.int32, (8, LANES), 0)
    tiles = []
    for matrix in (line_matrix(), line_matrix().T):
        columns = []
        for j in range(5):
            tile = jnp.zeros((8, LANES), jnp.float32)
            for i in range(5):
                tile = jnp.where(row == i, float(matrix[i, j]), tile)
            columns.append(tile)
        tiles.append(columns)
    return tiles


def tile_of(ref, bc, group=0, groups=1):
    start = (bc * groups + group) * 8
    return ref[start : start + 8, :]


def set_tile(ref, value, bc, group=0, groups=1):
    start = (bc * groups + group) * 8
    ref[start : start + 8, :] = value


def repeat_row(ref, row):
    return jnp.broadcast_to(ref[row : row + 1, :], (8, LANES))


def stiffness_tiles(x_ref, scale_ref, y_ref, grad_ref, groups, shared):
    forward = line_matrix()
    backward = forward.T.copy()
    to_grad, to_node = line_tiles()

    for g in range(groups):

        def scale(bc):
            return tile_of(scale_ref, bc) if shared else tile_of(scale_ref, bc, g, groups)

        def along(index):
            grads = apply_line(forward, [tile_of(x_ref, k, g, groups) for k in index])
            return apply_line(backward, [v * scale(k) for v, k in zip(grads, index)])

        for bc in range(25):
            start = (bc * groups + g) * 8
            total = to_grad[0] * repeat_row(x_ref, start)
            for j in range(1, 5):
                total = total + to_grad[j] * repeat_row(x_ref, start + j)
            grad_ref[start : start + 8, :] = total * scale(bc)
        total = [None] * 25
        for c in range(5):
            index = [5 * j + c for j in range(5)]
            for k, value in zip(index, along(index)):
                total[k] = value
        for b in range(5):
            index = [5 * b + j for j in range(5)]
            for k, value in zip(index, along(index)):
                total[k] = total[k] + value
        for bc in range(25):
            start = (bc * groups + g) * 8
            value = total[bc]
            for j in range(5):
                value = value + to_node[j] * repeat_row(grad_ref, start + j)
            set_tile(y_ref, value, bc, g, groups)


def partner_faces(ref, face_ref, side, group=0, groups=1):
    row = lax.broadcasted_iota(jnp.int32, (8, LANES), 0)
    is_side = [side == q for q in range(6)]
    on_a = (is_side[0] & (row == 0)) | (is_side[1] & (row == 4))
    arrived = []
    for t in range(5):
        first = ref[pl.ds((t * groups + group) * 8, 8, stride=40 * groups), :]
        last = ref[pl.ds((t * groups + group) * 8 + 4, 8, stride=40 * groups), :]
        value = jnp.where(is_side[1], last, first)
        value = jnp.where(is_side[2], tile_of(ref, t, group, groups), value)
        value = jnp.where(is_side[3], tile_of(ref, 20 + t, group, groups), value)
        value = jnp.where(is_side[4], tile_of(ref, 5 * t, group, groups), value)
        value = jnp.where(is_side[5], tile_of(ref, 5 * t + 4, group, groups), value)
        value = pltpu.roll(value, HALF, 1)
        arrived.append(value)
        set_tile(face_ref, value, t)
    extra = []
    for b in range(5):
        for c in range(5):
            value = jnp.where(on_a, repeat_row(face_ref, 8 * c + b), 0.0)
            if b == 0:
                value = jnp.where(is_side[2], arrived[c], value)
            if b == 4:
                value = jnp.where(is_side[3], arrived[c], value)
            if c == 0:
                value = jnp.where(is_side[4], arrived[b], value)
            if c == 4:
                value = jnp.where(is_side[5], arrived[b], value)
            extra.append(value)
    return extra


def load_tiles(flat_ref, out_ref, factor=None, group=0, groups=1, start=0):
    for bc in range(25):
        value = flat_ref[pl.ds(start + bc, 8, stride=25), :]
        set_tile(out_ref, value if factor is None else factor * value, bc, group, groups)


def across(row_values):
    return jnp.broadcast_to(row_values, (LANES, LANES)).T


def rank_among(row_values):
    down = lax.broadcasted_iota(jnp.int32, (LANES, LANES), 0)
    right = lax.broadcasted_iota(jnp.int32, (LANES, LANES), 1)
    same = (across(row_values) == row_values) & (down < right)
    return jnp.sum(jnp.where(same, 1.0, 0.0), axis=0, keepdims=True)


def one_hot(condition):
    return jnp.where(condition, 1.0, 0.0).astype(jnp.bfloat16)


def plain_dot(a, b):
    return jnp.dot(a.astype(jnp.bfloat16), b, preferred_element_type=jnp.float32)


def exact_pick(values, chosen, transposed=False):
    total = None
    rest = values
    for _ in range(3):
        part = rest.astype(jnp.bfloat16)
        if transposed:
            got = lax.dot_general(
                chosen, part, (((1,), (1,)), ((), ())), preferred_element_type=jnp.float32
            )
        else:
            got = jnp.dot(part, chosen, preferred_element_type=jnp.float32)
        total = got if total is None else total + got
        rest = rest - part.astype(jnp.float32)
    return total


def lane_row():
    return lax.broadcasted_iota(jnp.int32, (1, LANES), 1)


def pack_kernel(
    where_ref,
    wave_ref,
    mass_ref,
    source_ref,
    weight_ref,
    face_ref,
    couple_ref,
    links_ref,
    m0_ref,
    m1_ref,
    m2_ref,
    m3_ref,
    count_ref,
):
    me = where_ref[1]
    me_f = me.astype(jnp.float32)
    is_box = where_ref[0] == 0
    down = lax.broadcasted_iota(jnp.int32, (LANES, LANES), 0)
    right = lax.broadcasted_iota(jnp.int32, (LANES, LANES), 1)
    right_f = right.astype(jnp.float32)
    lane = lane_row()

    live = couple_ref[:, 0:LANES].astype(jnp.float32)
    owner = jnp.where(lane < HALF, live[2:3], -1.0)
    slot = jnp.where(owner >= 0.0, owner * CAPC + rank_among(owner), -1.0)
    to_slot = one_hot(across(slot) == right_f)
    named = jnp.concatenate([live[0:2], live[3:5], jnp.full((4, LANES), -1.0)], axis=0) + 1.0
    links = plain_dot(named, to_slot)
    for k in range(links_ref.shape[0]):
        links_ref[k] = links

    faces = face_ref[:, 0, :]
    peer = faces[2:3]
    linked = peer != me
    distance = peer ^ me
    bit = jnp.zeros((1, LANES), jnp.float32)
    for j in range(1, 4):
        bit = bit + jnp.where(distance == 1 << j, float(j), 0.0)
    face_slot = jnp.where(linked, bit * 16.0 + rank_among(peer.astype(jnp.float32)), -1.0)
    to_record = one_hot(across(face_slot) == right_f)
    facts = jnp.concatenate([faces[0:2].astype(jnp.float32) + 1.0, jnp.zeros((6, LANES))], axis=0)
    record = plain_dot(facts, to_record)

    node_one = lax.broadcasted_iota(jnp.int32, (LANES, LANES), 0).astype(jnp.float32) + 1.0
    own_nodes = one_hot(node_one == links[1:2])
    point_column = across(links[0:1])
    record_column = across(record[0:1])
    side_column = across(record[1:2])
    counts = []
    taken = []
    for g in range(2):
        column_one = right_f + float(g * LANES + 1)
        counts.append(
            jnp.dot(own_nodes, one_hot(point_column == column_one), preferred_element_type=jnp.float32)
        )
        taken.append(one_hot(record_column == column_one)[:HALF])
    count = jnp.concatenate(counts, axis=1) * jnp.where(is_box, 1.0, 0.0)
    count_ref[...] = count
    take = jnp.concatenate(taken, axis=1)
    pad = jnp.zeros((LANES - NODES, 2 * LANES), jnp.float32)
    stiff = jnp.concatenate([weight_ref[...] * wave_ref[:, 0, :], pad], axis=0)
    mass = jnp.concatenate([DT_SQUARED * mass_ref[:, 0, :], pad], axis=0)
    source = jnp.concatenate([source_ref[:, 0, :], pad], axis=0)
    first = exact_pick(stiff, take, True)
    first = jnp.where(right[:HALF] == 125, record_column[:HALF], first)
    first = jnp.where(right[:HALF] == 126, side_column[:HALF], first)
    parts = [
        first,
        exact_pick(mass, take, True),
        exact_pick(source, take, True),
        lax.dot_general(
            take,
            count.astype(jnp.bfloat16),
            (((1,), (1,)), ((), ())),
            preferred_element_type=jnp.float32,
        ),
    ]
    for j, out in enumerate((m0_ref, m1_ref, m2_ref, m3_ref)):
        for k in range(4):
            out[:, k * LANES : (k + 1) * LANES] = parts[k][16 * j : 16 * j + 16]


def point_tables(where_ref, every_ref):
    me = where_ref[1]
    is_box = where_ref[0] == 0
    lane = lane_row()
    low = lane < HALF
    blocks = every_ref.shape[0]
    down = lax.broadcasted_iota(jnp.int32, (blocks, LANES), 0)
    right = lax.broadcasted_iota(jnp.int32, (blocks, LANES), 1)
    mine = right // CAPC == down
    tables = []
    for offset in (0, 1, 2, 4, 8):
        beta = me ^ offset
        at = beta * CAPC + right % CAPC
        rows = []
        for f in range(2):
            direct = every_ref[beta, f : f + 1, :]
            column = every_ref[:, 2 + f, :]
            picked = jnp.concatenate(
                [
                    jnp.take_along_axis(column[8 * h : 8 * h + 8], at[8 * h : 8 * h + 8], axis=1,
                                        mode="promise_in_bounds")
                    for h in range(blocks // 8)
                ],
                axis=0,
            )
            turned = jnp.sum(jnp.where(mine, picked, 0.0), axis=0, keepdims=True)
            row = jnp.where(is_box, direct, turned)
            rows.append(jnp.where(low, row, 0.0))
        inputs = lane // CAPC * HALF + beta * CAPC + lane % CAPC
        rows.append(jnp.where(low, inputs, 0).astype(jnp.float32))
        tables.append(rows)
    tables.append([jnp.zeros((1, LANES), jnp.float32)] * 3)
    chunks = []
    for c in range(3):
        chunks.append(
            [
                jnp.where(low, tables[2 * c][f], pltpu.roll(tables[2 * c + 1][f], HALF, 1))
                for f in range(3)
            ]
        )
    keys = []
    for c in range(3):
        table = jnp.where(low, float(2 * c), float(2 * c + 1))
        element, node, _ = chunks[c]
        keys.append(jnp.where(node > 0.0, table * 256.0 + element - 1.0, -1.0))
    return chunks, keys


def gather_packed(packed, at):
    rows = at // LANES
    lanes = at % LANES
    out = jnp.zeros(at.shape, jnp.float32)
    for k in range(8):
        source = jnp.broadcast_to(packed[k : k + 1], at.shape)
        picked = jnp.take_along_axis(source, lanes, axis=1, mode="promise_in_bounds")
        out = jnp.where(rows == k, picked, out)
    return out


def response_kernel(
    where_ref,
    coef_ref,
    wave_ref,
    mass_ref,
    source_ref,
    weight_ref,
    count_ref,
    m0_ref,
    m1_ref,
    m2_ref,
    m3_ref,
    g0_ref,
    g1_ref,
    g2_ref,
    g3_ref,
    every_ref,
    out_ref,
    pair_ref,
    note_ref,
    flat_ref,
    scale_ref,
    inverse_ref,
    force_ref,
    damp_ref,
    state_ref,
    z_ref,
    hc_ref,
    hz_ref,
    y_ref,
    grad_ref,
    face_ref,
    code_ref,
    seen_ref,
):
    down = lax.broadcasted_iota(jnp.int32, (LANES, LANES), 0)
    right = lax.broadcasted_iota(jnp.int32, (LANES, LANES), 1)
    right_f = right.astype(jnp.float32)
    lane = lane_row()
    lane_low = lane < HALF
    lane_f = lane.astype(jnp.float32)

    stacked = jnp.concatenate(
        [r[...] for r in (m0_ref, m1_ref, m2_ref, m3_ref, g0_ref, g1_ref, g2_ref, g3_ref)], axis=0
    )
    pair = [stacked[:, k * LANES : (k + 1) * LANES].T for k in range(4)]
    for k in range(4):
        pair_ref[k] = pair[k]
    pair_element = pair[0][125:126]
    pair_side = pair[0][126:127]
    own_column = jnp.broadcast_to(stacked[:HALF, 125:126], (HALF, LANES))
    own_column = jnp.concatenate([own_column, own_column], axis=0)

    chunks, keys = point_tables(where_ref, every_ref)
    element, node, _ = chunks[0]
    element_both = jnp.where(lane_low, element, pltpu.roll(element, HALF, 1))
    node_low = jnp.where(lane_low, node, 0.0)
    present = element_both > 0.0
    same_half = (down < HALF) == (right < HALF)
    of_record = (own_column == element_both) & present & same_half
    facts_matrix = one_hot(of_record)
    partner_matrix = one_hot(of_record & (down >= HALF))
    table_row = jnp.where(lane_low, 0.0, (1 + (lane - HALF) // 16).astype(jnp.float32))
    facts = plain_dot(
        jnp.concatenate([pair_side, pair_element, table_row, jnp.zeros((5, LANES))], axis=0),
        facts_matrix,
    )
    side_row = facts[0:1].astype(jnp.int32) - 1
    partner = pltpu.roll(facts, HALF, 1)
    ghost_key = jnp.where(partner[1:2] > 0.0, partner[2:3] * 256.0 + partner[1:2] - 1.0, -5.0)
    own_key = jnp.where(element > 0.0, element - 1.0, -5.0)
    own_key = jnp.where(lane_low, own_key, -5.0)
    ghost_key = jnp.where(lane_low, ghost_key, -5.0)

    match = [(across(keys[c]) == own_key) | (across(keys[c]) == ghost_key) for c in range(3)]
    match[0] = match[0] & (down != right)
    matched = [jnp.where(m, 1.0, 0.0) for m in match]
    lower = one_hot(right < down)
    before = jnp.zeros((1, LANES), jnp.float32)
    lists = [jnp.zeros((8, LANES), jnp.float32)] * OTHERS
    for c in range(3):
        place = jnp.dot(lower, matched[c].astype(jnp.bfloat16), preferred_element_type=jnp.float32)
        place = jnp.where(match[c], place + before, -1.0)
        before = before + jnp.sum(matched[c], axis=0, keepdims=True)
        _, node_c, gid_c = chunks[c]
        gid_high = jnp.floor(gid_c * (1.0 / 256.0))
        table_c = jnp.where(lane_low, float(2 * c), float(2 * c + 1))
        described = jnp.concatenate(
            [node_c, gid_high, gid_c - 256.0 * gid_high, table_c, jnp.zeros((4, LANES))], axis=0
        )
        for q in range(OTHERS):
            lists[q] = lists[q] + plain_dot(described, one_hot(place == float(q)))
    own_node = jnp.where(lane_low, node - 1.0, -1.0)
    wanted = [own_node]
    gids = [jnp.zeros((1, LANES), jnp.float32)]
    for q in range(OTHERS):
        node_q = lists[q][0:1] - 1.0
        there = lists[q][3:4] > 0.0
        gids.append(lists[q][1:2] * 256.0 + lists[q][2:3])
        wanted.append(
            jnp.where(
                lane_low,
                jnp.where(there, -1.0, node_q),
                pltpu.roll(jnp.where(there, node_q, -1.0), HALF, 1),
            )
        )
    gids.append(jnp.zeros((7 - OTHERS, LANES), jnp.float32))

    length = jnp.minimum(before, 200.0)
    start = plain_dot(jnp.broadcast_to(length, (8, LANES)), one_hot(down < right))[0:1]
    too_long = (jnp.max(before) > float(OTHERS)) | (jnp.max(start + length) > float(HALF))
    entry = right % HALF
    entry_f = entry.astype(jnp.float32)
    is_point = down < HALF
    owner_of = jnp.sum(
        jnp.where(is_point & (across(start + length) <= entry_f), 1.0, 0.0), axis=0, keepdims=True
    )
    begun = jnp.sum(
        jnp.where(down.astype(jnp.float32) == owner_of, across(start), 0.0), axis=0, keepdims=True
    )
    used = owner_of < float(HALF)
    which = jnp.clip(entry_f[0:1] - begun, 0.0, float(OTHERS - 1)) + 1.0
    entry_at = jnp.where(used, which * float(LANES) + owner_of, 0.0).astype(jnp.int32)
    entry_at = jnp.broadcast_to(entry_at, (8, LANES))
    entry_gid = jnp.where(used, gather_packed(jnp.concatenate(gids, axis=0), entry_at)[0:1], 0.0)

    take = [
        one_hot((down.astype(jnp.float32) + float(g * LANES + 1) == element_both) & (right < HALF))
        for g in range(2)
    ]
    take = jnp.concatenate(take, axis=0)
    own_fields = [
        weight_ref[...] * wave_ref[:, 0, :],
        DT_SQUARED * mass_ref[:, 0, :],
        source_ref[:, 0, :],
        count_ref[...][:NODES],
    ]
    flat_ref[...] = jnp.zeros(flat_ref.shape, jnp.float32)
    for k, out in enumerate((scale_ref, inverse_ref, force_ref, damp_ref)):
        flat_ref[0:NODES] = (
            exact_pick(own_fields[k], take) + exact_pick(pair[k], partner_matrix)[:NODES]
        )
        load_tiles(flat_ref, out, PENALTY if k == 3 else None)

    home = []
    for g in range(2):
        hit = one_hot(own_column[:HALF] == right_f[:HALF] + float(g * LANES + 1))
        home.append(
            jnp.dot(
                jnp.broadcast_to(lane_f[:, :HALF] + 1.0, (8, HALF)).astype(jnp.bfloat16),
                hit,
                preferred_element_type=jnp.float32,
            )[0:1]
            - 1.0
        )
    pair_key = jnp.where(pair_element > 0.0, table_row * 256.0 + pair_element - 1.0, -3.0)
    notes = (
        [chunks[c][2] for c in range(3)]
        + [chunks[c][1] - 1.0 for c in range(3)]
        + keys
        + [pair_key, lane_f, lane_f + float(LANES)]
        + [pair_side - 1.0]
        + home
        + [jnp.zeros((1, LANES), jnp.float32)]
    )
    note_ref[...] = jnp.concatenate(notes, axis=0)

    row = lax.broadcasted_iota(jnp.int32, (8, LANES), 0)
    side = jnp.broadcast_to(side_row, (8, LANES))
    own_here = jnp.broadcast_to(own_node.astype(jnp.int32), (8, LANES))
    zero = jnp.zeros((8, LANES), jnp.float32)
    for q in range(OTHERS + 1):
        node_q = jnp.broadcast_to(wanted[q], (8, LANES)).astype(jnp.int32)
        code_ref[q] = jnp.where((node_q >= 0) & (node_q // 25 == row), node_q % 25, -1)
    for bc in range(25):
        set_tile(z_ref, jnp.where(own_here == 25 * row + bc, jnp.where(row < 5, 1.0, 0.0), 0.0), bc)
        set_tile(hc_ref, zero, bc)
        set_tile(hz_ref, zero, bc)
        set_tile(state_ref, zero, bc, 0, 2)
        set_tile(y_ref, zero, bc, 0, 2)
    for n in range(STEPS):
        seen_ref[n] = zero
    for bc in range(25, 40):
        set_tile(z_ref, zero, bc)
        set_tile(y_ref, zero, bc, 0, 2)
        set_tile(y_ref, zero, bc, 1, 2)

    is_box = jnp.where(where_ref[0] == 0, 1.0, 0.0)

    def note_free(moment, drive):
        extra = partner_faces(y_ref, face_ref, side, 0, 2)
        code = code_ref[0]
        seen = zero
        for bc in range(25):
            assembled = tile_of(y_ref, bc, 0, 2) + extra[bc]
            x = tile_of(state_ref, bc, 0, 2)
            h = tile_of(hc_ref, bc)
            seen = seen + jnp.where(code == bc, is_box * assembled + (1.0 - is_box) * (x - h), 0.0)
            if drive is not None:
                inverse = tile_of(inverse_ref, bc)
                dx = tile_of(damp_ref, bc) * x
                advanced = 2.0 * x - h + inverse * (drive * tile_of(force_ref, bc) - assembled - dx)
                set_tile(state_ref, advanced, bc, 0, 2)
                set_tile(hc_ref, x - inverse * dx, bc)
        seen_ref[moment, 7:8] = jnp.sum(seen, axis=0, keepdims=True)

    def step(moment, _):
        keep = jnp.where(moment > 0, 1.0, 0.0)
        stiff = jnp.where(moment > 0, -1.0, is_box)
        begin = jnp.where(moment > 0, 0.0, 1.0 - is_box)
        note_free(moment, coef_ref[0, moment])
        extra = partner_faces(z_ref, face_ref, side)
        for bc in range(25):
            set_tile(state_ref, tile_of(z_ref, bc) + extra[bc], bc, 1, 2)
        stiffness_tiles(state_ref, scale_ref, y_ref, grad_ref, 2, True)
        codes = [code_ref[q] for q in range(OTHERS + 1)]
        seen = [zero] * (OTHERS + 1)
        for bc in range(25):
            inverse = tile_of(inverse_ref, bc)
            x = tile_of(z_ref, bc)
            h = tile_of(hz_ref, bc)
            dx = tile_of(damp_ref, bc) * x
            adjoint = (2.0 * keep) * x - h + inverse * (
                stiff * tile_of(y_ref, bc, 1, 2) - keep * dx + begin * x
            )
            set_tile(z_ref, adjoint, bc)
            set_tile(hz_ref, keep * (x - inverse * dx) + begin * (inverse * x), bc)
            for q in range(OTHERS + 1):
                seen[q] = seen[q] + jnp.where(codes[q] == bc, adjoint, 0.0)
        for q in range(OTHERS + 1):
            seen_ref[moment, q : q + 1] = jnp.sum(seen[q], axis=0, keepdims=True)
        return 0

    lax.fori_loop(0, STEPS - 1, step, 0)
    note_free(STEPS - 1, None)
    seen = []
    extras = []
    for n in range(STEPS):
        rows = seen_ref[n]
        rows = rows + pltpu.roll(rows, HALF, 1)
        seen.append(rows)
        extras.append(jnp.where(used, gather_packed(rows, entry_at)[0:1], 0.0))
    for k in range(FREE_ROWS):
        out_ref[0, k : k + 1] = jnp.where(lane_low, seen[2 * k][7:8], seen[2 * k + 1][7:8])
    for k in range(PAIRS):
        r = GAIN_ROW + k
        out_ref[0, r : r + 1] = jnp.where(lane_low, seen[2 * k][0:1], seen[2 * k + 1][0:1])
        r = EXTRA_ROW + k
        out_ref[0, r : r + 1] = jnp.where(lane_low, extras[2 * k], extras[2 * k + 1])
    starts = jnp.where(lane == HALF, jnp.where(too_long, 1.0, 0.0), pltpu.roll(start, HALF, 1))
    out_ref[0, INDEX_ROW : INDEX_ROW + 1] = jnp.where(lane_low, entry_gid, starts)
    for k in range(1, out_ref.shape[0]):
        out_ref[k] = out_ref[0]


def final_kernel(
    where_ref,
    time_ref,
    mine_ref,
    other_ref,
    wave_ref,
    mass_ref,
    source_ref,
    weight_ref,
    count_ref,
    pair_ref,
    note_ref,
    now_ref,
    before_ref,
    both_ref,
    spread_ref,
    input_ref,
    scale_ref,
    inverse_ref,
    force_ref,
    damp_ref,
    x_ref,
    old_ref,
    h_ref,
    y_ref,
    grad_ref,
    face_ref,
    kick_ref,
):
    is_box = where_ref[0] == 0
    parity = where_ref[1] % 2
    both_ref[parity] = mine_ref[...]
    both_ref[1 - parity] = other_ref[...]
    low = lax.broadcasted_iota(jnp.int32, (8, LANES), 1) < HALF

    def rows(section, core, r):
        return both_ref[core, section * 8 : section * 8 + 8, r, :]

    row = lax.broadcasted_iota(jnp.int32, (8, LANES), 0)
    point = lax.broadcasted_iota(jnp.int32, (8, LANES), 1) % HALF
    index = {}
    for s in range(2):
        for p in range(2):
            pair = rows(s, p, INDEX_ROW).astype(jnp.int32)
            turned = pltpu.roll(pair, HALF, 1)
            start = jnp.where(point == 0, 0, jnp.where(low, turned, pair))
            stop = jnp.where(point == HALF - 1, HALF, pltpu.roll(start, LANES - 1, 1))
            own = point // CAPC * HALF + (2 * row + p) * CAPC + point % CAPC
            index[s, p] = (own, jnp.where(low, pair, turned), start, stop)
    note = note_ref[...]
    at = jnp.where(row < 3, note[0:8], 0.0).astype(jnp.int32)
    packed = {}
    pairs = {}
    last = {}
    zero = jnp.zeros((8, LANES), jnp.float32)
    for n in range(1, STEPS):
        value = {}
        for s in range(2):
            for p in range(2):
                free = rows(s, p, n // 2)
                total = jnp.where(low, free, 0.0) if n % 2 == 0 else jnp.where(low, 0.0, free)
                more = zero
                for k in range(PAIRS):
                    m = n - 2 * k - 1
                    if m >= 1:
                        total = total + rows(s, p, GAIN_ROW + k) * pairs[s, p, 0, m]
                        more = more + rows(s, p, EXTRA_ROW + k) * pairs[s, p, 1, m]
                total = total + pltpu.roll(total, HALF, 1)
                if n > 1:
                    more = more + pltpu.roll(more, HALF, 1)
                    _, _, start, stop = index[s, p]
                    for q in range(OTHERS):
                        got = jnp.take_along_axis(
                            more, jnp.minimum(start + q, HALF - 1), axis=1, mode="promise_in_bounds"
                        )
                        total = total + jnp.where(start + q < stop, got, 0.0)
                value[s, p] = total
        for s in range(2):
            packed[s] = jnp.where(low, value[s, 0], value[s, 1])
        packed[1] = PENALTY * packed[1]
        input_ref[n] = gather_packed(jnp.where(is_box, packed[1], packed[0]), at)
        if n < STEPS - 1:
            for s in range(2):
                for p in range(2):
                    for q in range(2):
                        got = gather_packed(packed[1 - s], index[s, p][q])
                        pairs[s, p, q, n] = jnp.where(low, got, last.get((s, p, q), zero))
                        last[s, p, q] = got
    for c in range(3):
        point_key = across(note[6 + c : 7 + c])
        for g in range(3):
            matrix = one_hot(point_key == note[9 + g : 10 + g])
            spread_ref[c * LANES : (c + 1) * LANES, g * LANES : (g + 1) * LANES] = matrix
            spread_ref[(c + 3) * LANES : (c + 4) * LANES, g * LANES : (g + 1) * LANES] = matrix
    side = jnp.broadcast_to(note[12:13].astype(jnp.int32), (8, LANES))
    own_fields = [
        weight_ref[...] * wave_ref[:, 0, :],
        DT_SQUARED * mass_ref[:, 0, :],
        source_ref[:, 0, :],
        count_ref[...][:NODES],
    ]
    kick_ref[...] = jnp.zeros(kick_ref.shape, jnp.float32)
    for k, out in enumerate((scale_ref, inverse_ref, force_ref, damp_ref)):
        kick_ref[0:NODES] = pair_ref[k][:NODES]
        kick_ref[200 : 200 + NODES] = own_fields[k][:, :LANES]
        kick_ref[400 : 400 + NODES] = own_fields[k][:, LANES:]
        for g in range(3):
            load_tiles(kick_ref, out, PENALTY if k == 3 else None, g, 3, 200 * g)
    for g in range(3):
        for bc in range(25, 40):
            set_tile(y_ref, zero, bc, g, 3)
        for bc in range(25):
            first = time_ref[0, 0] * tile_of(force_ref, bc, g, 3)
            set_tile(x_ref, tile_of(inverse_ref, bc, g, 3) * first, bc, g, 3)
            set_tile(h_ref, zero, bc, g, 3)
    point_node = note[3:6].astype(jnp.int32)
    node_row = lax.broadcasted_iota(jnp.int32, (LANES, LANES), 0)

    def step(moment, _):
        drive = time_ref[0, moment]
        stiffness_tiles(x_ref, scale_ref, y_ref, grad_ref, 3, False)
        inputs = input_ref[moment]
        chosen = [
            jnp.where(node_row == point_node[c : c + 1], inputs[c : c + 1], 0.0) for c in range(3)
        ]
        high = [part.astype(jnp.bfloat16) for part in chosen]
        rest = [
            (part - top.astype(jnp.float32)).astype(jnp.bfloat16) for part, top in zip(chosen, high)
        ]
        kick = jnp.dot(
            jnp.concatenate(high + rest, axis=1), spread_ref[...], preferred_element_type=jnp.float32
        )
        for g in range(3):
            kick_ref[200 * g : 200 * g + LANES] = kick[:, g * LANES : (g + 1) * LANES]
        extra = partner_faces(y_ref, face_ref, side, 0, 3)
        for g in range(3):
            for bc in range(25):
                assembled = tile_of(y_ref, bc, g, 3)
                if g == 0:
                    assembled = assembled + extra[bc]
                inverse = tile_of(inverse_ref, bc, g, 3)
                x = tile_of(x_ref, bc, g, 3)
                h = tile_of(h_ref, bc, g, 3)
                arrived = kick_ref[pl.ds(200 * g + bc, 8, stride=25), :]
                dx = tile_of(damp_ref, bc, g, 3) * x
                advanced = 2.0 * x - h + inverse * (
                    drive * tile_of(force_ref, bc, g, 3) - assembled - dx + arrived
                )
                set_tile(h_ref, x - inverse * dx, bc, g, 3)
                set_tile(old_ref, x, bc, g, 3)
                set_tile(x_ref, advanced, bc, g, 3)
        return 0

    lax.fori_loop(1, STEPS, step, 0)
    home = jnp.concatenate([note[13:14], note[14:15]], axis=1).astype(jnp.int32)
    linked = jnp.where(
        home == lax.broadcasted_iota(jnp.int32, (LANES, 2 * LANES), 0), 1.0, 0.0
    ).astype(jnp.bfloat16)
    alone = home < 0

    for tiles_ref, out_ref in ((old_ref, before_ref), (x_ref, now_ref)):
        for g in range(3):
            for bc in range(25):
                kick_ref[pl.ds(200 * g + bc, 8, stride=25), :] = tile_of(tiles_ref, bc, g, 3)
        moved = exact_pick(kick_ref[0:LANES], linked)
        for g in range(2):
            own = kick_ref[200 * (g + 1) : 200 * (g + 1) + LANES]
            cut = slice(g * LANES, (g + 1) * LANES)
            out_ref[:, 0, cut] = jnp.where(alone[:, cut], own, moved[:, cut])[:NODES]


def fast_body(wave_speed, inverse_mass, source_field, source_time, face_links, coupling_links):
    _, weight_np, _ = node_tables()
    weight = jnp.asarray(weight_np).reshape(NODES, 1)
    wave, mass, source = [
        jnp.transpose(field, (1, 0, 2)) for field in (wave_speed, inverse_mass, source_field)
    ]
    faces = jnp.transpose(face_links, (1, 0, 2))
    blocks = lax.axis_size("blk")
    columns = wave_speed.shape[-1]
    me = lax.axis_index("blk")
    place = jnp.stack([lax.axis_index("sec"), me]).astype(jnp.int32)
    vmem = pl.BlockSpec(memory_space=pltpu.VMEM)
    smem = pl.BlockSpec(memory_space=pltpu.SMEM)
    params = pltpu.CompilerParams(vmem_limit_bytes=16 << 20)

    def shape(*dims):
        return jax.ShapeDtypeStruct(dims, jnp.float32)

    links, m0, m1, m2, m3, count = pl.pallas_call(
        pack_kernel,
        out_shape=[shape(blocks, 8, LANES)] + [shape(16, 4 * LANES)] * 4 + [shape(LANES, columns)],
        in_specs=[smem] + [vmem] * 6,
        out_specs=[vmem] * 6,
        compiler_params=params,
    )(place, wave, mass, source, weight, faces, coupling_links)
    mine = [m0, m1, m2, m3]
    ghost = [partner_2(part, "blk", j) for j, part in enumerate(mine)]
    every = lax.all_to_all(links, "blk", 0, 0, tiled=True)

    def tiles(count):
        return pltpu.VMEM((8 * count, LANES), jnp.float32)

    payload, pair, note = pl.pallas_call(
        response_kernel,
        out_shape=[shape(blocks, PAYLOAD, LANES), shape(4, LANES, LANES), shape(16, LANES)],
        in_specs=[smem] * 2 + [vmem] * 14,
        out_specs=[vmem] * 3,
        compiler_params=params,
        scratch_shapes=[tiles(25)] * 5
        + [tiles(50), tiles(40), tiles(25), tiles(25), tiles(80), tiles(50), tiles(5)]
        + [pltpu.VMEM((8, 8, LANES), jnp.int32), pltpu.VMEM((STEPS, 8, LANES), jnp.float32)],
    )(
        place,
        source_time,
        wave,
        mass,
        source,
        weight,
        count,
        *mine,
        *ghost,
        every,
    )

    same_core = [[c + 2 * i for i in range(blocks)] for c in range(2)]
    received = lax.all_to_all(
        payload, ("sec", "blk"), 0, 0, axis_index_groups=same_core, tiled=True
    )
    sibling = partner_2(received, "blk", 0)
    overflow = jnp.max(
        jnp.maximum(received[:, INDEX_ROW, HALF], sibling[:, INDEX_ROW, HALF])
    ) > 0

    def quick(_):
        return tuple(
            pl.pallas_call(
                final_kernel,
                out_shape=[shape(NODES, 1, columns)] * 2,
                in_specs=[smem] * 2 + [vmem] * 9,
                out_specs=[vmem] * 2,
                compiler_params=params,
                scratch_shapes=[
                    pltpu.VMEM((2, blocks, PAYLOAD, LANES), jnp.float32),
                    pltpu.VMEM((6 * LANES, 3 * LANES), jnp.bfloat16),
                    pltpu.VMEM((STEPS, 8, LANES), jnp.float32),
                ]
                + [tiles(75)] * 7
                + [tiles(120), tiles(75), tiles(5), tiles(75)],
            )(
                place,
                source_time,
                received,
                sibling,
                wave,
                mass,
                source,
                weight,
                count,
                pair,
                note,
            )
        )

    def slow(_):
        results = general_body(
            wave_speed, inverse_mass, source_field, source_time, face_links, coupling_links
        )
        return tuple(jnp.transpose(field, (1, 0, 2)) for field in results)

    now, before = lax.cond(overflow, slow, quick, 0)
    return (jnp.transpose(now, (1, 0, 2)), jnp.transpose(before, (1, 0, 2)))


def body(*arguments):
    wave_speed, _, _, _, face_links, coupling_links = arguments
    fits = (
        lax.axis_size("blk") == 16
        and lax.axis_size("sec") == 2
        and wave_speed.shape[1:] == (NODES, 2 * LANES)
        and face_links.shape[-1] == LANES
        and coupling_links.shape[-1] >= CAPC * 16
    )
    return fast_body(*arguments) if fits else general_body(*arguments)


def solution(mesh):
    in_specs = (
        P("sec", None, "blk"),
        P("sec", None, "blk"),
        P("sec", None, "blk"),
        P("sec", None),
        P("sec", None, "blk"),
        P(None, "blk"),
    )
    out_specs = (P("sec", None, "blk"), P("sec", None, "blk"))
    return jax.shard_map(body, mesh=mesh, in_specs=in_specs, out_specs=out_specs, check_vma=False)
```

```python
import jax
import jax.numpy as jnp
import numpy as np
from jax import lax
from jax.experimental import pallas as pl
from jax.experimental.pallas import tpu as pltpu
from jax.sharding import PartitionSpec as P

CAPC = 4
STEPS = 12


DT_SQUARED = 0.05
PENALTY = 10.0


def partner_2(value, axis, stride):
    return lax.ppermute(value, axis, [(i, i ^ 1 << stride) for i in range(lax.axis_size(axis))])


def node_tables():
    abscissae = np.array([-1.0, -np.sqrt(3.0 / 7.0), 0.0, np.sqrt(3.0 / 7.0), 1.0])
    weights = np.array([0.1, 49.0 / 90.0, 32.0 / 45.0, 49.0 / 90.0, 0.1])
    legendre = (35.0 * abscissae**4 - 30.0 * abscissae**2 + 3.0) / 8.0
    derivative = np.zeros((5, 5))
    for i in range(5):
        for j in range(5):
            if i != j:
                derivative[i, j] = legendre[i] / (legendre[j] * (abscissae[i] - abscissae[j]))
    derivative[0, 0] = -2.5
    derivative[4, 4] = 2.5
    identity = np.eye(5)
    operator = np.concatenate(
        [
            np.kron(np.kron(derivative, identity), identity),
            np.kron(np.kron(identity, derivative), identity),
            np.kron(np.kron(identity, identity), derivative),
        ],
        axis=0,
    )
    weight_cube = weights[:, None, None] * weights[None, :, None] * weights[None, None, :]
    lattice = np.arange(125).reshape(5, 5, 5)
    face_nodes = np.stack(
        [
            lattice[0].ravel(),
            lattice[4].ravel(),
            lattice[:, 0].ravel(),
            lattice[:, 4].ravel(),
            lattice[:, :, 0].ravel(),
            lattice[:, :, 4].ravel(),
        ]
    )
    return (
        operator.astype(np.float32),
        weight_cube.reshape(125, 1).astype(np.float32),
        face_nodes.astype(np.int32),
    )


def stiffness(field_in, speed_sq, operator, weight_cube):
    columns = field_in.shape[-1]
    scaling = weight_cube * speed_sq
    grads = jnp.dot(
        operator, field_in, precision=lax.Precision.HIGHEST, preferred_element_type=jnp.float32
    )
    scaled = (grads.reshape(3, 125, columns) * scaling[None]).reshape(375, columns)
    return jnp.dot(
        operator.T, scaled, precision=lax.Precision.HIGHEST, preferred_element_type=jnp.float32
    )


def general_body(wave_speed, inverse_mass, source_field, source_time, face_links, coupling_links):
    operator_np, weight_np, faces_np = node_tables()
    operator = jnp.asarray(operator_np)
    weight_cube = jnp.asarray(weight_np)
    picker_np = np.zeros((150, 125), np.float32)
    for side_number in range(6):
        for node_number in range(25):
            picker_np[side_number * 25 + node_number, faces_np[side_number, node_number]] = 1.0
    picker = jnp.asarray(picker_np)
    spreader = jnp.asarray(picker_np.T.copy())
    speed_sq = wave_speed[0]
    inverse = inverse_mass[0]
    forcing = source_field[0]
    timing = source_time[0]
    element = face_links[0, 0]
    face_side = face_links[0, 1]
    face_peer = face_links[0, 2]
    blocks = lax.axis_size("blk")
    bit_count = blocks.bit_length() - 1
    myself = lax.axis_index("blk")
    is_box = lax.axis_index("sec") == 0
    records = element.shape[0]
    per_peer = records // 8
    ordinal = jnp.arange(records)
    linked = face_peer != myself
    side_mask = face_side[None, None, :] == jnp.arange(6, dtype=jnp.int32)[:, None, None]
    earlier = ordinal[None, :] < ordinal[:, None]
    face_slot = jnp.sum(
        ((face_peer[:, None] == face_peer[None, :]) & earlier).astype(jnp.int32), axis=1
    )
    offset_bits = jnp.bitwise_xor(face_peer, myself)
    bit_index = jnp.zeros((records,), jnp.int32)
    for bit_number in range(bit_count):
        bit_index = bit_index + bit_number * (offset_bits == 1 << bit_number).astype(jnp.int32)
    pair_column = jnp.where(linked, bit_index * per_peer + face_slot, 0)
    point_element = coupling_links[0]
    point_node = coupling_links[1]
    point_owner = coupling_links[2]
    target_element = coupling_links[3]
    target_node = coupling_links[4]
    in_use = point_owner >= 0
    owner_safe = jnp.maximum(point_owner, 0)
    point_ordinal = jnp.arange(point_owner.shape[0])
    point_earlier = point_ordinal[None, :] < point_ordinal[:, None]
    point_slot = jnp.sum(
        ((point_owner[:, None] == point_owner[None, :]) & point_earlier).astype(jnp.int32), axis=1
    )
    point_column = jnp.where(in_use, point_slot * blocks + owner_safe, 0)
    slot_total = CAPC * blocks
    outbound = jnp.zeros((3, slot_total), jnp.int32)
    outbound = outbound.at[0, point_column].add(jnp.where(in_use, target_element, 0))
    outbound = outbound.at[1, point_column].add(jnp.where(in_use, target_node, 0))
    outbound = outbound.at[2, point_column].add(in_use.astype(jnp.int32))
    inbound = lax.all_to_all(
        outbound.reshape(3, CAPC, blocks), "blk", split_axis=2, concat_axis=2, tiled=True
    ).reshape(3, slot_total)
    remote_element = inbound[0]
    remote_node = inbound[1]
    remote_flag = inbound[2].astype(jnp.float32)
    target_rows = jnp.concatenate([point_node, remote_node])
    target_cols = jnp.concatenate([point_element, remote_element])
    current = jnp.zeros(speed_sq.shape, jnp.float32)
    previous = jnp.zeros(speed_sq.shape, jnp.float32)
    def one_step(moment, state):
        current, previous = state
        internal = stiffness(current, speed_sq, operator, weight_cube)
        stacked = jnp.dot(
            picker,
            internal[:, element],
            precision=lax.Precision.HIGHEST,
            preferred_element_type=jnp.float32,
        ).reshape(6, 25, records)
        payload = jnp.sum(jnp.where(side_mask, stacked, 0.0), axis=0)
        payload = jnp.where(linked[None, :], payload, 0.0)
        outgoing = (
            jnp.zeros((25, bit_count * per_peer), jnp.float32).at[:, pair_column].add(payload)
        )
        arrived = []
        for bit_number in range(bit_count):
            piece = outgoing[:, bit_number * per_peer : (bit_number + 1) * per_peer]
            arrived.append(partner_2(piece, "blk", bit_number))
        partner = jnp.concatenate(arrived, axis=1)[:, pair_column]
        partner = jnp.where(linked[None, :], partner, 0.0)
        masked = jnp.where(side_mask, partner[None], 0.0).reshape(150, records)
        assembled = internal.at[:, element].add(
            jnp.dot(
                spreader,
                masked,
                precision=lax.Precision.HIGHEST,
                preferred_element_type=jnp.float32,
            )
        )
        velocity = current - previous
        traction = assembled[point_node, point_element]
        box_send = (
            jnp.zeros((slot_total,), jnp.float32)
            .at[point_column]
            .add(jnp.where(in_use, traction, 0.0))
        )
        global_send = velocity[remote_node, remote_element] * remote_flag
        dispatch = jnp.where(is_box, box_send, global_send).reshape(CAPC, blocks)
        crossed = partner_2(dispatch, "sec", 0)
        received = lax.all_to_all(crossed, "blk", split_axis=1, concat_axis=1, tiled=True)
        received = received.reshape(slot_total)
        remote_velocity = received[point_column]
        box_terms = jnp.where(
            in_use, PENALTY * (remote_velocity - velocity[point_node, point_element]), 0.0
        )
        values = jnp.concatenate(
            [jnp.where(is_box, box_terms, 0.0), jnp.where(is_box, 0.0, received * remote_flag)]
        )
        driving = timing[moment] * forcing - assembled
        driving = driving.at[target_rows, target_cols].add(values)
        advanced = 2.0 * current - previous + DT_SQUARED * inverse * driving
        return advanced, current

    current, previous = lax.fori_loop(0, STEPS, one_step, (current, previous))
    return (current[None], previous[None])


LANES = 128
HALF = 64
OTHERS = 5
LAGS = 10
PAIRS = LAGS // 2
FREE_ROWS = STEPS // 2
GAIN_ROW = FREE_ROWS
EXTRA_ROW = GAIN_ROW + PAIRS
INDEX_ROW = EXTRA_ROW + PAIRS
PAYLOAD = INDEX_ROW + 1
NODES = 125
EXACT = lax.Precision.HIGHEST


def line_matrix():
    abscissae = np.array([-1.0, -np.sqrt(3.0 / 7.0), 0.0, np.sqrt(3.0 / 7.0), 1.0])
    legendre = (35.0 * abscissae**4 - 30.0 * abscissae**2 + 3.0) / 8.0
    derivative = np.zeros((5, 5))
    for i in range(5):
        for j in range(5):
            if i != j:
                derivative[i, j] = legendre[i] / (legendre[j] * (abscissae[i] - abscissae[j]))
    derivative[0, 0] = -2.5
    derivative[4, 4] = 2.5
    return derivative


def apply_line(matrix, x):
    odd = [x[0] - x[4], x[1] - x[3]]
    even = [x[0] + x[4], x[1] + x[3]]
    out = [None] * 5
    for i in range(2):
        symmetric = (
            float(0.5 * (matrix[i, 0] - matrix[i, 4])) * odd[0]
            + float(0.5 * (matrix[i, 1] - matrix[i, 3])) * odd[1]
        )
        skew = (
            float(0.5 * (matrix[i, 0] + matrix[i, 4])) * even[0]
            + float(0.5 * (matrix[i, 1] + matrix[i, 3])) * even[1]
            + float(matrix[i, 2]) * x[2]
        )
        out[i] = symmetric + skew
        out[4 - i] = symmetric - skew
    out[2] = float(matrix[2, 0]) * odd[0] + float(matrix[2, 1]) * odd[1]
    return out


def line_tiles():
    row = lax.broadcasted_iota(jnp.int32, (8, LANES), 0)
    tiles = []
    for matrix in (line_matrix(), line_matrix().T):
        columns = []
        for j in range(5):
            tile = jnp.zeros((8, LANES), jnp.float32)
            for i in range(5):
                tile = jnp.where(row == i, float(matrix[i, j]), tile)
            columns.append(tile)
        tiles.append(columns)
    return tiles


def tile_of(ref, bc, group=0, groups=1):
    start = (bc * groups + group) * 8
    return ref[start : start + 8, :]


def set_tile(ref, value, bc, group=0, groups=1):
    start = (bc * groups + group) * 8
    ref[start : start + 8, :] = value


def repeat_row(ref, row):
    return jnp.broadcast_to(ref[row : row + 1, :], (8, LANES))


def stiffness_tiles(x_ref, scale_ref, y_ref, grad_ref, groups, shared):
    forward = line_matrix()
    backward = forward.T.copy()
    to_grad, to_node = line_tiles()

    for g in range(groups):

        def scale(bc):
            return tile_of(scale_ref, bc) if shared else tile_of(scale_ref, bc, g, groups)

        def along(index):
            grads = apply_line(forward, [tile_of(x_ref, k, g, groups) for k in index])
            return apply_line(backward, [v * scale(k) for v, k in zip(grads, index)])

        for bc in range(25):
            start = (bc * groups + g) * 8
            total = to_grad[0] * repeat_row(x_ref, start)
            for j in range(1, 5):
                total = total + to_grad[j] * repeat_row(x_ref, start + j)
            grad_ref[start : start + 8, :] = total * scale(bc)
        total = [None] * 25
        for c in range(5):
            index = [5 * j + c for j in range(5)]
            for k, value in zip(index, along(index)):
                total[k] = value
        for b in range(5):
            index = [5 * b + j for j in range(5)]
            for k, value in zip(index, along(index)):
                total[k] = total[k] + value
        for bc in range(25):
            start = (bc * groups + g) * 8
            value = total[bc]
            for j in range(5):
                value = value + to_node[j] * repeat_row(grad_ref, start + j)
            set_tile(y_ref, value, bc, g, groups)


def partner_faces(ref, face_ref, side, group=0, groups=1):
    row = lax.broadcasted_iota(jnp.int32, (8, LANES), 0)
    is_side = [side == q for q in range(6)]
    on_a = (is_side[0] & (row == 0)) | (is_side[1] & (row == 4))
    arrived = []
    for t in range(5):
        first = ref[pl.ds((t * groups + group) * 8, 8, stride=40 * groups), :]
        last = ref[pl.ds((t * groups + group) * 8 + 4, 8, stride=40 * groups), :]
        value = jnp.where(is_side[1], last, first)
        value = jnp.where(is_side[2], tile_of(ref, t, group, groups), value)
        value = jnp.where(is_side[3], tile_of(ref, 20 + t, group, groups), value)
        value = jnp.where(is_side[4], tile_of(ref, 5 * t, group, groups), value)
        value = jnp.where(is_side[5], tile_of(ref, 5 * t + 4, group, groups), value)
        value = pltpu.roll(value, HALF, 1)
        arrived.append(value)
        set_tile(face_ref, value, t)
    extra = []
    for b in range(5):
        for c in range(5):
            value = jnp.where(on_a, repeat_row(face_ref, 8 * c + b), 0.0)
            if b == 0:
                value = jnp.where(is_side[2], arrived[c], value)
            if b == 4:
                value = jnp.where(is_side[3], arrived[c], value)
            if c == 0:
                value = jnp.where(is_side[4], arrived[b], value)
            if c == 4:
                value = jnp.where(is_side[5], arrived[b], value)
            extra.append(value)
    return extra


def load_tiles(flat_ref, out_ref, group=0, groups=1, start=0):
    for bc in range(25):
        set_tile(out_ref, flat_ref[pl.ds(start + bc, 8, stride=25), :], bc, group, groups)


def fold_tiles(inverse_ref, force_ref, keep_ref, count):
    for k in range(count):
        inverse = tile_of(inverse_ref, k)
        set_tile(force_ref, inverse * tile_of(force_ref, k), k)
        set_tile(keep_ref, 2.0 - inverse * (PENALTY * tile_of(keep_ref, k)), k)


def across(row_values):
    return jnp.broadcast_to(row_values, (LANES, LANES)).T


def rank_among(row_values):
    down = lax.broadcasted_iota(jnp.int32, (LANES, LANES), 0)
    right = lax.broadcasted_iota(jnp.int32, (LANES, LANES), 1)
    same = (across(row_values) == row_values) & (down < right)
    return jnp.sum(jnp.where(same, 1.0, 0.0), axis=0, keepdims=True)


def one_hot(condition):
    return jnp.where(condition, 1.0, 0.0).astype(jnp.bfloat16)


def plain_dot(a, b):
    return jnp.dot(a.astype(jnp.bfloat16), b, preferred_element_type=jnp.float32)


def exact_pick(values, chosen, transposed=False):
    total = None
    rest = values
    for _ in range(3):
        part = rest.astype(jnp.bfloat16)
        if transposed:
            got = lax.dot_general(
                chosen, part, (((1,), (1,)), ((), ())), preferred_element_type=jnp.float32
            )
        else:
            got = jnp.dot(part, chosen, preferred_element_type=jnp.float32)
        total = got if total is None else total + got
        rest = rest - part.astype(jnp.float32)
    return total


def lane_row():
    return lax.broadcasted_iota(jnp.int32, (1, LANES), 1)


def pack_kernel(
    where_ref,
    wave_ref,
    mass_ref,
    source_ref,
    weight_ref,
    face_ref,
    couple_ref,
    links_ref,
    m0_ref,
    m1_ref,
    m2_ref,
    m3_ref,
    count_ref,
):
    me = where_ref[1]
    me_f = me.astype(jnp.float32)
    is_box = where_ref[0] == 0
    down = lax.broadcasted_iota(jnp.int32, (LANES, LANES), 0)
    right = lax.broadcasted_iota(jnp.int32, (LANES, LANES), 1)
    right_f = right.astype(jnp.float32)
    lane = lane_row()

    live = couple_ref[:, 0:LANES].astype(jnp.float32)
    owner = jnp.where(lane < HALF, live[2:3], -1.0)
    slot = jnp.where(owner >= 0.0, owner * CAPC + rank_among(owner), -1.0)
    to_slot = one_hot(across(slot) == right_f)
    named = jnp.concatenate([live[0:2], live[3:5], jnp.full((4, LANES), -1.0)], axis=0) + 1.0
    links = plain_dot(named, to_slot)
    for k in range(links_ref.shape[0]):
        links_ref[k] = links

    faces = face_ref[:, 0, :]
    peer = faces[2:3]
    linked = peer != me
    distance = peer ^ me
    bit = jnp.zeros((1, LANES), jnp.float32)
    for j in range(1, 4):
        bit = bit + jnp.where(distance == 1 << j, float(j), 0.0)
    face_slot = jnp.where(linked, bit * 16.0 + rank_among(peer.astype(jnp.float32)), -1.0)
    to_record = one_hot(across(face_slot) == right_f)
    facts = jnp.concatenate([faces[0:2].astype(jnp.float32) + 1.0, jnp.zeros((6, LANES))], axis=0)
    record = plain_dot(facts, to_record)

    node_one = lax.broadcasted_iota(jnp.int32, (LANES, LANES), 0).astype(jnp.float32) + 1.0
    own_nodes = one_hot(node_one == links[1:2])
    point_column = across(links[0:1])
    record_column = across(record[0:1])
    side_column = across(record[1:2])
    counts = []
    taken = []
    for g in range(2):
        column_one = right_f + float(g * LANES + 1)
        counts.append(
            jnp.dot(own_nodes, one_hot(point_column == column_one), preferred_element_type=jnp.float32)
        )
        taken.append(one_hot(record_column == column_one)[:HALF])
    count = jnp.concatenate(counts, axis=1) * jnp.where(is_box, 1.0, 0.0)
    count_ref[...] = count
    take = jnp.concatenate(taken, axis=1)
    pad = jnp.zeros((LANES - NODES, 2 * LANES), jnp.float32)
    stiff = jnp.concatenate([weight_ref[...] * wave_ref[:, 0, :], pad], axis=0)
    mass = jnp.concatenate([DT_SQUARED * mass_ref[:, 0, :], pad], axis=0)
    source = jnp.concatenate([source_ref[:, 0, :], pad], axis=0)
    first = exact_pick(stiff, take, True)
    first = jnp.where(right[:HALF] == 125, record_column[:HALF], first)
    first = jnp.where(right[:HALF] == 126, side_column[:HALF], first)
    parts = [
        first,
        exact_pick(mass, take, True),
        exact_pick(source, take, True),
        lax.dot_general(
            take,
            count.astype(jnp.bfloat16),
            (((1,), (1,)), ((), ())),
            preferred_element_type=jnp.float32,
        ),
    ]
    for j, out in enumerate((m0_ref, m1_ref, m2_ref, m3_ref)):
        for k in range(4):
            out[:, k * LANES : (k + 1) * LANES] = parts[k][16 * j : 16 * j + 16]


def point_tables(where_ref, every_ref):
    me = where_ref[1]
    is_box = where_ref[0] == 0
    lane = lane_row()
    low = lane < HALF
    blocks = every_ref.shape[0]
    down = lax.broadcasted_iota(jnp.int32, (blocks, LANES), 0)
    right = lax.broadcasted_iota(jnp.int32, (blocks, LANES), 1)
    mine = right // CAPC == down
    tables = []
    for offset in (0, 1, 2, 4, 8):
        beta = me ^ offset
        at = beta * CAPC + right % CAPC
        rows = []
        for f in range(2):
            direct = every_ref[beta, f : f + 1, :]
            column = every_ref[:, 2 + f, :]
            picked = jnp.concatenate(
                [
                    jnp.take_along_axis(column[8 * h : 8 * h + 8], at[8 * h : 8 * h + 8], axis=1,
                                        mode="promise_in_bounds")
                    for h in range(blocks // 8)
                ],
                axis=0,
            )
            turned = jnp.sum(jnp.where(mine, picked, 0.0), axis=0, keepdims=True)
            row = jnp.where(is_box, direct, turned)
            rows.append(jnp.where(low, row, 0.0))
        inputs = lane // CAPC * HALF + beta * CAPC + lane % CAPC
        rows.append(jnp.where(low, inputs, 0).astype(jnp.float32))
        tables.append(rows)
    tables.append([jnp.zeros((1, LANES), jnp.float32)] * 3)
    chunks = []
    for c in range(3):
        chunks.append(
            [
                jnp.where(low, tables[2 * c][f], pltpu.roll(tables[2 * c + 1][f], HALF, 1))
                for f in range(3)
            ]
        )
    keys = []
    for c in range(3):
        table = jnp.where(low, float(2 * c), float(2 * c + 1))
        element, node, _ = chunks[c]
        keys.append(jnp.where(node > 0.0, table * 256.0 + element - 1.0, -1.0))
    return chunks, keys


def gather_packed(packed, at):
    rows = at // LANES
    lanes = at % LANES
    out = jnp.zeros(at.shape, jnp.float32)
    for k in range(8):
        source = jnp.broadcast_to(packed[k : k + 1], at.shape)
        picked = jnp.take_along_axis(source, lanes, axis=1, mode="promise_in_bounds")
        out = jnp.where(rows == k, picked, out)
    return out


def response_kernel(
    where_ref,
    coef_ref,
    wave_ref,
    mass_ref,
    source_ref,
    weight_ref,
    count_ref,
    m0_ref,
    m1_ref,
    m2_ref,
    m3_ref,
    g0_ref,
    g1_ref,
    g2_ref,
    g3_ref,
    every_ref,
    out_ref,
    pair_ref,
    note_ref,
    flat_ref,
    scale_ref,
    inverse_ref,
    force_ref,
    keep_ref,
    state_ref,
    z_ref,
    hc_ref,
    hz_ref,
    y_ref,
    grad_ref,
    face_ref,
    code_ref,
    seen_ref,
):
    down = lax.broadcasted_iota(jnp.int32, (LANES, LANES), 0)
    right = lax.broadcasted_iota(jnp.int32, (LANES, LANES), 1)
    right_f = right.astype(jnp.float32)
    lane = lane_row()
    lane_low = lane < HALF
    lane_f = lane.astype(jnp.float32)

    stacked = jnp.concatenate(
        [r[...] for r in (m0_ref, m1_ref, m2_ref, m3_ref, g0_ref, g1_ref, g2_ref, g3_ref)], axis=0
    )
    pair = [stacked[:, k * LANES : (k + 1) * LANES].T for k in range(4)]
    for k in range(4):
        pair_ref[k] = pair[k]
    pair_element = pair[0][125:126]
    pair_side = pair[0][126:127]
    own_column = jnp.broadcast_to(stacked[:HALF, 125:126], (HALF, LANES))
    own_column = jnp.concatenate([own_column, own_column], axis=0)

    chunks, keys = point_tables(where_ref, every_ref)
    element, node, _ = chunks[0]
    element_both = jnp.where(lane_low, element, pltpu.roll(element, HALF, 1))
    node_low = jnp.where(lane_low, node, 0.0)
    present = element_both > 0.0
    same_half = (down < HALF) == (right < HALF)
    of_record = (own_column == element_both) & present & same_half
    facts_matrix = one_hot(of_record)
    partner_matrix = one_hot(of_record & (down >= HALF))
    table_row = jnp.where(lane_low, 0.0, (1 + (lane - HALF) // 16).astype(jnp.float32))
    facts = plain_dot(
        jnp.concatenate([pair_side, pair_element, table_row, jnp.zeros((5, LANES))], axis=0),
        facts_matrix,
    )
    side_row = facts[0:1].astype(jnp.int32) - 1
    partner = pltpu.roll(facts, HALF, 1)
    ghost_key = jnp.where(partner[1:2] > 0.0, partner[2:3] * 256.0 + partner[1:2] - 1.0, -5.0)
    own_key = jnp.where(element > 0.0, element - 1.0, -5.0)
    own_key = jnp.where(lane_low, own_key, -5.0)
    ghost_key = jnp.where(lane_low, ghost_key, -5.0)

    match = [(across(keys[c]) == own_key) | (across(keys[c]) == ghost_key) for c in range(3)]
    match[0] = match[0] & (down != right)
    matched = [jnp.where(m, 1.0, 0.0) for m in match]
    lower = one_hot(right < down)
    before = jnp.zeros((1, LANES), jnp.float32)
    lists = [jnp.zeros((8, LANES), jnp.float32)] * OTHERS
    for c in range(3):
        place = jnp.dot(lower, matched[c].astype(jnp.bfloat16), preferred_element_type=jnp.float32)
        place = jnp.where(match[c], place + before, -1.0)
        before = before + jnp.sum(matched[c], axis=0, keepdims=True)
        _, node_c, gid_c = chunks[c]
        gid_high = jnp.floor(gid_c * (1.0 / 256.0))
        table_c = jnp.where(lane_low, float(2 * c), float(2 * c + 1))
        described = jnp.concatenate(
            [node_c, gid_high, gid_c - 256.0 * gid_high, table_c, jnp.zeros((4, LANES))], axis=0
        )
        for q in range(OTHERS):
            lists[q] = lists[q] + plain_dot(described, one_hot(place == float(q)))
    own_node = jnp.where(lane_low, node - 1.0, -1.0)
    wanted = [own_node]
    gids = [jnp.zeros((1, LANES), jnp.float32)]
    for q in range(OTHERS):
        node_q = lists[q][0:1] - 1.0
        there = lists[q][3:4] > 0.0
        gids.append(lists[q][1:2] * 256.0 + lists[q][2:3])
        wanted.append(
            jnp.where(
                lane_low,
                jnp.where(there, -1.0, node_q),
                pltpu.roll(jnp.where(there, node_q, -1.0), HALF, 1),
            )
        )
    gids.append(jnp.zeros((7 - OTHERS, LANES), jnp.float32))

    length = jnp.minimum(before, 200.0)
    start = plain_dot(jnp.broadcast_to(length, (8, LANES)), one_hot(down < right))[0:1]
    too_long = (jnp.max(before) > float(OTHERS)) | (jnp.max(start + length) > float(HALF))
    entry = right % HALF
    entry_f = entry.astype(jnp.float32)
    is_point = down < HALF
    owner_of = jnp.sum(
        jnp.where(is_point & (across(start + length) <= entry_f), 1.0, 0.0), axis=0, keepdims=True
    )
    begun = jnp.sum(
        jnp.where(down.astype(jnp.float32) == owner_of, across(start), 0.0), axis=0, keepdims=True
    )
    used = owner_of < float(HALF)
    which = jnp.clip(entry_f[0:1] - begun, 0.0, float(OTHERS - 1)) + 1.0
    entry_at = jnp.where(used, which * float(LANES) + owner_of, 0.0).astype(jnp.int32)
    entry_at = jnp.broadcast_to(entry_at, (8, LANES))
    entry_gid = jnp.where(used, gather_packed(jnp.concatenate(gids, axis=0), entry_at)[0:1], 0.0)

    take = [
        one_hot((down.astype(jnp.float32) + float(g * LANES + 1) == element_both) & (right < HALF))
        for g in range(2)
    ]
    take = jnp.concatenate(take, axis=0)
    own_fields = [
        weight_ref[...] * wave_ref[:, 0, :],
        DT_SQUARED * mass_ref[:, 0, :],
        source_ref[:, 0, :],
        count_ref[...][:NODES],
    ]
    flat_ref[...] = jnp.zeros(flat_ref.shape, jnp.float32)
    for k, out in enumerate((scale_ref, inverse_ref, force_ref, keep_ref)):
        flat_ref[0:NODES] = (
            exact_pick(own_fields[k], take) + exact_pick(pair[k], partner_matrix)[:NODES]
        )
        load_tiles(flat_ref, out)
    fold_tiles(inverse_ref, force_ref, keep_ref, 25)

    home = []
    for g in range(2):
        hit = one_hot(own_column[:HALF] == right_f[:HALF] + float(g * LANES + 1))
        home.append(
            jnp.dot(
                jnp.broadcast_to(lane_f[:, :HALF] + 1.0, (8, HALF)).astype(jnp.bfloat16),
                hit,
                preferred_element_type=jnp.float32,
            )[0:1]
            - 1.0
        )
    pair_key = jnp.where(pair_element > 0.0, table_row * 256.0 + pair_element - 1.0, -3.0)
    notes = (
        [chunks[c][2] for c in range(3)]
        + [chunks[c][1] - 1.0 for c in range(3)]
        + keys
        + [pair_key, lane_f, lane_f + float(LANES)]
        + [pair_side - 1.0]
        + home
        + [jnp.zeros((1, LANES), jnp.float32)]
    )
    note_ref[...] = jnp.concatenate(notes, axis=0)

    row = lax.broadcasted_iota(jnp.int32, (8, LANES), 0)
    side = jnp.broadcast_to(side_row, (8, LANES))
    own_here = jnp.broadcast_to(own_node.astype(jnp.int32), (8, LANES))
    zero = jnp.zeros((8, LANES), jnp.float32)
    for q in range(OTHERS + 1):
        node_q = jnp.broadcast_to(wanted[q], (8, LANES)).astype(jnp.int32)
        code_ref[q] = jnp.where((node_q >= 0) & (node_q // 25 == row), node_q % 25, -1)
    for bc in range(25):
        set_tile(z_ref, jnp.where(own_here == 25 * row + bc, jnp.where(row < 5, 1.0, 0.0), 0.0), bc)
        set_tile(hc_ref, zero, bc)
        set_tile(hz_ref, zero, bc)
        set_tile(state_ref, zero, bc, 0, 2)
    for n in range(STEPS):
        seen_ref[n] = zero
    for bc in range(25, 40):
        set_tile(z_ref, zero, bc)
        set_tile(y_ref, zero, bc, 0, 2)
        set_tile(y_ref, zero, bc, 1, 2)

    is_box = where_ref[0] == 0

    def note_free(moment, drive):
        extra = partner_faces(y_ref, face_ref, side, 0, 2)
        code = code_ref[0]
        seen = zero
        for bc in range(25):
            assembled = tile_of(y_ref, bc, 0, 2) + extra[bc]
            x = tile_of(state_ref, bc, 0, 2)
            h = tile_of(hc_ref, bc)
            seen = seen + jnp.where(code == bc, jnp.where(is_box, assembled, x - h), 0.0)
            if drive is not None:
                kept = tile_of(keep_ref, bc) * x
                pushed = drive * tile_of(force_ref, bc)
                set_tile(
                    state_ref, kept - h + pushed - tile_of(inverse_ref, bc) * assembled, bc, 0, 2
                )
                set_tile(hc_ref, kept - x, bc)
        seen_ref[moment, 7:8] = jnp.sum(seen, axis=0, keepdims=True)

    def step(moment, begin):
        extra = partner_faces(z_ref, face_ref, side)
        for bc in range(25):
            set_tile(state_ref, tile_of(z_ref, bc) + extra[bc], bc, 1, 2)
        stiffness_tiles(state_ref, scale_ref, y_ref, grad_ref, 2, True)
        codes = [code_ref[q] for q in range(OTHERS + 1)]
        seen = [zero] * (OTHERS + 1)
        for bc in range(25):
            x = tile_of(z_ref, bc)
            pushed = tile_of(inverse_ref, bc) * tile_of(y_ref, bc, 1, 2)
            if begin:
                at_once = tile_of(inverse_ref, bc) * x
                adjoint = jnp.where(is_box, pushed, at_once)
                set_tile(hz_ref, jnp.where(is_box, 0.0, at_once), bc)
            else:
                kept = tile_of(keep_ref, bc) * x
                adjoint = kept - tile_of(hz_ref, bc) - pushed
                set_tile(hz_ref, kept - x, bc)
            set_tile(z_ref, adjoint, bc)
            for q in range(OTHERS + 1):
                seen[q] = seen[q] + jnp.where(codes[q] == bc, adjoint, 0.0)
        for q in range(OTHERS + 1):
            seen_ref[moment, q : q + 1] = jnp.sum(seen[q], axis=0, keepdims=True)

    def free_and_adjoint(moment, _):
        note_free(moment, coef_ref[0, moment])
        step(moment, False)
        return 0

    for bc in range(25):
        set_tile(state_ref, coef_ref[0, 0] * tile_of(force_ref, bc), bc, 0, 2)
    step(0, True)
    lax.fori_loop(1, STEPS - 1, free_and_adjoint, 0)
    note_free(STEPS - 1, None)
    seen = []
    extras = []
    for n in range(STEPS):
        rows = seen_ref[n]
        rows = rows + pltpu.roll(rows, HALF, 1)
        seen.append(rows)
        extras.append(jnp.where(used, gather_packed(rows, entry_at)[0:1], 0.0))
    for k in range(FREE_ROWS):
        out_ref[0, :, k * LANES : (k + 1) * LANES] = jnp.where(lane_low, seen[2 * k][7:8], seen[2 * k + 1][7:8])
    for k in range(PAIRS):
        r = GAIN_ROW + k
        out_ref[0, :, r * LANES : (r + 1) * LANES] = jnp.where(lane_low, seen[2 * k][0:1], seen[2 * k + 1][0:1])
        r = EXTRA_ROW + k
        out_ref[0, :, r * LANES : (r + 1) * LANES] = jnp.where(lane_low, extras[2 * k], extras[2 * k + 1])
    starts = jnp.where(lane == HALF, jnp.where(too_long, 1.0, 0.0), pltpu.roll(start, HALF, 1))
    out_ref[0, :, INDEX_ROW * LANES : PAYLOAD * LANES] = jnp.where(lane_low, entry_gid, starts)
    for k in range(1, out_ref.shape[0]):
        out_ref[k] = out_ref[0]


def final_kernel(
    where_ref,
    time_ref,
    mine_ref,
    other_ref,
    wave_ref,
    mass_ref,
    source_ref,
    weight_ref,
    count_ref,
    pair_ref,
    note_ref,
    now_ref,
    before_ref,
    both_ref,
    spread_ref,
    input_ref,
    scale_ref,
    inverse_ref,
    force_ref,
    keep_ref,
    x_ref,
    old_ref,
    h_ref,
    y_ref,
    grad_ref,
    face_ref,
    kick_ref,
    node_ref,
):
    is_box = where_ref[0] == 0
    parity = where_ref[1] % 2
    for core, source in ((parity, mine_ref), (1 - parity, other_ref)):
        for s in range(2):
            for r in range(PAYLOAD):
                both_ref[core, s, r] = source[8 * s : 8 * s + 8, 0, r * LANES : (r + 1) * LANES]
    low = lax.broadcasted_iota(jnp.int32, (8, LANES), 1) < HALF

    def rows(section, core, r):
        return both_ref[core, section, r]

    row = lax.broadcasted_iota(jnp.int32, (8, LANES), 0)
    point = lax.broadcasted_iota(jnp.int32, (8, LANES), 1) % HALF
    index = {}
    for s in range(2):
        for p in range(2):
            pair = rows(s, p, INDEX_ROW).astype(jnp.int32)
            turned = pltpu.roll(pair, HALF, 1)
            start = jnp.where(point == 0, 0, jnp.where(low, turned, pair))
            stop = jnp.where(point == HALF - 1, HALF, pltpu.roll(start, LANES - 1, 1))
            own = point // CAPC * HALF + (2 * row + p) * CAPC + point % CAPC
            index[s, p] = (own, jnp.where(low, pair, turned), start, stop)
    note = note_ref[...]
    at = jnp.where(row < 3, note[0:8], 0.0).astype(jnp.int32)
    packed = {}
    pairs = {}
    last = {}
    zero = jnp.zeros((8, LANES), jnp.float32)
    for n in range(1, STEPS):
        value = {}
        for s in range(2):
            for p in range(2):
                free = rows(s, p, n // 2)
                total = jnp.where(low, free, 0.0) if n % 2 == 0 else jnp.where(low, 0.0, free)
                more = zero
                for k in range(PAIRS):
                    m = n - 2 * k - 1
                    if m >= 1:
                        total = total + rows(s, p, GAIN_ROW + k) * pairs[s, p, 0, m]
                        more = more + rows(s, p, EXTRA_ROW + k) * pairs[s, p, 1, m]
                total = total + pltpu.roll(total, HALF, 1)
                if n > 1:
                    more = more + pltpu.roll(more, HALF, 1)
                    _, _, start, stop = index[s, p]
                    for q in range(OTHERS):
                        got = jnp.take_along_axis(
                            more, jnp.minimum(start + q, HALF - 1), axis=1, mode="promise_in_bounds"
                        )
                        total = total + jnp.where(start + q < stop, got, 0.0)
                value[s, p] = total
        for s in range(2):
            packed[s] = jnp.where(low, value[s, 0], value[s, 1])
        packed[1] = PENALTY * packed[1]
        input_ref[n] = gather_packed(jnp.where(is_box, packed[1], packed[0]), at)
        if n < STEPS - 1:
            for s in range(2):
                for p in range(2):
                    for q in range(2):
                        got = gather_packed(packed[1 - s], index[s, p][q])
                        pairs[s, p, q, n] = jnp.where(low, got, last.get((s, p, q), zero))
                        last[s, p, q] = got
    for c in range(3):
        point_key = across(note[6 + c : 7 + c])
        for g in range(3):
            matrix = one_hot(point_key == note[9 + g : 10 + g])
            spread_ref[c * LANES : (c + 1) * LANES, g * LANES : (g + 1) * LANES] = matrix
            spread_ref[(c + 3) * LANES : (c + 4) * LANES, g * LANES : (g + 1) * LANES] = matrix
    side = jnp.broadcast_to(note[12:13].astype(jnp.int32), (8, LANES))
    own_fields = [
        weight_ref[...] * wave_ref[:, 0, :],
        DT_SQUARED * mass_ref[:, 0, :],
        source_ref[:, 0, :],
        count_ref[...][:NODES],
    ]
    kick_ref[...] = jnp.zeros(kick_ref.shape, jnp.float32)
    for k, out in enumerate((scale_ref, inverse_ref, force_ref, keep_ref)):
        kick_ref[0:NODES] = pair_ref[k][:NODES]
        kick_ref[200 : 200 + NODES] = own_fields[k][:, :LANES]
        kick_ref[400 : 400 + NODES] = own_fields[k][:, LANES:]
        for g in range(3):
            load_tiles(kick_ref, out, g, 3, 200 * g)
    fold_tiles(inverse_ref, force_ref, keep_ref, 75)
    for g in range(3):
        for bc in range(25, 40):
            set_tile(y_ref, zero, bc, g, 3)
        for bc in range(25):
            set_tile(x_ref, time_ref[0, 0] * tile_of(force_ref, bc, g, 3), bc, g, 3)
            set_tile(h_ref, zero, bc, g, 3)
    node_row = lax.broadcasted_iota(jnp.int32, (LANES, LANES), 0)
    point_node = note[3:6].astype(jnp.int32)
    for c in range(3):
        node_ref[:, c * LANES : (c + 1) * LANES] = one_hot(node_row == point_node[c : c + 1])

    def step(moment, _):
        drive = time_ref[0, moment]
        stiffness_tiles(x_ref, scale_ref, y_ref, grad_ref, 3, False)
        inputs = input_ref[moment]
        high = inputs.astype(jnp.bfloat16)
        rest = (inputs - high.astype(jnp.float32)).astype(jnp.bfloat16)
        parts = [
            node_ref[:, c * LANES : (c + 1) * LANES] * part[c : c + 1]
            for part in (high, rest)
            for c in range(3)
        ]
        kick = jnp.dot(
            jnp.concatenate(parts, axis=1), spread_ref[...], preferred_element_type=jnp.float32
        )
        for g in range(3):
            kick_ref[200 * g : 200 * g + LANES] = kick[:, g * LANES : (g + 1) * LANES]
        extra = partner_faces(y_ref, face_ref, side, 0, 3)
        for g in range(3):
            for bc in range(25):
                net = kick_ref[pl.ds(200 * g + bc, 8, stride=25), :] - tile_of(y_ref, bc, g, 3)
                if g == 0:
                    net = net - extra[bc]
                x = tile_of(x_ref, bc, g, 3)
                kept = tile_of(keep_ref, bc, g, 3) * x
                pushed = drive * tile_of(force_ref, bc, g, 3)
                advanced = kept - tile_of(h_ref, bc, g, 3) + pushed
                set_tile(x_ref, advanced + tile_of(inverse_ref, bc, g, 3) * net, bc, g, 3)
                set_tile(h_ref, kept - x, bc, g, 3)
                set_tile(old_ref, x, bc, g, 3)
        return 0

    lax.fori_loop(1, STEPS, step, 0)
    home = jnp.concatenate([note[13:14], note[14:15]], axis=1).astype(jnp.int32)
    linked = jnp.where(
        home == lax.broadcasted_iota(jnp.int32, (LANES, 2 * LANES), 0), 1.0, 0.0
    ).astype(jnp.bfloat16)
    alone = home < 0

    for tiles_ref, out_ref in ((old_ref, before_ref), (x_ref, now_ref)):
        for g in range(3):
            for bc in range(25):
                kick_ref[pl.ds(200 * g + bc, 8, stride=25), :] = tile_of(tiles_ref, bc, g, 3)
        moved = exact_pick(kick_ref[0:LANES], linked)
        for g in range(2):
            own = kick_ref[200 * (g + 1) : 200 * (g + 1) + LANES]
            cut = slice(g * LANES, (g + 1) * LANES)
            out_ref[:, 0, cut] = jnp.where(alone[:, cut], own, moved[:, cut])[:NODES]


def fast_body(wave_speed, inverse_mass, source_field, source_time, face_links, coupling_links):
    _, weight_np, _ = node_tables()
    weight = jnp.asarray(weight_np).reshape(NODES, 1)
    wave, mass, source = [
        jnp.transpose(field, (1, 0, 2)) for field in (wave_speed, inverse_mass, source_field)
    ]
    faces = jnp.transpose(face_links, (1, 0, 2))
    blocks = lax.axis_size("blk")
    columns = wave_speed.shape[-1]
    me = lax.axis_index("blk")
    place = jnp.stack([lax.axis_index("sec"), me]).astype(jnp.int32)
    vmem = pl.BlockSpec(memory_space=pltpu.VMEM)
    smem = pl.BlockSpec(memory_space=pltpu.SMEM)
    params = pltpu.CompilerParams(vmem_limit_bytes=16 << 20)

    def shape(*dims):
        return jax.ShapeDtypeStruct(dims, jnp.float32)

    links, m0, m1, m2, m3, count = pl.pallas_call(
        pack_kernel,
        out_shape=[shape(blocks, 8, LANES)] + [shape(16, 4 * LANES)] * 4 + [shape(LANES, columns)],
        in_specs=[smem] + [vmem] * 6,
        out_specs=[vmem] * 6,
        compiler_params=params,
    )(place, wave, mass, source, weight, faces, coupling_links)
    mine = [m0, m1, m2, m3]
    ghost = [partner_2(part, "blk", j) for j, part in enumerate(mine)]
    every = lax.all_to_all(links, "blk", 0, 0, tiled=True)

    def tiles(count):
        return pltpu.VMEM((8 * count, LANES), jnp.float32)

    payload, pair, note = pl.pallas_call(
        response_kernel,
        out_shape=[shape(blocks, 1, PAYLOAD * LANES), shape(4, LANES, LANES), shape(16, LANES)],
        in_specs=[smem] * 2 + [vmem] * 14,
        out_specs=[vmem] * 3,
        compiler_params=params,
        scratch_shapes=[tiles(25)] * 5
        + [tiles(50), tiles(40), tiles(25), tiles(25), tiles(80), tiles(50), tiles(5)]
        + [pltpu.VMEM((8, 8, LANES), jnp.int32), pltpu.VMEM((STEPS, 8, LANES), jnp.float32)],
    )(
        place,
        source_time,
        wave,
        mass,
        source,
        weight,
        count,
        *mine,
        *ghost,
        every,
    )

    same_core = [[c + 2 * i for i in range(blocks)] for c in range(2)]
    received = lax.all_to_all(
        payload, ("sec", "blk"), 0, 0, axis_index_groups=same_core, tiled=True
    )
    sibling = partner_2(received, "blk", 0)
    flag = INDEX_ROW * LANES + HALF
    overflow = jnp.max(
        jnp.maximum(received[:, 0, flag], sibling[:, 0, flag])
    ) > 0

    def quick(_):
        return tuple(
            pl.pallas_call(
                final_kernel,
                out_shape=[shape(NODES, 1, columns)] * 2,
                in_specs=[smem] * 2 + [vmem] * 9,
                out_specs=[vmem] * 2,
                compiler_params=params,
                scratch_shapes=[
                    pltpu.VMEM((2, 2, PAYLOAD, 8, LANES), jnp.float32),
                    pltpu.VMEM((6 * LANES, 3 * LANES), jnp.bfloat16),
                    pltpu.VMEM((STEPS, 8, LANES), jnp.float32),
                ]
                + [tiles(75)] * 7
                + [tiles(120), tiles(75), tiles(5), tiles(75)]
                + [pltpu.VMEM((LANES, 3 * LANES), jnp.bfloat16)],
            )(
                place,
                source_time,
                received,
                sibling,
                wave,
                mass,
                source,
                weight,
                count,
                pair,
                note,
            )
        )

    def slow(_):
        results = general_body(
            wave_speed, inverse_mass, source_field, source_time, face_links, coupling_links
        )
        return tuple(jnp.transpose(field, (1, 0, 2)) for field in results)

    now, before = lax.cond(overflow, slow, quick, 0)
    return (jnp.transpose(now, (1, 0, 2)), jnp.transpose(before, (1, 0, 2)))


def body(*arguments):
    wave_speed, _, _, _, face_links, coupling_links = arguments
    fits = (
        lax.axis_size("blk") == 16
        and lax.axis_size("sec") == 2
        and wave_speed.shape[1:] == (NODES, 2 * LANES)
        and face_links.shape[-1] == LANES
        and coupling_links.shape[-1] >= CAPC * 16
    )
    return fast_body(*arguments) if fits else general_body(*arguments)


def solution(mesh):
    in_specs = (
        P("sec", None, "blk"),
        P("sec", None, "blk"),
        P("sec", None, "blk"),
        P("sec", None),
        P("sec", None, "blk"),
        P(None, "blk"),
    )
    out_specs = (P("sec", None, "blk"), P("sec", None, "blk"))
    return jax.shard_map(body, mesh=mesh, in_specs=in_specs, out_specs=out_specs, check_vma=False)
```

```python
import jax
import jax.numpy as jnp
import numpy as np
from jax import lax
from jax.experimental import pallas as pl
from jax.experimental.pallas import tpu as pltpu
from jax.sharding import PartitionSpec as P

CAPC = 4
STEPS = 12


DT_SQUARED = 0.05
PENALTY = 10.0


def partner_2(value, axis, stride):
    return lax.ppermute(value, axis, [(i, i ^ 1 << stride) for i in range(lax.axis_size(axis))])


def node_tables():
    abscissae = np.array([-1.0, -np.sqrt(3.0 / 7.0), 0.0, np.sqrt(3.0 / 7.0), 1.0])
    weights = np.array([0.1, 49.0 / 90.0, 32.0 / 45.0, 49.0 / 90.0, 0.1])
    legendre = (35.0 * abscissae**4 - 30.0 * abscissae**2 + 3.0) / 8.0
    derivative = np.zeros((5, 5))
    for i in range(5):
        for j in range(5):
            if i != j:
                derivative[i, j] = legendre[i] / (legendre[j] * (abscissae[i] - abscissae[j]))
    derivative[0, 0] = -2.5
    derivative[4, 4] = 2.5
    identity = np.eye(5)
    operator = np.concatenate(
        [
            np.kron(np.kron(derivative, identity), identity),
            np.kron(np.kron(identity, derivative), identity),
            np.kron(np.kron(identity, identity), derivative),
        ],
        axis=0,
    )
    weight_cube = weights[:, None, None] * weights[None, :, None] * weights[None, None, :]
    lattice = np.arange(125).reshape(5, 5, 5)
    face_nodes = np.stack(
        [
            lattice[0].ravel(),
            lattice[4].ravel(),
            lattice[:, 0].ravel(),
            lattice[:, 4].ravel(),
            lattice[:, :, 0].ravel(),
            lattice[:, :, 4].ravel(),
        ]
    )
    return (
        operator.astype(np.float32),
        weight_cube.reshape(125, 1).astype(np.float32),
        face_nodes.astype(np.int32),
    )


def stiffness(field_in, speed_sq, operator, weight_cube):
    columns = field_in.shape[-1]
    scaling = weight_cube * speed_sq
    grads = jnp.dot(
        operator, field_in, precision=lax.Precision.HIGHEST, preferred_element_type=jnp.float32
    )
    scaled = (grads.reshape(3, 125, columns) * scaling[None]).reshape(375, columns)
    return jnp.dot(
        operator.T, scaled, precision=lax.Precision.HIGHEST, preferred_element_type=jnp.float32
    )


def general_body(wave_speed, inverse_mass, source_field, source_time, face_links, coupling_links):
    operator_np, weight_np, faces_np = node_tables()
    operator = jnp.asarray(operator_np)
    weight_cube = jnp.asarray(weight_np)
    picker_np = np.zeros((150, 125), np.float32)
    for side_number in range(6):
        for node_number in range(25):
            picker_np[side_number * 25 + node_number, faces_np[side_number, node_number]] = 1.0
    picker = jnp.asarray(picker_np)
    spreader = jnp.asarray(picker_np.T.copy())
    speed_sq = wave_speed[0]
    inverse = inverse_mass[0]
    forcing = source_field[0]
    timing = source_time[0]
    element = face_links[0, 0]
    face_side = face_links[0, 1]
    face_peer = face_links[0, 2]
    blocks = lax.axis_size("blk")
    bit_count = blocks.bit_length() - 1
    myself = lax.axis_index("blk")
    is_box = lax.axis_index("sec") == 0
    records = element.shape[0]
    per_peer = records // 8
    ordinal = jnp.arange(records)
    linked = face_peer != myself
    side_mask = face_side[None, None, :] == jnp.arange(6, dtype=jnp.int32)[:, None, None]
    earlier = ordinal[None, :] < ordinal[:, None]
    face_slot = jnp.sum(
        ((face_peer[:, None] == face_peer[None, :]) & earlier).astype(jnp.int32), axis=1
    )
    offset_bits = jnp.bitwise_xor(face_peer, myself)
    bit_index = jnp.zeros((records,), jnp.int32)
    for bit_number in range(bit_count):
        bit_index = bit_index + bit_number * (offset_bits == 1 << bit_number).astype(jnp.int32)
    pair_column = jnp.where(linked, bit_index * per_peer + face_slot, 0)
    point_element = coupling_links[0]
    point_node = coupling_links[1]
    point_owner = coupling_links[2]
    target_element = coupling_links[3]
    target_node = coupling_links[4]
    in_use = point_owner >= 0
    owner_safe = jnp.maximum(point_owner, 0)
    point_ordinal = jnp.arange(point_owner.shape[0])
    point_earlier = point_ordinal[None, :] < point_ordinal[:, None]
    point_slot = jnp.sum(
        ((point_owner[:, None] == point_owner[None, :]) & point_earlier).astype(jnp.int32), axis=1
    )
    point_column = jnp.where(in_use, point_slot * blocks + owner_safe, 0)
    slot_total = CAPC * blocks
    outbound = jnp.zeros((3, slot_total), jnp.int32)
    outbound = outbound.at[0, point_column].add(jnp.where(in_use, target_element, 0))
    outbound = outbound.at[1, point_column].add(jnp.where(in_use, target_node, 0))
    outbound = outbound.at[2, point_column].add(in_use.astype(jnp.int32))
    inbound = lax.all_to_all(
        outbound.reshape(3, CAPC, blocks), "blk", split_axis=2, concat_axis=2, tiled=True
    ).reshape(3, slot_total)
    remote_element = inbound[0]
    remote_node = inbound[1]
    remote_flag = inbound[2].astype(jnp.float32)
    target_rows = jnp.concatenate([point_node, remote_node])
    target_cols = jnp.concatenate([point_element, remote_element])
    current = jnp.zeros(speed_sq.shape, jnp.float32)
    previous = jnp.zeros(speed_sq.shape, jnp.float32)
    def one_step(moment, state):
        current, previous = state
        internal = stiffness(current, speed_sq, operator, weight_cube)
        stacked = jnp.dot(
            picker,
            internal[:, element],
            precision=lax.Precision.HIGHEST,
            preferred_element_type=jnp.float32,
        ).reshape(6, 25, records)
        payload = jnp.sum(jnp.where(side_mask, stacked, 0.0), axis=0)
        payload = jnp.where(linked[None, :], payload, 0.0)
        outgoing = (
            jnp.zeros((25, bit_count * per_peer), jnp.float32).at[:, pair_column].add(payload)
        )
        arrived = []
        for bit_number in range(bit_count):
            piece = outgoing[:, bit_number * per_peer : (bit_number + 1) * per_peer]
            arrived.append(partner_2(piece, "blk", bit_number))
        partner = jnp.concatenate(arrived, axis=1)[:, pair_column]
        partner = jnp.where(linked[None, :], partner, 0.0)
        masked = jnp.where(side_mask, partner[None], 0.0).reshape(150, records)
        assembled = internal.at[:, element].add(
            jnp.dot(
                spreader,
                masked,
                precision=lax.Precision.HIGHEST,
                preferred_element_type=jnp.float32,
            )
        )
        velocity = current - previous
        traction = assembled[point_node, point_element]
        box_send = (
            jnp.zeros((slot_total,), jnp.float32)
            .at[point_column]
            .add(jnp.where(in_use, traction, 0.0))
        )
        global_send = velocity[remote_node, remote_element] * remote_flag
        dispatch = jnp.where(is_box, box_send, global_send).reshape(CAPC, blocks)
        crossed = partner_2(dispatch, "sec", 0)
        received = lax.all_to_all(crossed, "blk", split_axis=1, concat_axis=1, tiled=True)
        received = received.reshape(slot_total)
        remote_velocity = received[point_column]
        box_terms = jnp.where(
            in_use, PENALTY * (remote_velocity - velocity[point_node, point_element]), 0.0
        )
        values = jnp.concatenate(
            [jnp.where(is_box, box_terms, 0.0), jnp.where(is_box, 0.0, received * remote_flag)]
        )
        driving = timing[moment] * forcing - assembled
        driving = driving.at[target_rows, target_cols].add(values)
        advanced = 2.0 * current - previous + DT_SQUARED * inverse * driving
        return advanced, current

    current, previous = lax.fori_loop(0, STEPS, one_step, (current, previous))
    return (current[None], previous[None])


LANES = 128
HALF = 64
OTHERS = 5
LAGS = 10
PAIRS = LAGS // 2
FREE_ROWS = STEPS // 2
GAIN_ROW = FREE_ROWS
EXTRA_ROW = GAIN_ROW + PAIRS
INDEX_ROW = EXTRA_ROW + PAIRS
PAYLOAD = INDEX_ROW + 1
NODES = 125
EXACT = lax.Precision.HIGHEST


def line_matrix():
    abscissae = np.array([-1.0, -np.sqrt(3.0 / 7.0), 0.0, np.sqrt(3.0 / 7.0), 1.0])
    legendre = (35.0 * abscissae**4 - 30.0 * abscissae**2 + 3.0) / 8.0
    derivative = np.zeros((5, 5))
    for i in range(5):
        for j in range(5):
            if i != j:
                derivative[i, j] = legendre[i] / (legendre[j] * (abscissae[i] - abscissae[j]))
    derivative[0, 0] = -2.5
    derivative[4, 4] = 2.5
    return derivative


def apply_line(matrix, x):
    odd = [x[0] - x[4], x[1] - x[3]]
    even = [x[0] + x[4], x[1] + x[3]]
    out = [None] * 5
    for i in range(2):
        symmetric = (
            float(0.5 * (matrix[i, 0] - matrix[i, 4])) * odd[0]
            + float(0.5 * (matrix[i, 1] - matrix[i, 3])) * odd[1]
        )
        skew = (
            float(0.5 * (matrix[i, 0] + matrix[i, 4])) * even[0]
            + float(0.5 * (matrix[i, 1] + matrix[i, 3])) * even[1]
            + float(matrix[i, 2]) * x[2]
        )
        out[i] = symmetric + skew
        out[4 - i] = symmetric - skew
    out[2] = float(matrix[2, 0]) * odd[0] + float(matrix[2, 1]) * odd[1]
    return out


def line_tiles():
    row = lax.broadcasted_iota(jnp.int32, (8, LANES), 0)
    tiles = []
    for matrix in (line_matrix(), line_matrix().T):
        columns = []
        for j in range(5):
            tile = jnp.zeros((8, LANES), jnp.float32)
            for i in range(5):
                tile = jnp.where(row == i, float(matrix[i, j]), tile)
            columns.append(tile)
        tiles.append(columns)
    return tiles


def tile_of(ref, bc, group=0, groups=1):
    start = (bc * groups + group) * 8
    return ref[start : start + 8, :]


def set_tile(ref, value, bc, group=0, groups=1):
    start = (bc * groups + group) * 8
    ref[start : start + 8, :] = value


def repeat_row(ref, row):
    return jnp.broadcast_to(ref[row : row + 1, :], (8, LANES))


def stiffness_tiles(x_ref, scale_of, y_ref, grad_ref, groups):
    forward = line_matrix()
    backward = forward.T.copy()
    to_grad, to_node = line_tiles()

    for g in range(groups):

        def scale(bc):
            return scale_of(bc, g)

        def along(index):
            grads = apply_line(forward, [tile_of(x_ref, k, g, groups) for k in index])
            return apply_line(backward, [v * scale(k) for v, k in zip(grads, index)])

        for bc in range(25):
            start = (bc * groups + g) * 8
            total = to_grad[0] * repeat_row(x_ref, start)
            for j in range(1, 5):
                total = total + to_grad[j] * repeat_row(x_ref, start + j)
            grad_ref[start : start + 8, :] = total * scale(bc)
        total = [None] * 25
        for c in range(5):
            index = [5 * j + c for j in range(5)]
            for k, value in zip(index, along(index)):
                total[k] = value
        for b in range(5):
            index = [5 * b + j for j in range(5)]
            for k, value in zip(index, along(index)):
                total[k] = total[k] + value
        for bc in range(25):
            start = (bc * groups + g) * 8
            value = total[bc]
            for j in range(5):
                value = value + to_node[j] * repeat_row(grad_ref, start + j)
            set_tile(y_ref, value, bc, g, groups)


def partner_faces(ref, face_ref, side, group=0, groups=1):
    row = lax.broadcasted_iota(jnp.int32, (8, LANES), 0)
    is_side = [side == q for q in range(6)]
    on_a = (is_side[0] & (row == 0)) | (is_side[1] & (row == 4))
    arrived = []
    for t in range(5):
        first = ref[pl.ds((t * groups + group) * 8, 8, stride=40 * groups), :]
        last = ref[pl.ds((t * groups + group) * 8 + 4, 8, stride=40 * groups), :]
        value = jnp.where(is_side[1], last, first)
        value = jnp.where(is_side[2], tile_of(ref, t, group, groups), value)
        value = jnp.where(is_side[3], tile_of(ref, 20 + t, group, groups), value)
        value = jnp.where(is_side[4], tile_of(ref, 5 * t, group, groups), value)
        value = jnp.where(is_side[5], tile_of(ref, 5 * t + 4, group, groups), value)
        value = pltpu.roll(value, HALF, 1)
        arrived.append(value)
        set_tile(face_ref, value, t)
    extra = []
    for b in range(5):
        for c in range(5):
            value = jnp.where(on_a, repeat_row(face_ref, 8 * c + b), 0.0)
            if b == 0:
                value = jnp.where(is_side[2], arrived[c], value)
            if b == 4:
                value = jnp.where(is_side[3], arrived[c], value)
            if c == 0:
                value = jnp.where(is_side[4], arrived[b], value)
            if c == 4:
                value = jnp.where(is_side[5], arrived[b], value)
            extra.append(value)
    return extra


def load_tiles(flat_ref, out_ref, group=0, groups=1, start=0):
    for bc in range(25):
        set_tile(out_ref, flat_ref[pl.ds(start + bc, 8, stride=25), :], bc, group, groups)


def fold_tiles(inverse_ref, force_ref, keep_ref, count):
    for k in range(count):
        inverse = tile_of(inverse_ref, k)
        set_tile(force_ref, inverse * tile_of(force_ref, k), k)
        set_tile(keep_ref, 2.0 - inverse * (PENALTY * tile_of(keep_ref, k)), k)


def across(row_values):
    return jnp.broadcast_to(row_values, (LANES, LANES)).T


def rank_among(row_values):
    down = lax.broadcasted_iota(jnp.int32, (LANES, LANES), 0)
    right = lax.broadcasted_iota(jnp.int32, (LANES, LANES), 1)
    same = (across(row_values) == row_values) & (down < right)
    return jnp.sum(jnp.where(same, 1.0, 0.0), axis=0, keepdims=True)


def one_hot(condition):
    return jnp.where(condition, 1.0, 0.0).astype(jnp.bfloat16)


def plain_dot(a, b):
    return jnp.dot(a.astype(jnp.bfloat16), b, preferred_element_type=jnp.float32)


def exact_pick(values, chosen, transposed=False):
    total = None
    rest = values
    for _ in range(3):
        part = rest.astype(jnp.bfloat16)
        if transposed:
            got = lax.dot_general(
                chosen, part, (((1,), (1,)), ((), ())), preferred_element_type=jnp.float32
            )
        else:
            got = jnp.dot(part, chosen, preferred_element_type=jnp.float32)
        total = got if total is None else total + got
        rest = rest - part.astype(jnp.float32)
    return total


def lane_row():
    return lax.broadcasted_iota(jnp.int32, (1, LANES), 1)


def pack_kernel(
    where_ref,
    wave_ref,
    mass_ref,
    source_ref,
    weight_ref,
    face_ref,
    couple_ref,
    links_ref,
    m0_ref,
    m1_ref,
    m2_ref,
    m3_ref,
    count_ref,
):
    me = where_ref[1]
    me_f = me.astype(jnp.float32)
    is_box = where_ref[0] == 0
    down = lax.broadcasted_iota(jnp.int32, (LANES, LANES), 0)
    right = lax.broadcasted_iota(jnp.int32, (LANES, LANES), 1)
    right_f = right.astype(jnp.float32)
    lane = lane_row()

    live = couple_ref[:, 0:LANES].astype(jnp.float32)
    owner = jnp.where(lane < HALF, live[2:3], -1.0)
    slot = jnp.where(owner >= 0.0, owner * CAPC + rank_among(owner), -1.0)
    to_slot = one_hot(across(slot) == right_f)
    named = jnp.concatenate([live[0:2], live[3:5], jnp.full((4, LANES), -1.0)], axis=0) + 1.0
    links = plain_dot(named, to_slot)
    for k in range(links_ref.shape[0]):
        links_ref[k] = links

    faces = face_ref[:, 0, :]
    peer = faces[2:3]
    linked = peer != me
    distance = peer ^ me
    bit = jnp.zeros((1, LANES), jnp.float32)
    for j in range(1, 4):
        bit = bit + jnp.where(distance == 1 << j, float(j), 0.0)
    face_slot = jnp.where(linked, bit * 16.0 + rank_among(peer.astype(jnp.float32)), -1.0)
    to_record = one_hot(across(face_slot) == right_f)
    facts = jnp.concatenate([faces[0:2].astype(jnp.float32) + 1.0, jnp.zeros((6, LANES))], axis=0)
    record = plain_dot(facts, to_record)

    node_one = lax.broadcasted_iota(jnp.int32, (LANES, LANES), 0).astype(jnp.float32) + 1.0
    own_nodes = one_hot(node_one == links[1:2])
    point_column = across(links[0:1])
    record_column = across(record[0:1])
    side_column = across(record[1:2])
    counts = []
    taken = []
    for g in range(2):
        column_one = right_f + float(g * LANES + 1)
        counts.append(
            jnp.dot(own_nodes, one_hot(point_column == column_one), preferred_element_type=jnp.float32)
        )
        taken.append(one_hot(record_column == column_one)[:HALF])
    count = jnp.concatenate(counts, axis=1) * jnp.where(is_box, 1.0, 0.0)
    count_ref[...] = count
    take = jnp.concatenate(taken, axis=1)
    pad = jnp.zeros((LANES - NODES, 2 * LANES), jnp.float32)
    stiff = jnp.concatenate([weight_ref[...] * wave_ref[:, 0, :], pad], axis=0)
    mass = jnp.concatenate([DT_SQUARED * mass_ref[:, 0, :], pad], axis=0)
    source = jnp.concatenate([source_ref[:, 0, :], pad], axis=0)
    first = exact_pick(stiff, take, True)
    first = jnp.where(right[:HALF] == 125, record_column[:HALF], first)
    first = jnp.where(right[:HALF] == 126, side_column[:HALF], first)
    parts = [
        first,
        exact_pick(mass, take, True),
        exact_pick(source, take, True),
        lax.dot_general(
            take,
            count.astype(jnp.bfloat16),
            (((1,), (1,)), ((), ())),
            preferred_element_type=jnp.float32,
        ),
    ]
    for j, out in enumerate((m0_ref, m1_ref, m2_ref, m3_ref)):
        for k in range(4):
            out[:, k * LANES : (k + 1) * LANES] = parts[k][16 * j : 16 * j + 16]


def point_tables(where_ref, every_ref):
    me = where_ref[1]
    is_box = where_ref[0] == 0
    lane = lane_row()
    low = lane < HALF
    blocks = every_ref.shape[0]
    down = lax.broadcasted_iota(jnp.int32, (blocks, LANES), 0)
    right = lax.broadcasted_iota(jnp.int32, (blocks, LANES), 1)
    mine = right // CAPC == down
    tables = []
    for offset in (0, 1, 2, 4, 8):
        beta = me ^ offset
        at = beta * CAPC + right % CAPC
        rows = []
        for f in range(2):
            direct = every_ref[beta, f : f + 1, :]
            column = every_ref[:, 2 + f, :]
            picked = jnp.concatenate(
                [
                    jnp.take_along_axis(column[8 * h : 8 * h + 8], at[8 * h : 8 * h + 8], axis=1,
                                        mode="promise_in_bounds")
                    for h in range(blocks // 8)
                ],
                axis=0,
            )
            turned = jnp.sum(jnp.where(mine, picked, 0.0), axis=0, keepdims=True)
            row = jnp.where(is_box, direct, turned)
            rows.append(jnp.where(low, row, 0.0))
        inputs = lane // CAPC * HALF + beta * CAPC + lane % CAPC
        rows.append(jnp.where(low, inputs, 0).astype(jnp.float32))
        tables.append(rows)
    tables.append([jnp.zeros((1, LANES), jnp.float32)] * 3)
    chunks = []
    for c in range(3):
        chunks.append(
            [
                jnp.where(low, tables[2 * c][f], pltpu.roll(tables[2 * c + 1][f], HALF, 1))
                for f in range(3)
            ]
        )
    keys = []
    for c in range(3):
        table = jnp.where(low, float(2 * c), float(2 * c + 1))
        element, node, _ = chunks[c]
        keys.append(jnp.where(node > 0.0, table * 256.0 + element - 1.0, -1.0))
    return chunks, keys


def gather_packed(packed, at):
    rows = at // LANES
    lanes = at % LANES
    out = jnp.zeros(at.shape, jnp.float32)
    for k in range(8):
        source = jnp.broadcast_to(packed[k : k + 1], at.shape)
        picked = jnp.take_along_axis(source, lanes, axis=1, mode="promise_in_bounds")
        out = jnp.where(rows == k, picked, out)
    return out


def point_kernel(
    where_ref,
    wave_ref,
    mass_ref,
    source_ref,
    weight_ref,
    count_ref,
    every_ref,
    table_ref,
    copy_ref,
    scale_ref,
    inverse_ref,
    force_ref,
    keep_ref,
    flat_ref,
):
    chunks, keys = point_tables(where_ref, every_ref)
    rows = [chunks[c][f] for c in range(3) for f in range(3)] + keys
    table_ref[...] = jnp.concatenate(rows + [jnp.zeros((4, LANES), jnp.float32)], axis=0)
    down = lax.broadcasted_iota(jnp.int32, (LANES, LANES), 0)
    right = lax.broadcasted_iota(jnp.int32, (LANES, LANES), 1)
    element = chunks[0][0]
    element_both = jnp.where(lane_row() < HALF, element, pltpu.roll(element, HALF, 1))
    take = [
        one_hot((down.astype(jnp.float32) + float(g * LANES + 1) == element_both) & (right < HALF))
        for g in range(2)
    ]
    take = jnp.concatenate(take, axis=0)
    own_fields = [
        weight_ref[...] * wave_ref[:, 0, :],
        DT_SQUARED * mass_ref[:, 0, :],
        source_ref[:, 0, :],
        count_ref[...][:NODES],
    ]
    flat_ref[...] = jnp.zeros(flat_ref.shape, jnp.float32)
    copy_ref[...] = jnp.zeros(copy_ref.shape, jnp.float32)
    for k, out in enumerate((scale_ref, inverse_ref, force_ref, keep_ref)):
        pick = plain_dot if k == 3 else exact_pick
        copy_ref[k, 0:NODES] = pick(own_fields[k], take)
        for g in range(2):
            flat_ref[200 * g : 200 * g + NODES] = own_fields[k][:, g * LANES : (g + 1) * LANES]
            load_tiles(flat_ref, out, g, 2, 200 * g)
    fold_tiles(inverse_ref, force_ref, keep_ref, 50)


def response_kernel(
    where_ref,
    coef_ref,
    table_ref,
    copy_ref,
    m0_ref,
    m1_ref,
    m2_ref,
    m3_ref,
    g0_ref,
    g1_ref,
    g2_ref,
    g3_ref,
    out_ref,
    pair_ref,
    note_ref,
    flat_ref,
    scale_ref,
    inverse_ref,
    force_ref,
    keep_ref,
    state_ref,
    z_ref,
    hc_ref,
    hz_ref,
    y_ref,
    grad_ref,
    face_ref,
    code_ref,
    seen_ref,
):
    down = lax.broadcasted_iota(jnp.int32, (LANES, LANES), 0)
    right = lax.broadcasted_iota(jnp.int32, (LANES, LANES), 1)
    right_f = right.astype(jnp.float32)
    lane = lane_row()
    lane_low = lane < HALF
    lane_f = lane.astype(jnp.float32)

    stacked = jnp.concatenate(
        [r[...] for r in (m0_ref, m1_ref, m2_ref, m3_ref, g0_ref, g1_ref, g2_ref, g3_ref)], axis=0
    )
    pair = [stacked[:, k * LANES : (k + 1) * LANES].T for k in range(4)]
    for k in range(4):
        pair_ref[k] = pair[k]
    pair_element = pair[0][125:126]
    pair_side = pair[0][126:127]
    own_column = jnp.broadcast_to(stacked[:HALF, 125:126], (HALF, LANES))
    own_column = jnp.concatenate([own_column, own_column], axis=0)

    chunks = [[table_ref[3 * c + f : 3 * c + f + 1] for f in range(3)] for c in range(3)]
    keys = [table_ref[9 + c : 10 + c] for c in range(3)]
    element, node, _ = chunks[0]
    element_both = jnp.where(lane_low, element, pltpu.roll(element, HALF, 1))
    node_low = jnp.where(lane_low, node, 0.0)
    present = element_both > 0.0
    same_half = (down < HALF) == (right < HALF)
    of_record = (own_column == element_both) & present & same_half
    facts_matrix = one_hot(of_record)
    partner_matrix = one_hot(of_record & (down >= HALF))
    table_row = jnp.where(lane_low, 0.0, (1 + (lane - HALF) // 16).astype(jnp.float32))
    facts = plain_dot(
        jnp.concatenate([pair_side, pair_element, table_row, jnp.zeros((5, LANES))], axis=0),
        facts_matrix,
    )
    side_row = facts[0:1].astype(jnp.int32) - 1
    partner = pltpu.roll(facts, HALF, 1)
    ghost_key = jnp.where(partner[1:2] > 0.0, partner[2:3] * 256.0 + partner[1:2] - 1.0, -5.0)
    own_key = jnp.where(element > 0.0, element - 1.0, -5.0)
    own_key = jnp.where(lane_low, own_key, -5.0)
    ghost_key = jnp.where(lane_low, ghost_key, -5.0)

    match = [(across(keys[c]) == own_key) | (across(keys[c]) == ghost_key) for c in range(3)]
    match[0] = match[0] & (down != right)
    matched = [jnp.where(m, 1.0, 0.0) for m in match]
    lower = one_hot(right < down)
    before = jnp.zeros((1, LANES), jnp.float32)
    lists = [jnp.zeros((8, LANES), jnp.float32)] * OTHERS
    for c in range(3):
        place = jnp.dot(lower, matched[c].astype(jnp.bfloat16), preferred_element_type=jnp.float32)
        place = jnp.where(match[c], place + before, -1.0)
        before = before + jnp.sum(matched[c], axis=0, keepdims=True)
        _, node_c, gid_c = chunks[c]
        gid_high = jnp.floor(gid_c * (1.0 / 256.0))
        table_c = jnp.where(lane_low, float(2 * c), float(2 * c + 1))
        described = jnp.concatenate(
            [node_c, gid_high, gid_c - 256.0 * gid_high, table_c, jnp.zeros((4, LANES))], axis=0
        )
        for q in range(OTHERS):
            lists[q] = lists[q] + plain_dot(described, one_hot(place == float(q)))
    own_node = jnp.where(lane_low, node - 1.0, -1.0)
    wanted = [own_node]
    gids = [jnp.zeros((1, LANES), jnp.float32)]
    for q in range(OTHERS):
        node_q = lists[q][0:1] - 1.0
        there = lists[q][3:4] > 0.0
        gids.append(lists[q][1:2] * 256.0 + lists[q][2:3])
        wanted.append(
            jnp.where(
                lane_low,
                jnp.where(there, -1.0, node_q),
                pltpu.roll(jnp.where(there, node_q, -1.0), HALF, 1),
            )
        )
    gids.append(jnp.zeros((7 - OTHERS, LANES), jnp.float32))

    length = jnp.minimum(before, 200.0)
    start = plain_dot(jnp.broadcast_to(length, (8, LANES)), one_hot(down < right))[0:1]
    too_long = (jnp.max(before) > float(OTHERS)) | (jnp.max(start + length) > float(HALF))
    entry = right % HALF
    entry_f = entry.astype(jnp.float32)
    is_point = down < HALF
    owner_of = jnp.sum(
        jnp.where(is_point & (across(start + length) <= entry_f), 1.0, 0.0), axis=0, keepdims=True
    )
    begun = jnp.sum(
        jnp.where(down.astype(jnp.float32) == owner_of, across(start), 0.0), axis=0, keepdims=True
    )
    used = owner_of < float(HALF)
    which = jnp.clip(entry_f[0:1] - begun, 0.0, float(OTHERS - 1)) + 1.0
    entry_at = jnp.where(used, which * float(LANES) + owner_of, 0.0).astype(jnp.int32)
    entry_at = jnp.broadcast_to(entry_at, (8, LANES))
    entry_gid = jnp.where(used, gather_packed(jnp.concatenate(gids, axis=0), entry_at)[0:1], 0.0)

    flat_ref[...] = jnp.zeros(flat_ref.shape, jnp.float32)
    for k, out in enumerate((scale_ref, inverse_ref, force_ref, keep_ref)):
        pick = plain_dot if k == 3 else exact_pick
        flat_ref[0:NODES] = (copy_ref[k] + pick(pair[k], partner_matrix))[:NODES]
        load_tiles(flat_ref, out)
    fold_tiles(inverse_ref, force_ref, keep_ref, 25)

    home = []
    for g in range(2):
        hit = one_hot(own_column[:HALF] == right_f[:HALF] + float(g * LANES + 1))
        home.append(
            jnp.dot(
                jnp.broadcast_to(lane_f[:, :HALF] + 1.0, (8, HALF)).astype(jnp.bfloat16),
                hit,
                preferred_element_type=jnp.float32,
            )[0:1]
            - 1.0
        )
    pair_key = jnp.where(pair_element > 0.0, table_row * 256.0 + pair_element - 1.0, -3.0)
    notes = (
        [chunks[c][2] for c in range(3)]
        + [chunks[c][1] - 1.0 for c in range(3)]
        + keys
        + [pair_key, lane_f, lane_f + float(LANES)]
        + [pair_side - 1.0]
        + home
        + [jnp.zeros((1, LANES), jnp.float32)]
    )
    note_ref[...] = jnp.concatenate(notes, axis=0)

    row = lax.broadcasted_iota(jnp.int32, (8, LANES), 0)
    side = jnp.broadcast_to(side_row, (8, LANES))
    own_here = jnp.broadcast_to(own_node.astype(jnp.int32), (8, LANES))
    zero = jnp.zeros((8, LANES), jnp.float32)
    for q in range(OTHERS + 1):
        node_q = jnp.broadcast_to(wanted[q], (8, LANES)).astype(jnp.int32)
        code_ref[q] = jnp.where((node_q >= 0) & (node_q // 25 == row), node_q % 25, -1)
    for bc in range(25):
        set_tile(z_ref, jnp.where(own_here == 25 * row + bc, jnp.where(row < 5, 1.0, 0.0), 0.0), bc)
        set_tile(hc_ref, zero, bc)
        set_tile(hz_ref, zero, bc)
        set_tile(state_ref, zero, bc, 0, 2)
    for n in range(STEPS):
        seen_ref[n] = zero
    for bc in range(25, 40):
        set_tile(z_ref, zero, bc)
        set_tile(y_ref, zero, bc, 0, 2)
        set_tile(y_ref, zero, bc, 1, 2)

    is_box = where_ref[0] == 0

    def note_free(moment, drive):
        extra = partner_faces(y_ref, face_ref, side, 0, 2)
        code = code_ref[0]
        seen = zero
        for bc in range(25):
            assembled = tile_of(y_ref, bc, 0, 2) + extra[bc]
            x = tile_of(state_ref, bc, 0, 2)
            h = tile_of(hc_ref, bc)
            seen = seen + jnp.where(code == bc, jnp.where(is_box, assembled, x - h), 0.0)
            if drive is not None:
                kept = tile_of(keep_ref, bc) * x
                pushed = drive * tile_of(force_ref, bc)
                set_tile(
                    state_ref, kept - h + pushed - tile_of(inverse_ref, bc) * assembled, bc, 0, 2
                )
                set_tile(hc_ref, kept - x, bc)
        seen_ref[moment, 7:8] = jnp.sum(seen, axis=0, keepdims=True)

    def step(moment, begin):
        extra = partner_faces(z_ref, face_ref, side)
        for bc in range(25):
            set_tile(state_ref, tile_of(z_ref, bc) + extra[bc], bc, 1, 2)
        stiffness_tiles(state_ref, lambda bc, g: tile_of(scale_ref, bc), y_ref, grad_ref, 2)
        codes = [code_ref[q] for q in range(OTHERS + 1)]
        seen = [zero] * (OTHERS + 1)
        for bc in range(25):
            x = tile_of(z_ref, bc)
            pushed = tile_of(inverse_ref, bc) * tile_of(y_ref, bc, 1, 2)
            if begin:
                at_once = tile_of(inverse_ref, bc) * x
                adjoint = jnp.where(is_box, pushed, at_once)
                set_tile(hz_ref, jnp.where(is_box, 0.0, at_once), bc)
            else:
                kept = tile_of(keep_ref, bc) * x
                adjoint = kept - tile_of(hz_ref, bc) - pushed
                set_tile(hz_ref, kept - x, bc)
            set_tile(z_ref, adjoint, bc)
            for q in range(OTHERS + 1):
                seen[q] = seen[q] + jnp.where(codes[q] == bc, adjoint, 0.0)
        for q in range(OTHERS + 1):
            seen_ref[moment, q : q + 1] = jnp.sum(seen[q], axis=0, keepdims=True)

    def free_and_adjoint(moment, _):
        note_free(moment, coef_ref[0, moment])
        step(moment, False)
        return 0

    for bc in range(25):
        set_tile(state_ref, coef_ref[0, 0] * tile_of(force_ref, bc), bc, 0, 2)
    step(0, True)
    lax.fori_loop(1, STEPS - 1, free_and_adjoint, 0)
    note_free(STEPS - 1, None)
    seen = []
    extras = []
    for n in range(STEPS):
        rows = seen_ref[n]
        rows = rows + pltpu.roll(rows, HALF, 1)
        seen.append(rows)
        extras.append(jnp.where(used, gather_packed(rows, entry_at)[0:1], 0.0))
    for k in range(FREE_ROWS):
        out_ref[0, :, k * LANES : (k + 1) * LANES] = jnp.where(lane_low, seen[2 * k][7:8], seen[2 * k + 1][7:8])
    for k in range(PAIRS):
        r = GAIN_ROW + k
        out_ref[0, :, r * LANES : (r + 1) * LANES] = jnp.where(lane_low, seen[2 * k][0:1], seen[2 * k + 1][0:1])
        r = EXTRA_ROW + k
        out_ref[0, :, r * LANES : (r + 1) * LANES] = jnp.where(lane_low, extras[2 * k], extras[2 * k + 1])
    starts = jnp.where(lane == HALF, jnp.where(too_long, 1.0, 0.0), pltpu.roll(start, HALF, 1))
    out_ref[0, :, INDEX_ROW * LANES : PAYLOAD * LANES] = jnp.where(lane_low, entry_gid, starts)
    for k in range(1, out_ref.shape[0]):
        out_ref[k] = out_ref[0]


def final_kernel(
    where_ref,
    time_ref,
    mine_ref,
    other_ref,
    own_scale_ref,
    own_inverse_ref,
    own_force_ref,
    own_keep_ref,
    pair_ref,
    note_ref,
    now_ref,
    before_ref,
    both_ref,
    spread_ref,
    input_ref,
    scale_ref,
    inverse_ref,
    force_ref,
    keep_ref,
    x_ref,
    old_ref,
    h_ref,
    y_ref,
    grad_ref,
    face_ref,
    kick_ref,
    node_ref,
):
    is_box = where_ref[0] == 0
    parity = where_ref[1] % 2
    for core, source in ((parity, mine_ref), (1 - parity, other_ref)):
        for s in range(2):
            for r in range(PAYLOAD):
                both_ref[core, s, r] = source[8 * s : 8 * s + 8, 0, r * LANES : (r + 1) * LANES]
    low = lax.broadcasted_iota(jnp.int32, (8, LANES), 1) < HALF

    def rows(section, core, r):
        return both_ref[core, section, r]

    row = lax.broadcasted_iota(jnp.int32, (8, LANES), 0)
    point = lax.broadcasted_iota(jnp.int32, (8, LANES), 1) % HALF
    index = {}
    for s in range(2):
        for p in range(2):
            pair = rows(s, p, INDEX_ROW).astype(jnp.int32)
            turned = pltpu.roll(pair, HALF, 1)
            start = jnp.where(point == 0, 0, jnp.where(low, turned, pair))
            stop = jnp.where(point == HALF - 1, HALF, pltpu.roll(start, LANES - 1, 1))
            own = point // CAPC * HALF + (2 * row + p) * CAPC + point % CAPC
            index[s, p] = (own, jnp.where(low, pair, turned), start, stop)
    note = note_ref[...]
    at = jnp.where(row < 3, note[0:8], 0.0).astype(jnp.int32)
    packed = {}
    pairs = {}
    last = {}
    zero = jnp.zeros((8, LANES), jnp.float32)
    for n in range(1, STEPS):
        value = {}
        for s in range(2):
            for p in range(2):
                free = rows(s, p, n // 2)
                total = jnp.where(low, free, 0.0) if n % 2 == 0 else jnp.where(low, 0.0, free)
                more = zero
                for k in range(PAIRS):
                    m = n - 2 * k - 1
                    if m >= 1:
                        total = total + rows(s, p, GAIN_ROW + k) * pairs[s, p, 0, m]
                        more = more + rows(s, p, EXTRA_ROW + k) * pairs[s, p, 1, m]
                total = total + pltpu.roll(total, HALF, 1)
                if n > 1:
                    more = more + pltpu.roll(more, HALF, 1)
                    _, _, start, stop = index[s, p]
                    for q in range(OTHERS):
                        got = jnp.take_along_axis(
                            more, jnp.minimum(start + q, HALF - 1), axis=1, mode="promise_in_bounds"
                        )
                        total = total + jnp.where(start + q < stop, got, 0.0)
                value[s, p] = total
        for s in range(2):
            packed[s] = jnp.where(low, value[s, 0], value[s, 1])
        packed[1] = PENALTY * packed[1]
        input_ref[n] = gather_packed(jnp.where(is_box, packed[1], packed[0]), at)
        if n < STEPS - 1:
            for s in range(2):
                for p in range(2):
                    for q in range(2):
                        got = gather_packed(packed[1 - s], index[s, p][q])
                        pairs[s, p, q, n] = jnp.where(low, got, last.get((s, p, q), zero))
                        last[s, p, q] = got
    for c in range(3):
        point_key = across(note[6 + c : 7 + c])
        for g in range(3):
            matrix = one_hot(point_key == note[9 + g : 10 + g])
            spread_ref[c * LANES : (c + 1) * LANES, g * LANES : (g + 1) * LANES] = matrix
            spread_ref[(c + 3) * LANES : (c + 4) * LANES, g * LANES : (g + 1) * LANES] = matrix
    side = jnp.broadcast_to(note[12:13].astype(jnp.int32), (8, LANES))
    kick_ref[...] = jnp.zeros(kick_ref.shape, jnp.float32)
    for k, out in enumerate((scale_ref, inverse_ref, force_ref, keep_ref)):
        kick_ref[0:NODES] = pair_ref[k][:NODES]
        load_tiles(kick_ref, out)
    fold_tiles(inverse_ref, force_ref, keep_ref, 25)

    def choose(linked_ref, own_ref):
        return lambda bc, g: tile_of(linked_ref, bc) if g == 0 else tile_of(own_ref, bc, g - 1, 2)

    scale_of = choose(scale_ref, own_scale_ref)
    inverse_of = choose(inverse_ref, own_inverse_ref)
    force_of = choose(force_ref, own_force_ref)
    keep_of = choose(keep_ref, own_keep_ref)
    for g in range(3):
        for bc in range(25, 40):
            set_tile(y_ref, zero, bc, g, 3)
        for bc in range(25):
            set_tile(x_ref, time_ref[0, 0] * force_of(bc, g), bc, g, 3)
            set_tile(h_ref, zero, bc, g, 3)
    node_row = lax.broadcasted_iota(jnp.int32, (LANES, LANES), 0)
    point_node = note[3:6].astype(jnp.int32)
    for c in range(3):
        node_ref[:, c * LANES : (c + 1) * LANES] = one_hot(node_row == point_node[c : c + 1])

    def step(moment, _):
        drive = time_ref[0, moment]
        stiffness_tiles(x_ref, scale_of, y_ref, grad_ref, 3)
        inputs = input_ref[moment]
        high = inputs.astype(jnp.bfloat16)
        rest = (inputs - high.astype(jnp.float32)).astype(jnp.bfloat16)
        parts = [
            node_ref[:, c * LANES : (c + 1) * LANES] * part[c : c + 1]
            for part in (high, rest)
            for c in range(3)
        ]
        kick = jnp.dot(
            jnp.concatenate(parts, axis=1), spread_ref[...], preferred_element_type=jnp.float32
        )
        for g in range(3):
            kick_ref[200 * g : 200 * g + LANES] = kick[:, g * LANES : (g + 1) * LANES]
        extra = partner_faces(y_ref, face_ref, side, 0, 3)
        for g in range(3):
            for bc in range(25):
                net = kick_ref[pl.ds(200 * g + bc, 8, stride=25), :] - tile_of(y_ref, bc, g, 3)
                if g == 0:
                    net = net - extra[bc]
                x = tile_of(x_ref, bc, g, 3)
                kept = keep_of(bc, g) * x
                pushed = drive * force_of(bc, g)
                advanced = kept - tile_of(h_ref, bc, g, 3) + pushed
                set_tile(x_ref, advanced + inverse_of(bc, g) * net, bc, g, 3)
                set_tile(h_ref, kept - x, bc, g, 3)
                set_tile(old_ref, x, bc, g, 3)
        return 0

    lax.fori_loop(1, STEPS, step, 0)
    home = jnp.concatenate([note[13:14], note[14:15]], axis=1).astype(jnp.int32)
    linked = jnp.where(
        home == lax.broadcasted_iota(jnp.int32, (LANES, 2 * LANES), 0), 1.0, 0.0
    ).astype(jnp.bfloat16)
    alone = home < 0

    for tiles_ref, out_ref in ((old_ref, before_ref), (x_ref, now_ref)):
        for g in range(3):
            for bc in range(25):
                kick_ref[pl.ds(200 * g + bc, 8, stride=25), :] = tile_of(tiles_ref, bc, g, 3)
        moved = exact_pick(kick_ref[0:LANES], linked)
        for g in range(2):
            own = kick_ref[200 * (g + 1) : 200 * (g + 1) + LANES]
            cut = slice(g * LANES, (g + 1) * LANES)
            out_ref[:, 0, cut] = jnp.where(alone[:, cut], own, moved[:, cut])[:NODES]


def fast_body(wave_speed, inverse_mass, source_field, source_time, face_links, coupling_links):
    _, weight_np, _ = node_tables()
    weight = jnp.asarray(weight_np).reshape(NODES, 1)
    wave, mass, source = [
        jnp.transpose(field, (1, 0, 2)) for field in (wave_speed, inverse_mass, source_field)
    ]
    faces = jnp.transpose(face_links, (1, 0, 2))
    blocks = lax.axis_size("blk")
    columns = wave_speed.shape[-1]
    me = lax.axis_index("blk")
    place = jnp.stack([lax.axis_index("sec"), me]).astype(jnp.int32)
    vmem = pl.BlockSpec(memory_space=pltpu.VMEM)
    smem = pl.BlockSpec(memory_space=pltpu.SMEM)
    params = pltpu.CompilerParams(vmem_limit_bytes=16 << 20)

    def shape(*dims):
        return jax.ShapeDtypeStruct(dims, jnp.float32)

    links, m0, m1, m2, m3, count = pl.pallas_call(
        pack_kernel,
        out_shape=[shape(blocks, 8, LANES)] + [shape(16, 4 * LANES)] * 4 + [shape(LANES, columns)],
        in_specs=[smem] + [vmem] * 6,
        out_specs=[vmem] * 6,
        compiler_params=params,
    )(place, wave, mass, source, weight, faces, coupling_links)
    mine = [m0, m1, m2, m3]
    ghost = [partner_2(part, "blk", j) for j, part in enumerate(mine)]
    every = lax.all_to_all(links, "blk", 0, 0, tiled=True)

    def tiles(count):
        return pltpu.VMEM((8 * count, LANES), jnp.float32)

    table, copies, *own_tiles = pl.pallas_call(
        point_kernel,
        out_shape=[shape(16, LANES), shape(4, LANES, LANES)] + [shape(400, LANES)] * 4,
        in_specs=[smem] + [vmem] * 6,
        out_specs=[vmem] * 6,
        scratch_shapes=[tiles(50)],
        compiler_params=params,
    )(place, wave, mass, source, weight, count, every)
    payload, pair, note = pl.pallas_call(
        response_kernel,
        out_shape=[shape(blocks, 1, PAYLOAD * LANES), shape(4, LANES, LANES), shape(16, LANES)],
        in_specs=[smem] * 2 + [vmem] * 10,
        out_specs=[vmem] * 3,
        compiler_params=params,
        scratch_shapes=[tiles(25)] * 5
        + [tiles(50), tiles(40), tiles(25), tiles(25), tiles(80), tiles(50), tiles(5)]
        + [pltpu.VMEM((8, 8, LANES), jnp.int32), pltpu.VMEM((STEPS, 8, LANES), jnp.float32)],
    )(
        place,
        source_time,
        table,
        copies,
        *mine,
        *ghost,
    )

    same_core = [[c + 2 * i for i in range(blocks)] for c in range(2)]
    received = lax.all_to_all(
        payload, ("sec", "blk"), 0, 0, axis_index_groups=same_core, tiled=True
    )
    sibling = partner_2(received, "blk", 0)
    flag = INDEX_ROW * LANES + HALF
    overflow = jnp.max(
        jnp.maximum(received[:, 0, flag], sibling[:, 0, flag])
    ) > 0

    def quick(_):
        return tuple(
            pl.pallas_call(
                final_kernel,
                out_shape=[shape(NODES, 1, columns)] * 2,
                in_specs=[smem] * 2 + [vmem] * 8,
                out_specs=[vmem] * 2,
                compiler_params=params,
                scratch_shapes=[
                    pltpu.VMEM((2, 2, PAYLOAD, 8, LANES), jnp.float32),
                    pltpu.VMEM((6 * LANES, 3 * LANES), jnp.bfloat16),
                    pltpu.VMEM((STEPS, 8, LANES), jnp.float32),
                ]
                + [tiles(25)] * 4
                + [tiles(75)] * 3
                + [tiles(120), tiles(75), tiles(5), tiles(75)]
                + [pltpu.VMEM((LANES, 3 * LANES), jnp.bfloat16)],
            )(
                place,
                source_time,
                received,
                sibling,
                *own_tiles,
                pair,
                note,
            )
        )

    def slow(_):
        results = general_body(
            wave_speed, inverse_mass, source_field, source_time, face_links, coupling_links
        )
        return tuple(jnp.transpose(field, (1, 0, 2)) for field in results)

    now, before = lax.cond(overflow, slow, quick, 0)
    return (jnp.transpose(now, (1, 0, 2)), jnp.transpose(before, (1, 0, 2)))


def body(*arguments):
    wave_speed, _, _, _, face_links, coupling_links = arguments
    fits = (
        lax.axis_size("blk") == 16
        and lax.axis_size("sec") == 2
        and wave_speed.shape[1:] == (NODES, 2 * LANES)
        and face_links.shape[-1] == LANES
        and coupling_links.shape[-1] >= CAPC * 16
    )
    return fast_body(*arguments) if fits else general_body(*arguments)


def solution(mesh):
    in_specs = (
        P("sec", None, "blk"),
        P("sec", None, "blk"),
        P("sec", None, "blk"),
        P("sec", None),
        P("sec", None, "blk"),
        P(None, "blk"),
    )
    out_specs = (P("sec", None, "blk"), P("sec", None, "blk"))
    return jax.shard_map(body, mesh=mesh, in_specs=in_specs, out_specs=out_specs, check_vma=False)
```

```python
import jax
import jax.numpy as jnp
import numpy as np
from jax import lax
from jax.experimental import pallas as pl
from jax.experimental.pallas import tpu as pltpu
from jax.sharding import PartitionSpec as P

CAPC = 4
STEPS = 12


DT_SQUARED = 0.05
PENALTY = 10.0


def partner_2(value, axis, stride):
    return lax.ppermute(value, axis, [(i, i ^ 1 << stride) for i in range(lax.axis_size(axis))])


def node_tables():
    abscissae = np.array([-1.0, -np.sqrt(3.0 / 7.0), 0.0, np.sqrt(3.0 / 7.0), 1.0])
    weights = np.array([0.1, 49.0 / 90.0, 32.0 / 45.0, 49.0 / 90.0, 0.1])
    legendre = (35.0 * abscissae**4 - 30.0 * abscissae**2 + 3.0) / 8.0
    derivative = np.zeros((5, 5))
    for i in range(5):
        for j in range(5):
            if i != j:
                derivative[i, j] = legendre[i] / (legendre[j] * (abscissae[i] - abscissae[j]))
    derivative[0, 0] = -2.5
    derivative[4, 4] = 2.5
    identity = np.eye(5)
    operator = np.concatenate(
        [
            np.kron(np.kron(derivative, identity), identity),
            np.kron(np.kron(identity, derivative), identity),
            np.kron(np.kron(identity, identity), derivative),
        ],
        axis=0,
    )
    weight_cube = weights[:, None, None] * weights[None, :, None] * weights[None, None, :]
    lattice = np.arange(125).reshape(5, 5, 5)
    face_nodes = np.stack(
        [
            lattice[0].ravel(),
            lattice[4].ravel(),
            lattice[:, 0].ravel(),
            lattice[:, 4].ravel(),
            lattice[:, :, 0].ravel(),
            lattice[:, :, 4].ravel(),
        ]
    )
    return (
        operator.astype(np.float32),
        weight_cube.reshape(125, 1).astype(np.float32),
        face_nodes.astype(np.int32),
    )


def stiffness(field_in, speed_sq, operator, weight_cube):
    columns = field_in.shape[-1]
    scaling = weight_cube * speed_sq
    grads = jnp.dot(
        operator, field_in, precision=lax.Precision.HIGHEST, preferred_element_type=jnp.float32
    )
    scaled = (grads.reshape(3, 125, columns) * scaling[None]).reshape(375, columns)
    return jnp.dot(
        operator.T, scaled, precision=lax.Precision.HIGHEST, preferred_element_type=jnp.float32
    )


def general_body(wave_speed, inverse_mass, source_field, source_time, face_links, coupling_links):
    operator_np, weight_np, faces_np = node_tables()
    operator = jnp.asarray(operator_np)
    weight_cube = jnp.asarray(weight_np)
    picker_np = np.zeros((150, 125), np.float32)
    for side_number in range(6):
        for node_number in range(25):
            picker_np[side_number * 25 + node_number, faces_np[side_number, node_number]] = 1.0
    picker = jnp.asarray(picker_np)
    spreader = jnp.asarray(picker_np.T.copy())
    speed_sq = wave_speed[0]
    inverse = inverse_mass[0]
    forcing = source_field[0]
    timing = source_time[0]
    element = face_links[0, 0]
    face_side = face_links[0, 1]
    face_peer = face_links[0, 2]
    blocks = lax.axis_size("blk")
    bit_count = blocks.bit_length() - 1
    myself = lax.axis_index("blk")
    is_box = lax.axis_index("sec") == 0
    records = element.shape[0]
    per_peer = records // 8
    ordinal = jnp.arange(records)
    linked = face_peer != myself
    side_mask = face_side[None, None, :] == jnp.arange(6, dtype=jnp.int32)[:, None, None]
    earlier = ordinal[None, :] < ordinal[:, None]
    face_slot = jnp.sum(
        ((face_peer[:, None] == face_peer[None, :]) & earlier).astype(jnp.int32), axis=1
    )
    offset_bits = jnp.bitwise_xor(face_peer, myself)
    bit_index = jnp.zeros((records,), jnp.int32)
    for bit_number in range(bit_count):
        bit_index = bit_index + bit_number * (offset_bits == 1 << bit_number).astype(jnp.int32)
    pair_column = jnp.where(linked, bit_index * per_peer + face_slot, 0)
    point_element = coupling_links[0]
    point_node = coupling_links[1]
    point_owner = coupling_links[2]
    target_element = coupling_links[3]
    target_node = coupling_links[4]
    in_use = point_owner >= 0
    owner_safe = jnp.maximum(point_owner, 0)
    point_ordinal = jnp.arange(point_owner.shape[0])
    point_earlier = point_ordinal[None, :] < point_ordinal[:, None]
    point_slot = jnp.sum(
        ((point_owner[:, None] == point_owner[None, :]) & point_earlier).astype(jnp.int32), axis=1
    )
    point_column = jnp.where(in_use, point_slot * blocks + owner_safe, 0)
    slot_total = CAPC * blocks
    outbound = jnp.zeros((3, slot_total), jnp.int32)
    outbound = outbound.at[0, point_column].add(jnp.where(in_use, target_element, 0))
    outbound = outbound.at[1, point_column].add(jnp.where(in_use, target_node, 0))
    outbound = outbound.at[2, point_column].add(in_use.astype(jnp.int32))
    inbound = lax.all_to_all(
        outbound.reshape(3, CAPC, blocks), "blk", split_axis=2, concat_axis=2, tiled=True
    ).reshape(3, slot_total)
    remote_element = inbound[0]
    remote_node = inbound[1]
    remote_flag = inbound[2].astype(jnp.float32)
    target_rows = jnp.concatenate([point_node, remote_node])
    target_cols = jnp.concatenate([point_element, remote_element])
    current = jnp.zeros(speed_sq.shape, jnp.float32)
    previous = jnp.zeros(speed_sq.shape, jnp.float32)
    def one_step(moment, state):
        current, previous = state
        internal = stiffness(current, speed_sq, operator, weight_cube)
        stacked = jnp.dot(
            picker,
            internal[:, element],
            precision=lax.Precision.HIGHEST,
            preferred_element_type=jnp.float32,
        ).reshape(6, 25, records)
        payload = jnp.sum(jnp.where(side_mask, stacked, 0.0), axis=0)
        payload = jnp.where(linked[None, :], payload, 0.0)
        outgoing = (
            jnp.zeros((25, bit_count * per_peer), jnp.float32).at[:, pair_column].add(payload)
        )
        arrived = []
        for bit_number in range(bit_count):
            piece = outgoing[:, bit_number * per_peer : (bit_number + 1) * per_peer]
            arrived.append(partner_2(piece, "blk", bit_number))
        partner = jnp.concatenate(arrived, axis=1)[:, pair_column]
        partner = jnp.where(linked[None, :], partner, 0.0)
        masked = jnp.where(side_mask, partner[None], 0.0).reshape(150, records)
        assembled = internal.at[:, element].add(
            jnp.dot(
                spreader,
                masked,
                precision=lax.Precision.HIGHEST,
                preferred_element_type=jnp.float32,
            )
        )
        velocity = current - previous
        traction = assembled[point_node, point_element]
        box_send = (
            jnp.zeros((slot_total,), jnp.float32)
            .at[point_column]
            .add(jnp.where(in_use, traction, 0.0))
        )
        global_send = velocity[remote_node, remote_element] * remote_flag
        dispatch = jnp.where(is_box, box_send, global_send).reshape(CAPC, blocks)
        crossed = partner_2(dispatch, "sec", 0)
        received = lax.all_to_all(crossed, "blk", split_axis=1, concat_axis=1, tiled=True)
        received = received.reshape(slot_total)
        remote_velocity = received[point_column]
        box_terms = jnp.where(
            in_use, PENALTY * (remote_velocity - velocity[point_node, point_element]), 0.0
        )
        values = jnp.concatenate(
            [jnp.where(is_box, box_terms, 0.0), jnp.where(is_box, 0.0, received * remote_flag)]
        )
        driving = timing[moment] * forcing - assembled
        driving = driving.at[target_rows, target_cols].add(values)
        advanced = 2.0 * current - previous + DT_SQUARED * inverse * driving
        return advanced, current

    current, previous = lax.fori_loop(0, STEPS, one_step, (current, previous))
    return (current[None], previous[None])


LANES = 128
HALF = 64
OTHERS = 5
LAGS = 10
PAIRS = LAGS // 2
FREE_ROWS = STEPS // 2
GAIN_ROW = FREE_ROWS
EXTRA_ROW = GAIN_ROW + PAIRS
INDEX_ROW = EXTRA_ROW + PAIRS
PAYLOAD = INDEX_ROW + 1
NODES = 125
EXACT = lax.Precision.HIGHEST


def line_matrix():
    abscissae = np.array([-1.0, -np.sqrt(3.0 / 7.0), 0.0, np.sqrt(3.0 / 7.0), 1.0])
    legendre = (35.0 * abscissae**4 - 30.0 * abscissae**2 + 3.0) / 8.0
    derivative = np.zeros((5, 5))
    for i in range(5):
        for j in range(5):
            if i != j:
                derivative[i, j] = legendre[i] / (legendre[j] * (abscissae[i] - abscissae[j]))
    derivative[0, 0] = -2.5
    derivative[4, 4] = 2.5
    return derivative


def apply_line(matrix, x):
    odd = [x[0] - x[4], x[1] - x[3]]
    even = [x[0] + x[4], x[1] + x[3]]
    out = [None] * 5
    for i in range(2):
        symmetric = (
            float(0.5 * (matrix[i, 0] - matrix[i, 4])) * odd[0]
            + float(0.5 * (matrix[i, 1] - matrix[i, 3])) * odd[1]
        )
        skew = (
            float(0.5 * (matrix[i, 0] + matrix[i, 4])) * even[0]
            + float(0.5 * (matrix[i, 1] + matrix[i, 3])) * even[1]
            + float(matrix[i, 2]) * x[2]
        )
        out[i] = symmetric + skew
        out[4 - i] = symmetric - skew
    out[2] = float(matrix[2, 0]) * odd[0] + float(matrix[2, 1]) * odd[1]
    return out


def line_tiles():
    row = lax.broadcasted_iota(jnp.int32, (8, LANES), 0)
    tiles = []
    for matrix in (line_matrix(), line_matrix().T):
        columns = []
        for j in range(5):
            tile = jnp.zeros((8, LANES), jnp.float32)
            for i in range(5):
                tile = jnp.where(row == i, float(matrix[i, j]), tile)
            columns.append(tile)
        tiles.append(columns)
    return tiles


def tile_of(ref, bc, group=0, groups=1):
    start = (bc * groups + group) * 8
    return ref[start : start + 8, :]


def set_tile(ref, value, bc, group=0, groups=1):
    start = (bc * groups + group) * 8
    ref[start : start + 8, :] = value


def repeat_row(ref, row):
    return jnp.broadcast_to(ref[row : row + 1, :], (8, LANES))


def stiffness_tiles(x_ref, scale_of, y_ref, grad_ref, groups):
    forward = line_matrix()
    backward = forward.T.copy()
    to_grad, to_node = line_tiles()

    for g in range(groups):

        def scale(bc):
            return scale_of(bc, g)

        def along(index):
            grads = apply_line(forward, [tile_of(x_ref, k, g, groups) for k in index])
            return apply_line(backward, [v * scale(k) for v, k in zip(grads, index)])

        for bc in range(25):
            start = (bc * groups + g) * 8
            total = to_grad[0] * repeat_row(x_ref, start)
            for j in range(1, 5):
                total = total + to_grad[j] * repeat_row(x_ref, start + j)
            grad_ref[start : start + 8, :] = total * scale(bc)
        total = [None] * 25
        for c in range(5):
            index = [5 * j + c for j in range(5)]
            for k, value in zip(index, along(index)):
                total[k] = value
        for b in range(5):
            index = [5 * b + j for j in range(5)]
            for k, value in zip(index, along(index)):
                total[k] = total[k] + value
        for bc in range(25):
            start = (bc * groups + g) * 8
            value = total[bc]
            for j in range(5):
                value = value + to_node[j] * repeat_row(grad_ref, start + j)
            set_tile(y_ref, value, bc, g, groups)


def partner_faces(ref, face_ref, side, group=0, groups=1):
    row = lax.broadcasted_iota(jnp.int32, (8, LANES), 0)
    is_side = [side == q for q in range(6)]
    on_a = (is_side[0] & (row == 0)) | (is_side[1] & (row == 4))
    arrived = []
    for t in range(5):
        first = ref[pl.ds((t * groups + group) * 8, 8, stride=40 * groups), :]
        last = ref[pl.ds((t * groups + group) * 8 + 4, 8, stride=40 * groups), :]
        value = jnp.where(is_side[1], last, first)
        value = jnp.where(is_side[2], tile_of(ref, t, group, groups), value)
        value = jnp.where(is_side[3], tile_of(ref, 20 + t, group, groups), value)
        value = jnp.where(is_side[4], tile_of(ref, 5 * t, group, groups), value)
        value = jnp.where(is_side[5], tile_of(ref, 5 * t + 4, group, groups), value)
        value = pltpu.roll(value, HALF, 1)
        arrived.append(value)
        set_tile(face_ref, value, t)
    extra = []
    for b in range(5):
        for c in range(5):
            value = jnp.where(on_a, repeat_row(face_ref, 8 * c + b), 0.0)
            if b == 0:
                value = jnp.where(is_side[2], arrived[c], value)
            if b == 4:
                value = jnp.where(is_side[3], arrived[c], value)
            if c == 0:
                value = jnp.where(is_side[4], arrived[b], value)
            if c == 4:
                value = jnp.where(is_side[5], arrived[b], value)
            extra.append(value)
    return extra


def load_tiles(flat_ref, out_ref, group=0, groups=1, start=0):
    for bc in range(25):
        set_tile(out_ref, flat_ref[pl.ds(start + bc, 8, stride=25), :], bc, group, groups)


def fold_tiles(inverse_ref, force_ref, keep_ref, count):
    for k in range(count):
        inverse = tile_of(inverse_ref, k)
        set_tile(force_ref, inverse * tile_of(force_ref, k), k)
        set_tile(keep_ref, 2.0 - inverse * (PENALTY * tile_of(keep_ref, k)), k)


def across(row_values):
    return jnp.broadcast_to(row_values, (LANES, LANES)).T


def rank_among(row_values):
    down = lax.broadcasted_iota(jnp.int32, (LANES, LANES), 0)
    right = lax.broadcasted_iota(jnp.int32, (LANES, LANES), 1)
    same = (across(row_values) == row_values) & (down < right)
    return jnp.sum(jnp.where(same, 1.0, 0.0), axis=0, keepdims=True)


def one_hot(condition):
    return jnp.where(condition, 1.0, 0.0).astype(jnp.bfloat16)


def plain_dot(a, b):
    return jnp.dot(a.astype(jnp.bfloat16), b, preferred_element_type=jnp.float32)


def exact_pick(values, chosen, transposed=False):
    total = None
    rest = values
    for _ in range(3):
        part = rest.astype(jnp.bfloat16)
        if transposed:
            got = lax.dot_general(
                chosen, part, (((1,), (1,)), ((), ())), preferred_element_type=jnp.float32
            )
        else:
            got = jnp.dot(part, chosen, preferred_element_type=jnp.float32)
        total = got if total is None else total + got
        rest = rest - part.astype(jnp.float32)
    return total


def lane_row():
    return lax.broadcasted_iota(jnp.int32, (1, LANES), 1)


def pack_kernel(
    where_ref,
    amplitude_ref,
    wave_ref,
    mass_ref,
    source_ref,
    weight_ref,
    face_ref,
    couple_ref,
    links_ref,
    m0_ref,
    m1_ref,
    m2_ref,
    m3_ref,
    count_ref,
    time_ref,
):
    for k in range(STEPS):
        time_ref[0, k] = amplitude_ref[0, k]
    me = where_ref[1]
    me_f = me.astype(jnp.float32)
    is_box = where_ref[0] == 0
    down = lax.broadcasted_iota(jnp.int32, (LANES, LANES), 0)
    right = lax.broadcasted_iota(jnp.int32, (LANES, LANES), 1)
    right_f = right.astype(jnp.float32)
    lane = lane_row()

    live = couple_ref[:, 0:LANES].astype(jnp.float32)
    owner = jnp.where(lane < HALF, live[2:3], -1.0)
    slot = jnp.where(owner >= 0.0, owner * CAPC + rank_among(owner), -1.0)
    to_slot = one_hot(across(slot) == right_f)
    named = jnp.concatenate([live[0:2], live[3:5], jnp.full((4, LANES), -1.0)], axis=0) + 1.0
    links = plain_dot(named, to_slot)
    for k in range(links_ref.shape[0]):
        links_ref[k] = links

    faces = face_ref[:, 0, :]
    peer = faces[2:3]
    linked = peer != me
    distance = peer ^ me
    bit = jnp.zeros((1, LANES), jnp.float32)
    for j in range(1, 4):
        bit = bit + jnp.where(distance == 1 << j, float(j), 0.0)
    face_slot = jnp.where(linked, bit * 16.0 + rank_among(peer.astype(jnp.float32)), -1.0)
    to_record = one_hot(across(face_slot) == right_f)
    facts = jnp.concatenate([faces[0:2].astype(jnp.float32) + 1.0, jnp.zeros((6, LANES))], axis=0)
    record = plain_dot(facts, to_record)

    node_one = lax.broadcasted_iota(jnp.int32, (LANES, LANES), 0).astype(jnp.float32) + 1.0
    own_nodes = one_hot(node_one == links[1:2])
    point_column = across(links[0:1])
    record_column = across(record[0:1])
    side_column = across(record[1:2])
    counts = []
    taken = []
    for g in range(2):
        column_one = right_f + float(g * LANES + 1)
        counts.append(
            jnp.dot(own_nodes, one_hot(point_column == column_one), preferred_element_type=jnp.float32)
        )
        taken.append(one_hot(record_column == column_one)[:HALF])
    count = jnp.concatenate(counts, axis=1) * jnp.where(is_box, 1.0, 0.0)
    count_ref[...] = count
    take = jnp.concatenate(taken, axis=1)
    pad = jnp.zeros((LANES - NODES, 2 * LANES), jnp.float32)
    stiff = jnp.concatenate([weight_ref[...] * wave_ref[:, 0, :], pad], axis=0)
    mass = jnp.concatenate([DT_SQUARED * mass_ref[:, 0, :], pad], axis=0)
    source = jnp.concatenate([source_ref[:, 0, :], pad], axis=0)
    first = exact_pick(stiff, take, True)
    first = jnp.where(right[:HALF] == 125, record_column[:HALF], first)
    first = jnp.where(right[:HALF] == 126, side_column[:HALF], first)
    parts = [
        first,
        exact_pick(mass, take, True),
        exact_pick(source, take, True),
        lax.dot_general(
            take,
            count.astype(jnp.bfloat16),
            (((1,), (1,)), ((), ())),
            preferred_element_type=jnp.float32,
        ),
    ]
    for j, out in enumerate((m0_ref, m1_ref, m2_ref, m3_ref)):
        for k in range(4):
            out[:, k * LANES : (k + 1) * LANES] = parts[k][16 * j : 16 * j + 16]


def point_tables(where_ref, every_ref):
    me = where_ref[1]
    is_box = where_ref[0] == 0
    lane = lane_row()
    low = lane < HALF
    blocks = every_ref.shape[0]
    down = lax.broadcasted_iota(jnp.int32, (blocks, LANES), 0)
    right = lax.broadcasted_iota(jnp.int32, (blocks, LANES), 1)
    mine = right // CAPC == down
    tables = []
    for offset in (0, 1, 2, 4, 8):
        beta = me ^ offset
        at = beta * CAPC + right % CAPC
        rows = []
        for f in range(2):
            direct = every_ref[beta, f : f + 1, :]
            column = every_ref[:, 2 + f, :]
            picked = jnp.concatenate(
                [
                    jnp.take_along_axis(column[8 * h : 8 * h + 8], at[8 * h : 8 * h + 8], axis=1,
                                        mode="promise_in_bounds")
                    for h in range(blocks // 8)
                ],
                axis=0,
            )
            turned = jnp.sum(jnp.where(mine, picked, 0.0), axis=0, keepdims=True)
            row = jnp.where(is_box, direct, turned)
            rows.append(jnp.where(low, row, 0.0))
        inputs = lane // CAPC * HALF + beta * CAPC + lane % CAPC
        rows.append(jnp.where(low, inputs, 0).astype(jnp.float32))
        tables.append(rows)
    tables.append([jnp.zeros((1, LANES), jnp.float32)] * 3)
    chunks = []
    for c in range(3):
        chunks.append(
            [
                jnp.where(low, tables[2 * c][f], pltpu.roll(tables[2 * c + 1][f], HALF, 1))
                for f in range(3)
            ]
        )
    keys = []
    for c in range(3):
        table = jnp.where(low, float(2 * c), float(2 * c + 1))
        element, node, _ = chunks[c]
        keys.append(jnp.where(node > 0.0, table * 256.0 + element - 1.0, -1.0))
    return chunks, keys


def gather_packed(packed, at):
    rows = at // LANES
    lanes = at % LANES
    out = jnp.zeros(at.shape, jnp.float32)
    for k in range(8):
        source = jnp.broadcast_to(packed[k : k + 1], at.shape)
        picked = jnp.take_along_axis(source, lanes, axis=1, mode="promise_in_bounds")
        out = jnp.where(rows == k, picked, out)
    return out


def point_kernel(
    where_ref,
    wave_ref,
    mass_ref,
    source_ref,
    weight_ref,
    count_ref,
    every_ref,
    table_ref,
    copy_ref,
    scale_ref,
    inverse_ref,
    force_ref,
    keep_ref,
    flat_ref,
):
    chunks, keys = point_tables(where_ref, every_ref)
    rows = [chunks[c][f] for c in range(3) for f in range(3)] + keys
    table_ref[...] = jnp.concatenate(rows + [jnp.zeros((4, LANES), jnp.float32)], axis=0)
    down = lax.broadcasted_iota(jnp.int32, (LANES, LANES), 0)
    right = lax.broadcasted_iota(jnp.int32, (LANES, LANES), 1)
    element = chunks[0][0]
    element_both = jnp.where(lane_row() < HALF, element, pltpu.roll(element, HALF, 1))
    take = [
        one_hot((down.astype(jnp.float32) + float(g * LANES + 1) == element_both) & (right < HALF))
        for g in range(2)
    ]
    take = jnp.concatenate(take, axis=0)
    own_fields = [
        weight_ref[...] * wave_ref[:, 0, :],
        DT_SQUARED * mass_ref[:, 0, :],
        source_ref[:, 0, :],
        count_ref[...][:NODES],
    ]
    flat_ref[...] = jnp.zeros(flat_ref.shape, jnp.float32)
    copy_ref[...] = jnp.zeros(copy_ref.shape, jnp.float32)
    for k, out in enumerate((scale_ref, inverse_ref, force_ref, keep_ref)):
        pick = plain_dot if k == 3 else exact_pick
        copy_ref[k, 0:NODES] = pick(own_fields[k], take)
        for g in range(2):
            flat_ref[200 * g : 200 * g + NODES] = own_fields[k][:, g * LANES : (g + 1) * LANES]
            load_tiles(flat_ref, out, g, 2, 200 * g)
    fold_tiles(inverse_ref, force_ref, keep_ref, 50)


def response_kernel(
    where_ref,
    coef_ref,
    table_ref,
    copy_ref,
    m0_ref,
    m1_ref,
    m2_ref,
    m3_ref,
    g0_ref,
    g1_ref,
    g2_ref,
    g3_ref,
    out_ref,
    pair_ref,
    note_ref,
    flat_ref,
    scale_ref,
    inverse_ref,
    force_ref,
    keep_ref,
    state_ref,
    z_ref,
    hc_ref,
    hz_ref,
    y_ref,
    grad_ref,
    face_ref,
    code_ref,
    seen_ref,
):
    down = lax.broadcasted_iota(jnp.int32, (LANES, LANES), 0)
    right = lax.broadcasted_iota(jnp.int32, (LANES, LANES), 1)
    right_f = right.astype(jnp.float32)
    lane = lane_row()
    lane_low = lane < HALF
    lane_f = lane.astype(jnp.float32)

    stacked = jnp.concatenate(
        [r[...] for r in (m0_ref, m1_ref, m2_ref, m3_ref, g0_ref, g1_ref, g2_ref, g3_ref)], axis=0
    )
    pair = [stacked[:, k * LANES : (k + 1) * LANES].T for k in range(4)]
    for k in range(4):
        pair_ref[k] = pair[k]
    pair_element = pair[0][125:126]
    pair_side = pair[0][126:127]
    own_column = jnp.broadcast_to(stacked[:HALF, 125:126], (HALF, LANES))
    own_column = jnp.concatenate([own_column, own_column], axis=0)

    chunks = [[table_ref[3 * c + f : 3 * c + f + 1] for f in range(3)] for c in range(3)]
    keys = [table_ref[9 + c : 10 + c] for c in range(3)]
    element, node, _ = chunks[0]
    element_both = jnp.where(lane_low, element, pltpu.roll(element, HALF, 1))
    node_low = jnp.where(lane_low, node, 0.0)
    present = element_both > 0.0
    same_half = (down < HALF) == (right < HALF)
    of_record = (own_column == element_both) & present & same_half
    facts_matrix = one_hot(of_record)
    partner_matrix = one_hot(of_record & (down >= HALF))
    table_row = jnp.where(lane_low, 0.0, (1 + (lane - HALF) // 16).astype(jnp.float32))
    facts = plain_dot(
        jnp.concatenate([pair_side, pair_element, table_row, jnp.zeros((5, LANES))], axis=0),
        facts_matrix,
    )
    side_row = facts[0:1].astype(jnp.int32) - 1
    partner = pltpu.roll(facts, HALF, 1)
    ghost_key = jnp.where(partner[1:2] > 0.0, partner[2:3] * 256.0 + partner[1:2] - 1.0, -5.0)
    own_key = jnp.where(element > 0.0, element - 1.0, -5.0)
    own_key = jnp.where(lane_low, own_key, -5.0)
    ghost_key = jnp.where(lane_low, ghost_key, -5.0)

    match = [(across(keys[c]) == own_key) | (across(keys[c]) == ghost_key) for c in range(3)]
    match[0] = match[0] & (down != right)
    matched = [jnp.where(m, 1.0, 0.0) for m in match]
    lower = one_hot(right < down)
    before = jnp.zeros((1, LANES), jnp.float32)
    lists = [jnp.zeros((8, LANES), jnp.float32)] * OTHERS
    for c in range(3):
        place = jnp.dot(lower, matched[c].astype(jnp.bfloat16), preferred_element_type=jnp.float32)
        place = jnp.where(match[c], place + before, -1.0)
        before = before + jnp.sum(matched[c], axis=0, keepdims=True)
        _, node_c, gid_c = chunks[c]
        gid_high = jnp.floor(gid_c * (1.0 / 256.0))
        table_c = jnp.where(lane_low, float(2 * c), float(2 * c + 1))
        described = jnp.concatenate(
            [node_c, gid_high, gid_c - 256.0 * gid_high, table_c, jnp.zeros((4, LANES))], axis=0
        )
        for q in range(OTHERS):
            lists[q] = lists[q] + plain_dot(described, one_hot(place == float(q)))
    own_node = jnp.where(lane_low, node - 1.0, -1.0)
    wanted = [own_node]
    gids = [jnp.zeros((1, LANES), jnp.float32)]
    for q in range(OTHERS):
        node_q = lists[q][0:1] - 1.0
        there = lists[q][3:4] > 0.0
        gids.append(lists[q][1:2] * 256.0 + lists[q][2:3])
        wanted.append(
            jnp.where(
                lane_low,
                jnp.where(there, -1.0, node_q),
                pltpu.roll(jnp.where(there, node_q, -1.0), HALF, 1),
            )
        )
    gids.append(jnp.zeros((7 - OTHERS, LANES), jnp.float32))

    length = jnp.minimum(before, 200.0)
    start = plain_dot(jnp.broadcast_to(length, (8, LANES)), one_hot(down < right))[0:1]
    too_long = (jnp.max(before) > float(OTHERS)) | (jnp.max(start + length) > float(HALF))
    entry = right % HALF
    entry_f = entry.astype(jnp.float32)
    is_point = down < HALF
    owner_of = jnp.sum(
        jnp.where(is_point & (across(start + length) <= entry_f), 1.0, 0.0), axis=0, keepdims=True
    )
    begun = jnp.sum(
        jnp.where(down.astype(jnp.float32) == owner_of, across(start), 0.0), axis=0, keepdims=True
    )
    used = owner_of < float(HALF)
    which = jnp.clip(entry_f[0:1] - begun, 0.0, float(OTHERS - 1)) + 1.0
    entry_at = jnp.where(used, which * float(LANES) + owner_of, 0.0).astype(jnp.int32)
    entry_at = jnp.broadcast_to(entry_at, (8, LANES))
    entry_gid = jnp.where(used, gather_packed(jnp.concatenate(gids, axis=0), entry_at)[0:1], 0.0)

    flat_ref[...] = jnp.zeros(flat_ref.shape, jnp.float32)
    for k, out in enumerate((scale_ref, inverse_ref, force_ref, keep_ref)):
        pick = plain_dot if k == 3 else exact_pick
        flat_ref[0:NODES] = (copy_ref[k] + pick(pair[k], partner_matrix))[:NODES]
        load_tiles(flat_ref, out)
    fold_tiles(inverse_ref, force_ref, keep_ref, 25)

    home = []
    for g in range(2):
        hit = one_hot(own_column[:HALF] == right_f[:HALF] + float(g * LANES + 1))
        home.append(
            jnp.dot(
                jnp.broadcast_to(lane_f[:, :HALF] + 1.0, (8, HALF)).astype(jnp.bfloat16),
                hit,
                preferred_element_type=jnp.float32,
            )[0:1]
            - 1.0
        )
    pair_key = jnp.where(pair_element > 0.0, table_row * 256.0 + pair_element - 1.0, -3.0)
    notes = (
        [chunks[c][2] for c in range(3)]
        + [chunks[c][1] - 1.0 for c in range(3)]
        + keys
        + [pair_key, lane_f, lane_f + float(LANES)]
        + [pair_side - 1.0]
        + home
        + [jnp.zeros((1, LANES), jnp.float32)]
    )
    note_ref[...] = jnp.concatenate(notes, axis=0)

    row = lax.broadcasted_iota(jnp.int32, (8, LANES), 0)
    side = jnp.broadcast_to(side_row, (8, LANES))
    own_here = jnp.broadcast_to(own_node.astype(jnp.int32), (8, LANES))
    zero = jnp.zeros((8, LANES), jnp.float32)
    for q in range(OTHERS + 1):
        node_q = jnp.broadcast_to(wanted[q], (8, LANES)).astype(jnp.int32)
        code_ref[q] = jnp.where((node_q >= 0) & (node_q // 25 == row), node_q % 25, -1)
    for bc in range(25):
        set_tile(z_ref, jnp.where(own_here == 25 * row + bc, jnp.where(row < 5, 1.0, 0.0), 0.0), bc)
        set_tile(hc_ref, zero, bc)
        set_tile(hz_ref, zero, bc)
        set_tile(state_ref, zero, bc, 0, 2)
    for n in range(STEPS):
        seen_ref[n] = zero
    for bc in range(25, 40):
        set_tile(z_ref, zero, bc)
        set_tile(y_ref, zero, bc, 0, 2)
        set_tile(y_ref, zero, bc, 1, 2)

    is_box = where_ref[0] == 0

    def note_free(moment, drive):
        extra = partner_faces(y_ref, face_ref, side, 0, 2)
        code = code_ref[0]
        seen = zero
        for bc in range(25):
            assembled = tile_of(y_ref, bc, 0, 2) + extra[bc]
            x = tile_of(state_ref, bc, 0, 2)
            h = tile_of(hc_ref, bc)
            seen = seen + jnp.where(code == bc, jnp.where(is_box, assembled, x - h), 0.0)
            if drive is not None:
                kept = tile_of(keep_ref, bc) * x
                pushed = drive * tile_of(force_ref, bc)
                set_tile(
                    state_ref, kept - h + pushed - tile_of(inverse_ref, bc) * assembled, bc, 0, 2
                )
                set_tile(hc_ref, kept - x, bc)
        seen_ref[moment, 7:8] = jnp.sum(seen, axis=0, keepdims=True)

    def step(moment, begin):
        extra = partner_faces(z_ref, face_ref, side)
        for bc in range(25):
            set_tile(state_ref, tile_of(z_ref, bc) + extra[bc], bc, 1, 2)
        stiffness_tiles(state_ref, lambda bc, g: tile_of(scale_ref, bc), y_ref, grad_ref, 2)
        codes = [code_ref[q] for q in range(OTHERS + 1)]
        seen = [zero] * (OTHERS + 1)
        for bc in range(25):
            x = tile_of(z_ref, bc)
            pushed = tile_of(inverse_ref, bc) * tile_of(y_ref, bc, 1, 2)
            if begin:
                at_once = tile_of(inverse_ref, bc) * x
                adjoint = jnp.where(is_box, pushed, at_once)
                set_tile(hz_ref, jnp.where(is_box, 0.0, at_once), bc)
            else:
                kept = tile_of(keep_ref, bc) * x
                adjoint = kept - tile_of(hz_ref, bc) - pushed
                set_tile(hz_ref, kept - x, bc)
            set_tile(z_ref, adjoint, bc)
            for q in range(OTHERS + 1):
                seen[q] = seen[q] + jnp.where(codes[q] == bc, adjoint, 0.0)
        for q in range(OTHERS + 1):
            seen_ref[moment, q : q + 1] = jnp.sum(seen[q], axis=0, keepdims=True)

    def free_and_adjoint(moment, _):
        note_free(moment, coef_ref[0, moment])
        step(moment, False)
        return 0

    for bc in range(25):
        set_tile(state_ref, coef_ref[0, 0] * tile_of(force_ref, bc), bc, 0, 2)
    step(0, True)
    lax.fori_loop(1, STEPS - 1, free_and_adjoint, 0)
    note_free(STEPS - 1, None)
    seen = []
    extras = []
    for n in range(STEPS):
        rows = seen_ref[n]
        rows = rows + pltpu.roll(rows, HALF, 1)
        seen.append(rows)
        extras.append(jnp.where(used, gather_packed(rows, entry_at)[0:1], 0.0))
    for k in range(FREE_ROWS):
        out_ref[0, :, k * LANES : (k + 1) * LANES] = jnp.where(lane_low, seen[2 * k][7:8], seen[2 * k + 1][7:8])
    for k in range(PAIRS):
        r = GAIN_ROW + k
        out_ref[0, :, r * LANES : (r + 1) * LANES] = jnp.where(lane_low, seen[2 * k][0:1], seen[2 * k + 1][0:1])
        r = EXTRA_ROW + k
        out_ref[0, :, r * LANES : (r + 1) * LANES] = jnp.where(lane_low, extras[2 * k], extras[2 * k + 1])
    starts = jnp.where(lane == HALF, jnp.where(too_long, 1.0, 0.0), pltpu.roll(start, HALF, 1))
    out_ref[0, :, INDEX_ROW * LANES : PAYLOAD * LANES] = jnp.where(lane_low, entry_gid, starts)
    for k in range(1, out_ref.shape[0]):
        out_ref[k] = out_ref[0]


def final_kernel(
    where_ref,
    time_ref,
    mine_ref,
    other_ref,
    own_scale_ref,
    own_inverse_ref,
    own_force_ref,
    own_keep_ref,
    pair_ref,
    note_ref,
    now_ref,
    before_ref,
    both_ref,
    spread_ref,
    input_ref,
    scale_ref,
    inverse_ref,
    force_ref,
    keep_ref,
    x_ref,
    old_ref,
    h_ref,
    y_ref,
    grad_ref,
    face_ref,
    kick_ref,
    node_ref,
):
    is_box = where_ref[0] == 0
    parity = where_ref[1] % 2
    for core, source in ((parity, mine_ref), (1 - parity, other_ref)):
        for s in range(2):
            for r in range(PAYLOAD):
                both_ref[core, s, r] = source[8 * s : 8 * s + 8, 0, r * LANES : (r + 1) * LANES]
    low = lax.broadcasted_iota(jnp.int32, (8, LANES), 1) < HALF

    def rows(section, core, r):
        return both_ref[core, section, r]

    row = lax.broadcasted_iota(jnp.int32, (8, LANES), 0)
    point = lax.broadcasted_iota(jnp.int32, (8, LANES), 1) % HALF
    index = {}
    for s in range(2):
        for p in range(2):
            pair = rows(s, p, INDEX_ROW).astype(jnp.int32)
            turned = pltpu.roll(pair, HALF, 1)
            start = jnp.where(point == 0, 0, jnp.where(low, turned, pair))
            stop = jnp.where(point == HALF - 1, HALF, pltpu.roll(start, LANES - 1, 1))
            own = point // CAPC * HALF + (2 * row + p) * CAPC + point % CAPC
            index[s, p] = (own, jnp.where(low, pair, turned), start, stop)
    note = note_ref[...]
    at = jnp.where(row < 3, note[0:8], 0.0).astype(jnp.int32)
    packed = {}
    pairs = {}
    last = {}
    zero = jnp.zeros((8, LANES), jnp.float32)
    for n in range(1, STEPS):
        value = {}
        for s in range(2):
            for p in range(2):
                free = rows(s, p, n // 2)
                total = jnp.where(low, free, 0.0) if n % 2 == 0 else jnp.where(low, 0.0, free)
                more = zero
                for k in range(PAIRS):
                    m = n - 2 * k - 1
                    if m >= 1:
                        total = total + rows(s, p, GAIN_ROW + k) * pairs[s, p, 0, m]
                        more = more + rows(s, p, EXTRA_ROW + k) * pairs[s, p, 1, m]
                total = total + pltpu.roll(total, HALF, 1)
                if n > 1:
                    more = more + pltpu.roll(more, HALF, 1)
                    _, _, start, stop = index[s, p]
                    for q in range(OTHERS):
                        got = jnp.take_along_axis(
                            more, jnp.minimum(start + q, HALF - 1), axis=1, mode="promise_in_bounds"
                        )
                        total = total + jnp.where(start + q < stop, got, 0.0)
                value[s, p] = total
        for s in range(2):
            packed[s] = jnp.where(low, value[s, 0], value[s, 1])
        packed[1] = PENALTY * packed[1]
        input_ref[n] = gather_packed(jnp.where(is_box, packed[1], packed[0]), at)
        if n < STEPS - 1:
            for s in range(2):
                for p in range(2):
                    for q in range(2):
                        got = gather_packed(packed[1 - s], index[s, p][q])
                        pairs[s, p, q, n] = jnp.where(low, got, last.get((s, p, q), zero))
                        last[s, p, q] = got
    for c in range(3):
        point_key = across(note[6 + c : 7 + c])
        for g in range(3):
            matrix = one_hot(point_key == note[9 + g : 10 + g])
            spread_ref[c * LANES : (c + 1) * LANES, g * LANES : (g + 1) * LANES] = matrix
            spread_ref[(c + 3) * LANES : (c + 4) * LANES, g * LANES : (g + 1) * LANES] = matrix
    side = jnp.broadcast_to(note[12:13].astype(jnp.int32), (8, LANES))
    kick_ref[...] = jnp.zeros(kick_ref.shape, jnp.float32)
    for k, out in enumerate((scale_ref, inverse_ref, force_ref, keep_ref)):
        kick_ref[0:NODES] = pair_ref[k][:NODES]
        load_tiles(kick_ref, out)
    fold_tiles(inverse_ref, force_ref, keep_ref, 25)

    def choose(linked_ref, own_ref):
        return lambda bc, g: tile_of(linked_ref, bc) if g == 0 else tile_of(own_ref, bc, g - 1, 2)

    scale_of = choose(scale_ref, own_scale_ref)
    inverse_of = choose(inverse_ref, own_inverse_ref)
    force_of = choose(force_ref, own_force_ref)
    keep_of = choose(keep_ref, own_keep_ref)
    for g in range(3):
        for bc in range(25, 40):
            set_tile(y_ref, zero, bc, g, 3)
        for bc in range(25):
            set_tile(x_ref, time_ref[0, 0] * force_of(bc, g), bc, g, 3)
            set_tile(h_ref, zero, bc, g, 3)
    node_row = lax.broadcasted_iota(jnp.int32, (LANES, LANES), 0)
    point_node = note[3:6].astype(jnp.int32)
    for c in range(3):
        node_ref[:, c * LANES : (c + 1) * LANES] = one_hot(node_row == point_node[c : c + 1])

    def step(moment, _):
        drive = time_ref[0, moment]
        stiffness_tiles(x_ref, scale_of, y_ref, grad_ref, 3)
        inputs = input_ref[moment]
        high = inputs.astype(jnp.bfloat16)
        rest = (inputs - high.astype(jnp.float32)).astype(jnp.bfloat16)
        parts = [
            node_ref[:, c * LANES : (c + 1) * LANES] * part[c : c + 1]
            for part in (high, rest)
            for c in range(3)
        ]
        kick = jnp.dot(
            jnp.concatenate(parts, axis=1), spread_ref[...], preferred_element_type=jnp.float32
        )
        for g in range(3):
            kick_ref[200 * g : 200 * g + LANES] = kick[:, g * LANES : (g + 1) * LANES]
        extra = partner_faces(y_ref, face_ref, side, 0, 3)
        for g in range(3):
            for bc in range(25):
                net = kick_ref[pl.ds(200 * g + bc, 8, stride=25), :] - tile_of(y_ref, bc, g, 3)
                if g == 0:
                    net = net - extra[bc]
                x = tile_of(x_ref, bc, g, 3)
                kept = keep_of(bc, g) * x
                pushed = drive * force_of(bc, g)
                advanced = kept - tile_of(h_ref, bc, g, 3) + pushed
                set_tile(x_ref, advanced + inverse_of(bc, g) * net, bc, g, 3)
                set_tile(h_ref, kept - x, bc, g, 3)
                set_tile(old_ref, x, bc, g, 3)
        return 0

    lax.fori_loop(1, STEPS, step, 0)
    home = jnp.concatenate([note[13:14], note[14:15]], axis=1).astype(jnp.int32)
    linked = jnp.where(
        home == lax.broadcasted_iota(jnp.int32, (LANES, 2 * LANES), 0), 1.0, 0.0
    ).astype(jnp.bfloat16)
    alone = home < 0

    for tiles_ref, out_ref in ((old_ref, before_ref), (x_ref, now_ref)):
        for g in range(3):
            for bc in range(25):
                kick_ref[pl.ds(200 * g + bc, 8, stride=25), :] = tile_of(tiles_ref, bc, g, 3)
        moved = exact_pick(kick_ref[0:LANES], linked)
        for g in range(2):
            own = kick_ref[200 * (g + 1) : 200 * (g + 1) + LANES]
            cut = slice(g * LANES, (g + 1) * LANES)
            out_ref[:, 0, cut] = jnp.where(alone[:, cut], own, moved[:, cut])[:NODES]


def fast_body(wave_speed, inverse_mass, source_field, source_time, face_links, coupling_links):
    _, weight_np, _ = node_tables()
    weight = jnp.asarray(weight_np).reshape(NODES, 1)
    wave, mass, source = [
        jnp.transpose(field, (1, 0, 2)) for field in (wave_speed, inverse_mass, source_field)
    ]
    faces = jnp.transpose(face_links, (1, 0, 2))
    blocks = lax.axis_size("blk")
    columns = wave_speed.shape[-1]
    me = lax.axis_index("blk")
    place = jnp.stack([lax.axis_index("sec"), me]).astype(jnp.int32)
    vmem = pl.BlockSpec(memory_space=pltpu.VMEM)
    smem = pl.BlockSpec(memory_space=pltpu.SMEM)
    params = pltpu.CompilerParams(vmem_limit_bytes=16 << 20)

    def shape(*dims):
        return jax.ShapeDtypeStruct(dims, jnp.float32)

    links, m0, m1, m2, m3, count, amplitude = pl.pallas_call(
        pack_kernel,
        out_shape=[shape(blocks, 8, LANES)] + [shape(16, 4 * LANES)] * 4 + [shape(LANES, columns), shape(1, STEPS)],
        in_specs=[smem] * 2 + [vmem] * 6,
        out_specs=[vmem] * 6 + [smem],
        compiler_params=params,
    )(place, source_time, wave, mass, source, weight, faces, coupling_links)
    mine = [m0, m1, m2, m3]
    ghost = [partner_2(part, "blk", j) for j, part in enumerate(mine)]
    every = lax.all_to_all(links, "blk", 0, 0, tiled=True)

    def tiles(count):
        return pltpu.VMEM((8 * count, LANES), jnp.float32)

    table, copies, *own_tiles = pl.pallas_call(
        point_kernel,
        out_shape=[shape(16, LANES), shape(4, LANES, LANES)] + [shape(400, LANES)] * 4,
        in_specs=[smem] + [vmem] * 6,
        out_specs=[vmem] * 6,
        scratch_shapes=[tiles(50)],
        compiler_params=params,
    )(place, wave, mass, source, weight, count, every)
    payload, pair, note = pl.pallas_call(
        response_kernel,
        out_shape=[shape(blocks, 1, PAYLOAD * LANES), shape(4, LANES, LANES), shape(16, LANES)],
        in_specs=[smem] * 2 + [vmem] * 10,
        out_specs=[vmem] * 3,
        compiler_params=params,
        scratch_shapes=[tiles(25)] * 5
        + [tiles(50), tiles(40), tiles(25), tiles(25), tiles(80), tiles(50), tiles(5)]
        + [pltpu.VMEM((8, 8, LANES), jnp.int32), pltpu.VMEM((STEPS, 8, LANES), jnp.float32)],
    )(
        place,
        amplitude,
        table,
        copies,
        *mine,
        *ghost,
    )

    same_core = [[c + 2 * i for i in range(blocks)] for c in range(2)]
    received = lax.all_to_all(
        payload, ("sec", "blk"), 0, 0, axis_index_groups=same_core, tiled=True
    )
    sibling = partner_2(received, "blk", 0)
    flag = INDEX_ROW * LANES + HALF
    overflow = jnp.max(
        jnp.maximum(received[:, 0, flag], sibling[:, 0, flag])
    ) > 0

    def quick(_):
        return tuple(
            pl.pallas_call(
                final_kernel,
                out_shape=[shape(NODES, 1, columns)] * 2,
                in_specs=[smem] * 2 + [vmem] * 8,
                out_specs=[vmem] * 2,
                compiler_params=params,
                scratch_shapes=[
                    pltpu.VMEM((2, 2, PAYLOAD, 8, LANES), jnp.float32),
                    pltpu.VMEM((6 * LANES, 3 * LANES), jnp.bfloat16),
                    pltpu.VMEM((STEPS, 8, LANES), jnp.float32),
                ]
                + [tiles(25)] * 4
                + [tiles(75)] * 3
                + [tiles(120), tiles(75), tiles(5), tiles(75)]
                + [pltpu.VMEM((LANES, 3 * LANES), jnp.bfloat16)],
            )(
                place,
                amplitude,
                received,
                sibling,
                *own_tiles,
                pair,
                note,
            )
        )

    def slow(_):
        results = general_body(
            wave_speed, inverse_mass, source_field, source_time, face_links, coupling_links
        )
        return tuple(jnp.transpose(field, (1, 0, 2)) for field in results)

    now, before = lax.cond(overflow, slow, quick, 0)
    return (jnp.transpose(now, (1, 0, 2)), jnp.transpose(before, (1, 0, 2)))


def body(*arguments):
    wave_speed, _, _, _, face_links, coupling_links = arguments
    fits = (
        lax.axis_size("blk") == 16
        and lax.axis_size("sec") == 2
        and wave_speed.shape[1:] == (NODES, 2 * LANES)
        and face_links.shape[-1] == LANES
        and coupling_links.shape[-1] >= CAPC * 16
    )
    return fast_body(*arguments) if fits else general_body(*arguments)


def solution(mesh):
    in_specs = (
        P("sec", None, "blk"),
        P("sec", None, "blk"),
        P("sec", None, "blk"),
        P("sec", None),
        P("sec", None, "blk"),
        P(None, "blk"),
    )
    out_specs = (P("sec", None, "blk"), P("sec", None, "blk"))
    return jax.shard_map(body, mesh=mesh, in_specs=in_specs, out_specs=out_specs, check_vma=False)
```
